32 devices in a mesh: ctx: 8 (over y, x, core), ch: 4 (over z).
Axes of the slice: x: 2, y: 2, z: 4, core: 2. Of those that a mesh axis runs over, the one named last changes fastest.
Arguments:
- query_input: bfloat16 [1024, 4608], P('ctx', 'ch'), may hold values from -6 to 6
- key_input: bfloat16 [1024, 4608], P('ctx', 'ch'), may hold values from -6 to 6
- value_input: bfloat16 [1024, 4608], P('ctx', 'ch'), may hold values from -6 to 6
- filters: bfloat16 [4608, 128], P('ch'), may hold values from -1.7 to 1.7
- complement: int32 [4608], P('ch'), may hold values from 0 to 4607, as said below
- doc_lengths: int32 [16], replicated, may hold values from 1 to 256, 1024 in all
- cotangent: bfloat16 [1024, 4608], P('ctx', 'ch'), may hold values from -6 to 6
Outputs:
- mixer_out: bfloat16 [1024, 4608], P('ctx', 'ch')
- grad_query: bfloat16 [1024, 4608], P('ctx', 'ch')
- grad_key: bfloat16 [1024, 4608], P('ctx', 'ch')
- grad_value: bfloat16 [1024, 4608], P('ctx', 'ch')
- grad_filter: float32 [4608, 128], P('ch', 'ctx')
The draws below stay inside these ranges and needn't reach their ends.
Inputs may be any that keep to these rules, and one draw needn't show every extreme that they name: complement pairs the channels: complement[complement[c]] = c and complement[c] != c for every channel c. `doc_lengths`: the 16 lengths sum to 1024.
All inputs are finite; a program needn't handle non-finite values.
Results may differ from the reference program's by a relative error of at most 0.0065.
Values may be sent and summed in bfloat16 or wider, within the bound.
A program may use at most 192 MiB of HBM per device.

```python
import math
import jax
import jax.numpy as jnp
import numpy as np
from jax import lax

D = 4608
TAPS = 128
DOCS = 16
L = 1024


def draw_filters(key, part):
    key_scale, key_taps = jax.random.split(key)
    low_end = math.log(12.0)
    high_end = math.log(512.0)
    spans = jnp.exp(jax.random.uniform(key_scale, (D, 1), jnp.float32, low_end, high_end))
    offsets = jnp.arange(TAPS, dtype=jnp.float32)[None, :]
    noise = jax.random.truncated_normal(key_taps, -4.0, 4.0, (D, TAPS), jnp.float32)
    values = noise * jnp.exp(-offsets / spans) * jnp.sqrt(2.0 / spans)
    return values.astype(jnp.bfloat16)


def draw_complement(key, part):
    order = jax.random.permutation(key, D).astype(jnp.int32)
    leaders = order[0::2]
    partners = order[1::2]
    table = jnp.zeros((D,), jnp.int32).at[leaders].set(partners).at[partners].set(leaders)
    return table.astype(jnp.int32)


def block_levels(key, extent, cuts, low, top_value):
    gain, own = 1.0, jax.random.fold_in(key, 6)
    for dim, blocks in cuts:
        heights = jnp.exp(jax.random.uniform(jax.random.fold_in(own, dim), (blocks,), jnp.float32, low / len(cuts), top_value / len(cuts)))
        gain = gain * jnp.repeat(heights, extent[dim] // blocks).reshape([-1 if axis == dim else 1 for axis in range(len(extent))])
    return gain


def split_up(count, total, most, skew):
    loads = [(1 << 20) // math.isqrt(rank ** skew) + 1 for rank in range(2, count + 1)]
    rest, holding = total - most - (count - 1), [1] * (count - 1)
    while rest > 0:
        candidates = [i for i in range(count - 1) if holding[i] < most]
        pool, budget = sum([loads[i] for i in candidates]), rest
        for i in candidates:
            addition = min(most - holding[i], max(1, budget * loads[i] // pool), rest)
            holding[i] = holding[i] + addition
            rest = rest - addition
    return np.array([most] + holding)


def ragged_sizes(rng, amount, total, most, lean):
    if amount == 2:
        one = jax.random.randint(rng, (), max(1, total - most), min(most, total - 1) + 1)
        return jnp.stack([one, total - one])
    sizes = jnp.asarray(split_up(amount, total, most, lean), jnp.int32)
    pairs = (amount - 1) // 2
    giver, taker = sizes[1:1 + 2 * pairs:2], sizes[2:2 + 2 * pairs:2]
    room = jnp.minimum(giver - 1, most - taker)
    shifted = jax.random.randint(jax.random.fold_in(rng, 1), (pairs,), 0, 1 << 20) % (room + 1)
    sizes = sizes.at[1:1 + 2 * pairs:2].set(giver - shifted).at[2:2 + 2 * pairs:2].set(taker + shifted)
    return sizes[jax.random.permutation(jax.random.fold_in(rng, 2), amount)]


def normal_values(key, dims, scale, bound, cuts=(), kind=jnp.bfloat16):
    array = jax.random.normal(key, dims, jnp.float32) * scale
    if len(cuts) > 0:
        array = block_levels(key, dims, cuts, -0.22, 0.18) * array
    return jnp.clip(array, min=-bound, max=bound).astype(kind)


def setup_inputs(seed: int = 0) -> dict:
    key_list = jax.random.split(jax.random.key(seed), 8)
    query_input = normal_values(key_list[0], (L, D), 1.0, 6.0, ((0, 8), (1, 4)))
    key_input = normal_values(key_list[1], (L, D), 1.0, 6.0, ((0, 8), (1, 4)))
    value_input = normal_values(key_list[2], (L, D), 1.0, 6.0, ((0, 8), (1, 4)))
    filters = draw_filters(jax.random.fold_in(key_list[7], 71), 0)
    complement = draw_complement(jax.random.fold_in(key_list[7], 71), 0)
    doc_lengths = ragged_sizes(key_list[5], DOCS, L, L // 4, 0).astype(jnp.int32)
    cotangent = normal_values(key_list[6], (L, D), 1.0, 6.0, ((0, 8), (1, 4)))
    return dict(query_input=query_input, key_input=key_input, value_input=value_input, filters=filters, complement=complement, doc_lengths=doc_lengths, cotangent=cotangent)


def reference(query_input, key_input, value_input, filters, complement, doc_lengths, cotangent):
    rim_width = TAPS - 1
    places = jnp.arange(L, dtype=jnp.int32)
    doc_ends = jnp.cumsum(doc_lengths).astype(jnp.int32)
    starts = doc_ends - doc_lengths
    inside = (places[:, None] >= starts[None, :]) & (places[:, None] < doc_ends[None, :])
    doc_first = jnp.sum(jnp.where(inside, starts[None, :], 0), axis=1).astype(jnp.int32)
    doc_last = jnp.sum(jnp.where(inside, doc_ends[None, :] - 1, 0), axis=1).astype(jnp.int32)
    key_f = key_input.astype(jnp.float32)
    value_f = value_input.astype(jnp.float32)
    query_f = query_input.astype(jnp.float32)
    cot_f = cotangent.astype(jnp.float32)
    product = (key_f * value_f).astype(jnp.bfloat16)
    kernel_t = filters.astype(jnp.float32).T
    partner_t = filters.astype(jnp.float32)[complement].T
    padded_u = jnp.pad(product.astype(jnp.float32), ((rim_width, rim_width), (0, 0)))
    offsets = jnp.arange(TAPS, dtype=jnp.int32)

    def masks(offset):
        behind = (places - offset >= doc_first).astype(jnp.float32)[:, None]
        forward = (places + offset <= doc_last).astype(jnp.float32)[:, None]
        return behind, forward

    def forward_tap(carry, offset):
        causal, anti = carry
        behind, forward = masks(offset)
        earlier = lax.dynamic_slice_in_dim(padded_u, (rim_width - offset).astype(jnp.int32), L, 0)
        later = lax.dynamic_slice_in_dim(padded_u, (rim_width + offset).astype(jnp.int32), L, 0)
        causal = causal + kernel_t[offset][None, :] * earlier * behind
        anti = anti + partner_t[offset][None, :] * later * forward
        return (causal, anti), None

    zeros = jnp.zeros((L, D), jnp.float32)
    (causal, anti), _ = lax.scan(forward_tap, (zeros, zeros), offsets)
    strand_rc = anti.astype(jnp.bfloat16)
    combined = causal + strand_rc.astype(jnp.float32)
    mixer_out = (query_f * combined).astype(jnp.bfloat16)
    grad_query = (cot_f * combined).astype(jnp.bfloat16)
    upstream = (cot_f * query_f).astype(jnp.bfloat16)
    upstream_f = upstream.astype(jnp.float32)
    padded_r = jnp.pad(upstream_f, ((rim_width, rim_width), (0, 0)))

    def backward_tap(carry, offset):
        ahead_sum, behind_sum = carry
        behind, forward = masks(offset)
        low = (rim_width - offset).astype(jnp.int32)
        high = (rim_width + offset).astype(jnp.int32)
        earlier_u = lax.dynamic_slice_in_dim(padded_u, low, L, 0)
        later_u = lax.dynamic_slice_in_dim(padded_u, high, L, 0)
        earlier_r = lax.dynamic_slice_in_dim(padded_r, low, L, 0)
        later_r = lax.dynamic_slice_in_dim(padded_r, high, L, 0)
        ahead_sum = ahead_sum + kernel_t[offset][None, :] * later_r * forward
        behind_sum = behind_sum + partner_t[offset][None, :] * earlier_r * behind
        own = jnp.sum(upstream_f * earlier_u * behind, axis=0)
        mirrored = jnp.sum(upstream_f * later_u * forward, axis=0)
        return (ahead_sum, behind_sum), (own, mirrored)

    (ahead_sum, behind_sum), (own_rows, mirrored_rows) = lax.scan(backward_tap, (zeros, zeros), offsets)
    rc_grad = behind_sum.astype(jnp.bfloat16)
    grad_product = ahead_sum + rc_grad.astype(jnp.float32)
    grad_key = (grad_product * value_f).astype(jnp.bfloat16)
    grad_value = (grad_product * key_f).astype(jnp.bfloat16)
    grad_filter = (own_rows + mirrored_rows[:, complement]).T.astype(jnp.float32)
    return (mixer_out, grad_query, grad_key, grad_value, grad_filter)
```

```python
import functools

import jax
import jax.numpy as jnp
import numpy as np
from jax import lax
from jax.experimental import pallas as pl
from jax.experimental.pallas import tpu as pltpu
from jax.sharding import PartitionSpec as P

F32, BF16 = jnp.float32, jnp.bfloat16
LANES, TILE = 128, 16


def split_bf16(table):
    high = table.astype(BF16)
    low = (table - high.astype(np.float64)).astype(BF16)
    return high, low


def fourier_tables(rows, taps, owners):
    length = 2 * rows
    angle = 2.0 * np.pi * (np.arange(length // 2) + 0.5) / length
    places = np.arange(3 * rows) - rows
    turns = angle[:, None] * places[None, :]
    analyse = np.concatenate([np.cos(turns), -np.sin(turns)], axis=0)
    own = np.arange(rows)[:, None] * angle[None, :]
    rebuild = np.concatenate([np.cos(own), -np.sin(own)], axis=1) * (2.0 / length)
    lags = angle[:, None] * np.arange(taps)[None, :]
    causal = np.concatenate([np.cos(lags), -np.sin(lags)], axis=0)
    anti = np.concatenate([np.cos(lags), np.sin(lags)], axis=0)
    spread = np.arange(taps)[:, None] * angle[None, :]
    forward = np.concatenate([np.cos(spread), -np.sin(spread)], axis=1) * (2.0 / length)
    backward = np.concatenate([np.cos(spread), np.sin(spread)], axis=1) * (2.0 / length)
    return (
        analyse.astype(BF16),
        rebuild.astype(BF16),
        *split_bf16(causal),
        *split_bf16(anti),
        *split_bf16(forward),
        *split_bf16(backward),
    )


def mm(a, b):
    return jnp.dot(a, b, preferred_element_type=F32)


def mm_t(a, b):
    return lax.dot_general(a, b, (((1,), (1,)), ((), ())), preferred_element_type=F32)


def product_of(a, b):
    return (a.astype(F32) * b.astype(F32)).astype(BF16)


def between(index, low, high):
    return ((index >= low) & (index < high)).astype(F32).astype(BF16)


def mix_kernel(
    lens, query, key, value, cot, u_prev, u_next, r_prev, r_next, taps_own, taps_partner,
    analyse, rebuild, causal_hi, causal_lo, anti_hi, anti_lo, fwd_hi, fwd_lo, bwd_hi, bwd_lo,
    mixer_out, grad_query, grad_key, grad_value, tap_sums,
    ahead, behind, own_u, own_r, acc_y, acc_p, acc_g, z_ref, q_ref,
):
    rows = query.shape[0]
    taps = fwd_hi.shape[0]
    half = rows
    first_place = lax.axis_index("ctx") * rows

    f, g = taps_own[...], taps_partner[...]
    ahead[...] = mm_t(causal_hi[...], f) + mm_t(causal_lo[...], f)
    behind[...] = mm(anti_hi[...], g) + mm(anti_lo[...], g)
    own_u[...] = product_of(key[...], value[...])
    own_r[...] = product_of(cot[...], query[...])
    acc_g[...] = jnp.zeros_like(acc_g)
    lane = lax.broadcasted_iota(jnp.int32, (1, rows), 1)
    column = lax.broadcasted_iota(jnp.int32, (rows, 1), 0)

    def locate(d, carry):
        start, first_low, first_high, last_low, last_high = carry
        end = start + lens[d]
        low, high = start - first_place, end - first_place
        is_first = (low <= 0) & (high > 0)
        is_last = (low <= rows - 1) & (high > rows - 1)
        return (
            end,
            jnp.where(is_first, low, first_low),
            jnp.where(is_first, high, first_high),
            jnp.where(is_last, low, last_low),
            jnp.where(is_last, high, last_high),
        )

    zero = jnp.int32(0)
    _, first_low, first_high, last_low, last_high = lax.fori_loop(
        0, lens.shape[0], locate, (zero, zero, zero, zero, zero)
    )

    def halo(u_halo, r_halo, section, inside, own_low, own_high, filter_u, filter_r, total):
        outer = analyse[:, section] * inside
        inner = analyse[:, rows : 2 * rows] * between(lane, own_low, own_high)
        back = rebuild[...] * between(column, own_low, own_high)
        u_hat = mm(outer, u_halo[...])
        r_hat = mm(outer, r_halo[...])
        o_hat = mm(inner, own_r[...])
        u_re, u_im, r_re, r_im = u_hat[:half], u_hat[half:], r_hat[:half], r_hat[half:]
        o_re, o_im = o_hat[:half], o_hat[half:]
        a_re, a_im = filter_u[:half], filter_u[half:]
        b_re, b_im = filter_r[:half], filter_r[half:]
        z_ref[:half] = (a_re * u_re - a_im * u_im).astype(BF16)
        z_ref[half:] = (a_re * u_im + a_im * u_re).astype(BF16)
        q_ref[:half] = (b_re * r_re + b_im * r_im).astype(BF16)
        q_ref[half:] = (b_re * r_im - b_im * r_re).astype(BF16)
        total[:half] = o_re * u_re + o_im * u_im
        total[half:] = o_im * u_re - o_re * u_im
        return mm(back, z_ref[...]), mm(back, q_ref[...])

    prev_y, prev_p = halo(
        u_prev, r_prev, slice(0, rows), between(lane - rows, first_low, first_high),
        first_low, first_high, ahead, behind, acc_g.at[1],
    )
    acc_y[...], acc_p[...] = prev_y, prev_p
    next_y, next_p = halo(
        u_next, r_next, slice(2 * rows, 3 * rows), between(lane + rows, last_low, last_high),
        last_low, last_high, behind, ahead, acc_g.at[2],
    )
    acc_y[...] += next_y
    acc_p[...] += next_p
    ahead[...] += behind[...]

    def document(d, start):
        end = start + lens[d]

        @pl.when((start < first_place + rows) & (end > first_place))
        def _():
            low, high = start - first_place, end - first_place
            masked = analyse[:, rows : 2 * rows] * between(lane, low, high)
            back = rebuild[...] * between(column, low, high)
            u_hat = mm(masked, own_u[...])
            o_hat = mm(masked, own_r[...])
            h_re, h_im = ahead[:half], ahead[half:]
            u_re, u_im = u_hat[:half], u_hat[half:]
            o_re, o_im = o_hat[:half], o_hat[half:]
            z_ref[:half] = (h_re * u_re - h_im * u_im).astype(BF16)
            z_ref[half:] = (h_re * u_im + h_im * u_re).astype(BF16)
            q_ref[:half] = (h_re * o_re + h_im * o_im).astype(BF16)
            q_ref[half:] = (h_re * o_im - h_im * o_re).astype(BF16)
            acc_g[0, :half] += o_re * u_re + o_im * u_im
            acc_g[0, half:] += o_im * u_re - o_re * u_im
            acc_y[...] += mm(back, z_ref[...])
            acc_p[...] += mm(back, q_ref[...])

        return end

    lax.fori_loop(0, lens.shape[0], document, jnp.int32(0))
    combined, grad_product = acc_y[...], acc_p[...]
    mixer_out[...] = (query[...].astype(F32) * combined).astype(BF16)
    grad_query[...] = (cot[...].astype(F32) * combined).astype(BF16)
    grad_key[...] = (grad_product * value[...].astype(F32)).astype(BF16)
    grad_value[...] = (grad_product * key[...].astype(F32)).astype(BF16)
    for part, hi, lo in ((1, fwd_hi, fwd_lo), (2, bwd_hi, bwd_lo)):
        g_sum = acc_g[0] + acc_g[part]
        g_hi = g_sum.astype(BF16)
        g_lo = (g_sum - g_hi.astype(F32)).astype(BF16)
        sums = mm(hi[...], g_hi) + mm(hi[...], g_lo) + mm(lo[...], g_hi)
        tap_sums[part - 1] = sums.astype(BF16)


def channel_block(channels):
    for block in (384, 256, 128):
        if channels % block == 0:
            return block
    return channels


def mix(doc_lengths, fields, filters, partner, owners):
    rows, channels = fields[0].shape
    taps = filters.shape[1]
    block = channel_block(channels)
    tables = fourier_tables(rows, taps, owners)
    length = 2 * rows
    field_spec = pl.BlockSpec((rows, block), lambda i: (0, i))
    filter_spec = pl.BlockSpec((block, taps), lambda i: (i, 0))
    partner_spec = pl.BlockSpec((taps, block), lambda i: (0, i))
    table_specs = [pl.BlockSpec(t.shape, lambda i: (0, 0)) for t in tables]
    return pl.pallas_call(
        mix_kernel,
        grid=(channels // block,),
        in_specs=[pl.BlockSpec(memory_space=pltpu.SMEM)]
        + [field_spec] * 8
        + [filter_spec, partner_spec]
        + table_specs,
        out_specs=[field_spec] * 4 + [pl.BlockSpec((2, taps, block), lambda i: (0, 0, i))],
        out_shape=[jax.ShapeDtypeStruct((rows, channels), BF16)] * 4
        + [jax.ShapeDtypeStruct((2, taps, channels), BF16)],
        scratch_shapes=[
            pltpu.VMEM((length, block), F32),
            pltpu.VMEM((length, block), F32),
            pltpu.VMEM((rows, block), BF16),
            pltpu.VMEM((rows, block), BF16),
            pltpu.VMEM((rows, block), F32),
            pltpu.VMEM((rows, block), F32),
            pltpu.VMEM((3, length, block), F32),
            pltpu.VMEM((length, block), BF16),
            pltpu.VMEM((length, block), BF16),
        ],
        name="mix",
    )(doc_lengths, *fields, filters, partner, *[jnp.asarray(t) for t in tables])


def remote(src, dst, sems, index, device):
    return pltpu.make_async_remote_copy(
        src_ref=src, dst_ref=dst, send_sem=sems[0].at[index], recv_sem=sems[1].at[index],
        device_id=device, device_id_type=pl.DeviceIdType.MESH,
    )


def announce(devices):
    barrier = pltpu.get_barrier_semaphore()
    for device in devices:
        pl.semaphore_signal(barrier, inc=1, device_id=device, device_id_type=pl.DeviceIdType.MESH)


def gathered_in(devices):
    pl.semaphore_wait(pltpu.get_barrier_semaphore(), len(devices))


def pick_partners(complement, landed, ch, channels):
    mine = lax.axis_index("ch")
    owner = sum((complement >= k * channels).astype(jnp.int32) for k in range(1, ch)) + jnp.zeros_like(complement)
    step = mine - owner
    step = jnp.where(step < 0, step + ch, step)
    local = complement - owner * channels
    blocks = channels // LANES
    block = step * blocks + lax.shift_right_logical(local, 7)
    within = lax.bitwise_and(local, LANES - 1)
    sublane = lax.broadcasted_iota(jnp.int32, (LANES, channels), 0)
    chosen = (sublane == within).astype(F32).astype(BF16)
    stacked = jnp.concatenate(
        [landed[s, :, b * LANES : (b + 1) * LANES] for s in range(ch) for b in range(blocks)], axis=0
    )
    spread_out = mm(stacked, chosen)
    height = landed.shape[1]
    total = jnp.zeros((height, channels), F32)
    for b in range(ch * blocks):
        total = total + jnp.where(block == b, spread_out[b * height : (b + 1) * height], 0.0)
    return total


def spread_kernel(ctx, ch, groups, query, key, value, cot, filters, complement,
                  u_prev, u_next, r_prev, r_next, partner,
                  u, r, landed, picked, halo_send, halo_recv, ch_send, ch_recv, mate_send, mate_recv, local):
    me, mine = lax.axis_index("ctx"), lax.axis_index("ch")
    channels, taps = filters.shape
    after, before = {"ctx": (me + 1) % ctx}, {"ctx": (me + ctx - 1) % ctx}
    group, base = me % groups, me - me % groups
    height = taps // groups
    peers = [{"ch": (mine + step) % ch} for step in range(1, ch)]
    mates = [{"ctx": base + (group + step) % groups} for step in range(1, groups)]
    everyone = [after, before] + peers + mates
    announce(everyone)
    row = lax.broadcasted_iota(jnp.int32, (height, taps), 0)
    tap = lax.broadcasted_iota(jnp.int32, (height, taps), 1)
    wanted = (tap == row + group * height).astype(F32).astype(BF16)
    landed[0] = mm_t(wanted, filters[...]).astype(BF16)
    u[...] = product_of(key[...], value[...])
    r[...] = product_of(cot[...], query[...])
    gathered_in(everyone)
    along = [
        remote(landed.at[0], landed.at[step], (ch_send, ch_recv), step - 1, peers[step - 1])
        for step in range(1, ch)
    ]
    for copy in along[::-1]:
        copy.start()
    to_next = [remote(field, place, (halo_send, halo_recv), index, after)
               for index, (field, place) in enumerate(((u, u_prev), (r, r_prev)))]
    to_prev = [remote(field, place, (halo_send, halo_recv), index + 2, before)
               for index, (field, place) in enumerate(((u, u_next), (r, r_next)))]

    for copy in to_next + to_prev:
        copy.start()
    for copy in along:
        copy.wait()
    picked[...] = pick_partners(complement[...], landed, ch, channels).astype(BF16)
    keep = pltpu.make_async_copy(picked, partner.at[group], local)
    keep.start()
    shared = [
        remote(picked, partner.at[group], (mate_send, mate_recv), step - 1, mates[step - 1])
        for step in range(1, groups)
    ]
    for copy in shared:
        copy.start()
    for copy in shared:
        copy.wait()
    for copy in to_next + to_prev:
        copy.wait()
    keep.wait()


def spread(query, key, value, cot, filters, complement):
    ctx, ch = lax.axis_size("ctx"), lax.axis_size("ch")
    channels, taps = filters.shape
    groups = min(ctx, taps // TILE)
    height = taps // groups
    hbm = pl.BlockSpec(memory_space=pl.ANY)
    vmem = pl.BlockSpec(memory_space=pltpu.VMEM)
    dma = pltpu.SemaphoreType.DMA
    field = jax.ShapeDtypeStruct(query.shape, BF16)
    *halos, partner = pl.pallas_call(
        functools.partial(spread_kernel, ctx, ch, groups),
        in_specs=[vmem] * 6,
        out_specs=[hbm] * 5,
        out_shape=[field] * 4 + [jax.ShapeDtypeStruct((groups, height, channels), BF16)],
        scratch_shapes=[
            pltpu.VMEM(query.shape, BF16),
            pltpu.VMEM(query.shape, BF16),
            pltpu.VMEM((ch, height, channels), BF16),
            pltpu.VMEM((height, channels), BF16),
            dma((4,)), dma((4,)), dma((ch - 1,)), dma((ch - 1,)), dma((groups - 1,)), dma((groups - 1,)), dma,
        ],
        compiler_params=pltpu.CompilerParams(collective_id=0, has_side_effects=True),
        name="spread",
    )(query, key, value, cot, filters, complement)
    return halos, partner.reshape(taps, channels)


def collect_kernel(ctx, ch, pieces, complement, grad, landed, sent, sum_send, sum_recv, ch_send, ch_recv, local):
    me, mine = lax.axis_index("ctx"), lax.axis_index("ch")
    share, channels = grad.shape
    others = [{"ctx": (me + step) % ctx} for step in range(1, ctx)]
    peers = [{"ch": (mine + step) % ch} for step in range(1, ch)]
    announce(others + peers)
    keep = pltpu.make_async_copy(pieces.at[:, me], landed.at[0], local)
    keep.start()
    if share < sent.shape[1]:
        sent[...] = jnp.zeros_like(sent)
    gathered_in(others + peers)
    copies = [
        remote(pieces.at[:, (me + step) % ctx], landed.at[step], (sum_send, sum_recv), step - 1, others[step - 1])
        for step in range(1, ctx)
    ]
    for copy in copies:
        copy.start()
    keep.wait()
    for copy in copies:
        copy.wait()
    sent[0, :share] = sum(landed[step, 1].astype(F32) for step in range(ctx)).astype(BF16)
    copies = [
        remote(sent.at[0], sent.at[step], (ch_send, ch_recv), step - 1, peers[step - 1]) for step in range(1, ch)
    ]
    for copy in copies:
        copy.start()
    own = sum(landed[step, 0].astype(F32) for step in range(ctx))
    for copy in copies:
        copy.wait()
    grad[...] = own + pick_partners(complement[...], sent, ch, channels)[:share]


def collect(pieces, complement):
    ctx, ch = lax.axis_size("ctx"), lax.axis_size("ch")
    _, _, share, channels = pieces.shape
    vmem = pl.BlockSpec(memory_space=pltpu.VMEM)
    dma = pltpu.SemaphoreType.DMA
    return pl.pallas_call(
        functools.partial(collect_kernel, ctx, ch),
        in_specs=[pl.BlockSpec(memory_space=pl.ANY), vmem],
        out_specs=vmem,
        out_shape=jax.ShapeDtypeStruct((share, channels), F32),
        scratch_shapes=[
            pltpu.VMEM((ctx, 2, share, channels), BF16),
            pltpu.VMEM((ch, -(-share // TILE) * TILE, channels), BF16),
            dma((ctx - 1,)), dma((ctx - 1,)), dma((ch - 1,)), dma((ch - 1,)), dma,
        ],
        compiler_params=pltpu.CompilerParams(collective_id=1, has_side_effects=True),
        name="collect",
    )(pieces, complement)


def shards(query_input, key_input, value_input, filters, complement, doc_lengths, cotangent):
    channels, taps = filters.shape
    ctx = lax.axis_size("ctx")
    table = complement.reshape(1, channels)
    halos, partner = spread(query_input, key_input, value_input, cotangent, filters, table)
    *mixed, tap_sums = mix(
        doc_lengths, (query_input, key_input, value_input, cotangent, *halos), filters, partner, ctx
    )
    share = taps // ctx
    grad_filter = collect(tap_sums.reshape(2, ctx, share, channels), table)
    return (*mixed, grad_filter.T)


def solution(mesh):
    placed = (
        P("ctx", "ch"),
        P("ctx", "ch"),
        P("ctx", "ch"),
        P("ch", None),
        P("ch"),
        P(),
        P("ctx", "ch"),
    )
    return jax.shard_map(
        shards,
        mesh=mesh,
        in_specs=placed,
        out_specs=(P("ctx", "ch"), P("ctx", "ch"), P("ctx", "ch"), P("ctx", "ch"), P("ch", "ctx")),
        check_vma=False,
    )
```

```python
import functools

import jax
import jax.numpy as jnp
import numpy as np
from jax import lax
from jax.experimental import pallas as pl
from jax.experimental.pallas import tpu as pltpu
from jax.sharding import PartitionSpec as P

F32, BF16 = jnp.float32, jnp.bfloat16
LANES, TILE, PACK = 128, 16, 4
VMEM_BYTES = 56 * 2**20


def split_bf16(table):
    high = table.astype(BF16)
    low = (table - high.astype(np.float64)).astype(BF16)
    return high, low


def wave(places, length):
    angle = 2.0 * np.pi * (np.arange(length // 2) + 0.5) / length
    turns = angle[:, None] * np.asarray(places)[None, :]
    return np.cos(turns), np.sin(turns)


def fourier_tables(rows, taps):
    long, short = 2 * rows, 2 * rows // PACK
    cos, sin = wave(np.arange(3 * rows) - rows, long)
    analyse = np.concatenate([cos, -sin], axis=0)
    cos_s, sin_s = wave(np.arange(rows), short)
    pack = lambda table: np.tile(table, (PACK, 1))
    analyse_short = np.concatenate([pack(cos_s), pack(-sin_s)], axis=0)
    near = (np.arange(taps) < short // 2)[None, :]
    lag_cos, lag_sin = wave(np.arange(taps), long)
    near_cos, near_sin = [pack(table * near) for table in wave(np.arange(taps), short)]
    causal = np.concatenate([lag_cos, -lag_sin, near_cos, -near_sin], axis=0)
    anti = np.concatenate([lag_cos, lag_sin, near_cos, near_sin], axis=0)
    forward = causal.T.copy()
    backward = anti.T.copy()
    for table in (forward, backward):
        table[:, : 2 * rows] *= 2.0 / long
        table[:, 2 * rows :] *= 2.0 / short
    rebuild = analyse[:, rows : 2 * rows].T * (2.0 / long)
    rebuild_short = analyse_short.T * (2.0 / short)
    return (
        analyse.astype(BF16),
        analyse_short.astype(BF16),
        rebuild.astype(BF16),
        rebuild_short.astype(BF16),
        *split_bf16(causal),
        *split_bf16(anti),
        *split_bf16(forward),
        *split_bf16(backward),
    )


def mm(a, b):
    return jnp.dot(a, b, preferred_element_type=F32)


def mm_t(a, b):
    return lax.dot_general(a, b, (((1,), (1,)), ((), ())), preferred_element_type=F32)


def mm_fine(hi, lo, x):
    x_hi = x.astype(BF16)
    x_lo = (x - x_hi.astype(F32)).astype(BF16)
    return mm(hi, x_hi) + mm(hi, x_lo) + mm(lo, x_hi)


def product_of(a, b):
    return (a.astype(F32) * b.astype(F32)).astype(BF16)


def flag(mask):
    return mask.astype(F32).astype(BF16)


def times(a, x):
    half = a.shape[0] // 2
    a_re, a_im, x_re, x_im = a[:half], a[half:], x[:half], x[half:]
    return a_re * x_re - a_im * x_im, a_re * x_im + a_im * x_re


def times_conj(a, x):
    half = a.shape[0] // 2
    a_re, a_im, x_re, x_im = a[:half], a[half:], x[:half], x[half:]
    return a_re * x_re + a_im * x_im, a_re * x_im - a_im * x_re


def remote(src, dst, sems, index, device):
    return pltpu.make_async_remote_copy(
        src_ref=src, dst_ref=dst, send_sem=sems[0].at[index], recv_sem=sems[1].at[index],
        device_id=device, device_id_type=pl.DeviceIdType.MESH,
    )


def announce(devices):
    barrier = pltpu.get_barrier_semaphore()
    for device in devices:
        pl.semaphore_signal(barrier, inc=1, device_id=device, device_id_type=pl.DeviceIdType.MESH)


def gathered_in(devices):
    pl.semaphore_wait(pltpu.get_barrier_semaphore(), len(devices))


def pick_partners(complement, landed, ch, channels):
    mine = lax.axis_index("ch")
    owner = sum((complement >= k * channels).astype(jnp.int32) for k in range(1, ch)) + jnp.zeros_like(complement)
    step = mine - owner
    step = jnp.where(step < 0, step + ch, step)
    local = complement - owner * channels
    blocks = channels // LANES
    block = step * blocks + lax.shift_right_logical(local, 7)
    within = lax.bitwise_and(local, LANES - 1)
    sublane = lax.broadcasted_iota(jnp.int32, (LANES, channels), 0)
    chosen = flag(sublane == within)
    stacked = jnp.concatenate(
        [landed[s, :, b * LANES : (b + 1) * LANES] for s in range(ch) for b in range(blocks)], axis=0
    )
    spread_out = mm(stacked, chosen)
    height = landed.shape[1]
    total = jnp.zeros((height, channels), F32)
    for b in range(ch * blocks):
        total = total + jnp.where(block == b, spread_out[b * height : (b + 1) * height], 0.0)
    return total


def survey(lens, rows, first_place):
    limit = rows // PACK
    lane3 = lax.broadcasted_iota(jnp.int32, (1, 3 * rows), 1) - rows
    lane = lax.broadcasted_iota(jnp.int32, (1, rows), 1)
    column = lax.broadcasted_iota(jnp.int32, (rows, 1), 0)
    low = -first_place
    found, base, last = jnp.int32(0), jnp.int32(0), jnp.int32(0)
    seen = jnp.zeros_like(lane3)
    seen_column = jnp.zeros_like(column)
    long_lane, short_lane = jnp.zeros_like(lane), jnp.zeros_like(lane)
    long_column, short_column = jnp.zeros_like(column), jnp.zeros_like(column)
    for d in range(lens.shape[0]):
        high = low + lens[d]
        own = jnp.minimum(high, rows) - jnp.maximum(low, 0)
        is_long = jnp.where(own > limit, 1, 0)
        found = found + is_long
        long_code = is_long * found
        short_code = (1 - is_long) * (d + 1)
        inside = (lane >= low) & (lane < high)
        long_lane = jnp.where(inside, long_code, long_lane)
        short_lane = jnp.where(inside, short_code, short_lane)
        inside = (column >= low) & (column < high)
        long_column = jnp.where(inside, long_code, long_column)
        short_column = jnp.where(inside, short_code, short_column)
        seen = seen + jnp.where(lane3 >= low, 1, 0)
        seen_column = seen_column + jnp.where(column >= low, 1, 0)
        base = base + jnp.where(low <= 0, 1, 0)
        last = last + jnp.where(low <= rows - 1, 1, 0)
        low = high
    seen = seen + jnp.where(lane3 >= low, 1, 0)
    return long_lane, short_lane, long_column, short_column, seen, seen_column, base, last


def mixer_kernel(
    ctx, ch, groups, block,
    lens, query, key, value, cot, filters, complement,
    analyse, analyse_short, rebuild, rebuild_short,
    causal_hi, causal_lo, anti_hi, anti_lo, fwd_hi, fwd_lo, bwd_hi, bwd_lo,
    mixer_out, grad_query, grad_key, grad_value, grad,
    u, r, halos, landed, picked, partner, outs, pieces, arrived, sent,
    masked, back, outer, back_outer, own_ends,
    ahead, behind, both, u_hat, o_hat, ends_hat, acc_g, z_ref, q_ref, acc_y, acc_p, acc_t,
    halo_send, halo_recv, ch_send, ch_recv, mate_send, mate_recv,
    sum_send, sum_recv, back_send, back_recv, local,
):
    me, mine = lax.axis_index("ctx"), lax.axis_index("ch")
    rows, channels = query.shape
    taps = filters.shape[1]
    size = 2 * rows
    chunks = channels // block
    slots = masked.shape[0]
    longs = PACK - 1
    after, before = {"ctx": (me + 1) % ctx}, {"ctx": (me + ctx - 1) % ctx}
    group, octet = me % groups, me - me % groups
    height = taps // groups
    share = grad.shape[0]
    others = [{"ctx": (me + step) % ctx} for step in range(1, ctx)]
    peers = [{"ch": (mine + step) % ch} for step in range(1, ch)]
    mates = [{"ctx": octet + (group + step) % groups} for step in range(1, groups)]
    announce(others + peers)

    row = lax.broadcasted_iota(jnp.int32, (height, taps), 0)
    tap = lax.broadcasted_iota(jnp.int32, (height, taps), 1)
    landed[0] = mm_t(flag(tap == row + group * height), filters[...]).astype(BF16)
    u[...] = product_of(key[...], value[...])
    r[...] = product_of(cot[...], query[...])

    gathered_in(others + peers)
    along = [
        remote(landed.at[0], landed.at[step], (ch_send, ch_recv), step - 1, peers[step - 1])
        for step in range(1, ch)
    ]
    for copy in along[::-1]:
        copy.start()
    has_next, has_prev = me < ctx - 1, me > 0
    right, left = [], []
    for c in range(chunks):
        lanes = pl.ds(c * block, block)
        for kind, field in enumerate((u, r)):
            right.append(remote(field.at[:, lanes], halos.at[kind, :, lanes],
                                (halo_send, halo_recv), c * 4 + kind, after))
            left.append(remote(field.at[:, lanes], halos.at[2 + kind, :, lanes],
                               (halo_send, halo_recv), c * 4 + 2 + kind, before))
    for to_next, to_prev in zip(right, left):
        @pl.when(has_next)
        def _():
            to_next.start()

        @pl.when(has_prev)
        def _():
            to_prev.start()

    @pl.when(jnp.logical_not(has_prev))
    def _():
        halos[0:2] = jnp.zeros((2, rows, channels), BF16)

    @pl.when(jnp.logical_not(has_next))
    def _():
        halos[2:4] = jnp.zeros((2, rows, channels), BF16)

    long_lane, short_lane, long_column, short_column, seen, seen_column, base, last = survey(
        lens, rows, me * rows
    )
    quarter = rows // PACK
    packed_row = (lax.broadcasted_iota(jnp.int32, (size, 1), 0) % rows) // quarter
    packed_lane = (lax.broadcasted_iota(jnp.int32, (1, size), 1) % rows) // quarter
    for s in range(slots):
        cols = pl.ds(s * size, size)
        if s < longs:
            masked[s] = analyse[:, rows : 2 * rows] * flag(long_lane == s + 1)
            back[:, cols] = rebuild[...] * flag(long_column == s + 1)
        else:
            first = (s - longs) * PACK + 1
            masked[s] = analyse_short[...] * flag(short_lane == first + packed_row)
            back[:, cols] = rebuild_short[...] * flag(short_column == first + packed_lane)
    for e, code in enumerate((base, last)):
        section = slice(2 * e * rows, (2 * e + 1) * rows)
        outer[e] = analyse[:, section] * flag(seen[:, section] == code)
        own_ends[e] = analyse[:, rows : 2 * rows] * flag(seen[:, rows : 2 * rows] == code)
        back_outer[:, pl.ds(e * size, size)] = rebuild[...] * flag(seen_column == code)

    ahead[...] = mm_t(causal_hi[...], filters[...]) + mm_t(causal_lo[...], filters[...])

    def analysis(c, carry):
        lanes = pl.ds(pl.multiple_of(c * block, LANES), block)
        u_own, r_own = u[:, lanes], r[:, lanes]
        for s in range(slots):
            u_now, o_now = mm(masked[s], u_own), mm(masked[s], r_own)
            u_hat[s, :, lanes] = u_now
            o_hat[s, :, lanes] = o_now
            g_re, g_im = times_conj(u_now, o_now)
            kind = 0 if s < longs else 1
            if s == 0 or s == longs:
                acc_g[kind, :rows, lanes] = g_re
                acc_g[kind, rows:, lanes] = g_im
            else:
                acc_g[kind, :rows, lanes] += g_re
                acc_g[kind, rows:, lanes] += g_im
        for e in range(2):
            ends_hat[e, :, lanes] = mm(own_ends[e], r_own)
        own = jnp.concatenate([acc_g[0, :, lanes], acc_g[1, :, lanes]], axis=0)
        acc_t[0, :, lanes] = mm_fine(fwd_hi[...], fwd_lo[...], own)
        acc_t[1, :, lanes] = mm_fine(bwd_hi[...], bwd_lo[...], own)
        return carry

    lax.fori_loop(0, chunks, analysis, 0)

    for copy in along:
        copy.wait()
    picked[...] = pick_partners(complement[...], landed, ch, channels).astype(BF16)
    shared = [
        remote(picked, partner.at[group], (mate_send, mate_recv), step - 1, mates[step - 1])
        for step in range(1, groups)
    ]
    for copy in shared:
        copy.start()
    keep = pltpu.make_async_copy(picked, partner.at[group], local.at[0])
    keep.start()
    for copy in shared:
        copy.wait()
    keep.wait()
    g = partner[...].reshape(taps, channels)
    behind[...] = mm(anti_hi[...], g) + mm(anti_lo[...], g)
    both[...] = ahead[...] + behind[...]

    def filtering(c, carry):
        lanes = pl.ds(pl.multiple_of(c * block, LANES), block)
        for s in range(slots):
            kind = 0 if s < longs else 1
            h = both[kind * size : (kind + 1) * size, lanes]
            z_re, z_im = times(h, u_hat[s, :, lanes])
            q_re, q_im = times_conj(h, o_hat[s, :, lanes])
            z_ref[s * size : s * size + rows] = z_re.astype(BF16)
            z_ref[s * size + rows : (s + 1) * size] = z_im.astype(BF16)
            q_ref[s * size : s * size + rows] = q_re.astype(BF16)
            q_ref[s * size + rows : (s + 1) * size] = q_im.astype(BF16)
        acc_y[:, lanes] = mm(back[...], z_ref[...])
        acc_p[:, lanes] = mm(back[...], q_ref[...])
        return carry

    lax.fori_loop(0, chunks, filtering, 0)

    sums, stores = [], []
    for c in range(chunks):
        lanes = pl.ds(c * block, block)
        for kind in range(2):
            to_next, to_prev = right[c * 2 + kind], left[c * 2 + kind]

            @pl.when(has_next)
            def _():
                to_next.wait_send()
                to_prev.wait_recv()

            @pl.when(has_prev)
            def _():
                to_prev.wait_send()
                to_next.wait_recv()

        for e in range(2):
            u_far = mm(outer[e], halos[2 * e, :, lanes])
            r_far = mm(outer[e], halos[2 * e + 1, :, lanes])
            for_u, for_r = (ahead, behind) if e == 0 else (behind, ahead)
            z_re, z_im = times(for_u[:size, lanes], u_far)
            q_re, q_im = times_conj(for_r[:size, lanes], r_far)
            z_ref[e * size : e * size + rows] = z_re.astype(BF16)
            z_ref[e * size + rows : (e + 1) * size] = z_im.astype(BF16)
            q_ref[e * size : e * size + rows] = q_re.astype(BF16)
            q_ref[e * size + rows : (e + 1) * size] = q_im.astype(BF16)
            g_re, g_im = times_conj(u_far, ends_hat[e, :, lanes])
            hi, lo = (fwd_hi, fwd_lo) if e == 0 else (bwd_hi, bwd_lo)
            far = jnp.concatenate([g_re, g_im], axis=0)
            tap_sums = acc_t[e, :, lanes] + mm_fine(hi[:, :size], lo[:, :size], far)
            for i in range(ctx):
                pieces[e, i, :, lanes] = tap_sums[i * share : (i + 1) * share].astype(BF16)
        for step in range(1, ctx):
            copy = remote(pieces.at[:, (me + step) % ctx, :, lanes], arrived.at[step, :, :, lanes],
                          (sum_send, sum_recv), c * (ctx - 1) + step - 1, others[step - 1])
            copy.start()
            sums.append(copy)
        combined = acc_y[:, lanes] + mm(back_outer[...], z_ref[: 2 * size])
        grad_product = acc_p[:, lanes] + mm(back_outer[...], q_ref[: 2 * size])
        outs[0, :, lanes] = (query[:, lanes].astype(F32) * combined).astype(BF16)
        outs[1, :, lanes] = (cot[:, lanes].astype(F32) * combined).astype(BF16)
        outs[2, :, lanes] = (grad_product * value[:, lanes].astype(F32)).astype(BF16)
        outs[3, :, lanes] = (grad_product * key[:, lanes].astype(F32)).astype(BF16)
    for index, place in enumerate((mixer_out, grad_query, grad_key, grad_value)):
        copy = pltpu.make_async_copy(outs.at[index], place, local.at[1 + index])
        copy.start()
        stores.append(copy)

    if share < sent.shape[1]:
        sent[...] = jnp.zeros_like(sent)
    arrived[0] = pieces[:, me]
    for copy in sums:
        copy.wait()
    sent[0, :share] = sum(arrived[step, 1].astype(F32) for step in range(ctx)).astype(BF16)
    across = [
        remote(sent.at[0], sent.at[step], (back_send, back_recv), step - 1, peers[step - 1]) for step in range(1, ch)
    ]
    for copy in across:
        copy.start()
    own = sum(arrived[step, 0].astype(F32) for step in range(ctx))
    for copy in across:
        copy.wait()
    grad[...] = own + pick_partners(complement[...], sent, ch, channels)[:share]
    for copy in stores:
        copy.wait()


def channel_block(channels):
    for block in (384, 256, 128):
        if channels % block == 0:
            return block
    return channels


def shards(query_input, key_input, value_input, filters, complement, doc_lengths, cotangent):
    rows, channels = query_input.shape
    taps = filters.shape[1]
    ctx, ch = lax.axis_size("ctx"), lax.axis_size("ch")
    groups = min(ctx, taps // TILE)
    height, share, size = taps // groups, taps // ctx, 2 * rows
    block = channel_block(channels)
    chunks = channels // block
    slots = PACK - 1 + -(-doc_lengths.shape[0] // PACK)
    tables = fourier_tables(rows, taps)
    hbm = pl.BlockSpec(memory_space=pl.ANY)
    vmem = pl.BlockSpec(memory_space=pltpu.VMEM)
    dma = pltpu.SemaphoreType.DMA
    field = jax.ShapeDtypeStruct((rows, channels), BF16)
    *mixed, grad_filter = pl.pallas_call(
        functools.partial(mixer_kernel, ctx, ch, groups, block),
        in_specs=[pl.BlockSpec(memory_space=pltpu.SMEM)] + [vmem] * (6 + len(tables)),
        out_specs=[hbm] * 4 + [vmem],
        out_shape=[field] * 4 + [jax.ShapeDtypeStruct((share, channels), F32)],
        scratch_shapes=[
            pltpu.VMEM((rows, channels), BF16),
            pltpu.VMEM((rows, channels), BF16),
            pltpu.VMEM((4, rows, channels), BF16),
            pltpu.VMEM((ch, height, channels), BF16),
            pltpu.VMEM((height, channels), BF16),
            pltpu.VMEM((groups, height, channels), BF16),
            pltpu.VMEM((4, rows, channels), BF16),
            pltpu.VMEM((2, ctx, share, channels), BF16),
            pltpu.VMEM((ctx, 2, share, channels), BF16),
            pltpu.VMEM((ch, -(-share // TILE) * TILE, channels), BF16),
            pltpu.VMEM((slots, size, rows), BF16),
            pltpu.VMEM((rows, slots * size), BF16),
            pltpu.VMEM((2, size, rows), BF16),
            pltpu.VMEM((rows, 2 * size), BF16),
            pltpu.VMEM((2, size, rows), BF16),
            pltpu.VMEM((2 * size, channels), F32),
            pltpu.VMEM((2 * size, channels), F32),
            pltpu.VMEM((2 * size, channels), F32),
            pltpu.VMEM((slots, size, channels), F32),
            pltpu.VMEM((slots, size, channels), F32),
            pltpu.VMEM((2, size, channels), F32),
            pltpu.VMEM((2, size, channels), F32),
            pltpu.VMEM((slots * size, block), BF16),
            pltpu.VMEM((slots * size, block), BF16),
            pltpu.VMEM((rows, channels), F32),
            pltpu.VMEM((rows, channels), F32),
            pltpu.VMEM((2, taps, channels), F32),
            dma((4 * chunks,)), dma((4 * chunks,)), dma((ch - 1,)), dma((ch - 1,)),
            dma((groups - 1,)), dma((groups - 1,)),
            dma(((ctx - 1) * chunks,)), dma(((ctx - 1) * chunks,)), dma((ch - 1,)), dma((ch - 1,)), dma((5,)),
        ],
        compiler_params=pltpu.CompilerParams(
            collective_id=0, has_side_effects=True, vmem_limit_bytes=VMEM_BYTES
        ),
        name="mixer",
    )(
        doc_lengths, query_input, key_input, value_input, cotangent, filters,
        complement.reshape(1, channels), *[jnp.asarray(t) for t in tables],
    )
    return (*mixed, grad_filter.T)


def solution(mesh):
    placed = (
        P("ctx", "ch"),
        P("ctx", "ch"),
        P("ctx", "ch"),
        P("ch", None),
        P("ch"),
        P(),
        P("ctx", "ch"),
    )
    return jax.shard_map(
        shards,
        mesh=mesh,
        in_specs=placed,
        out_specs=(P("ctx", "ch"), P("ctx", "ch"), P("ctx", "ch"), P("ctx", "ch"), P("ch", "ctx")),
        check_vma=False,
    )
```

```python
import functools

import jax
import jax.numpy as jnp
import numpy as np
from jax import lax
from jax.experimental import pallas as pl
from jax.experimental.pallas import tpu as pltpu
from jax.sharding import PartitionSpec as P

F32, BF16 = jnp.float32, jnp.bfloat16
LANES, TILE, PACK = 128, 16, 4
VMEM_BYTES = 56 * 2**20


def split_bf16(table):
    high = table.astype(BF16)
    low = (table - high.astype(np.float64)).astype(BF16)
    return high, low


def wave(places, length):
    angle = 2.0 * np.pi * (np.arange(length // 2) + 0.5) / length
    turns = angle[:, None] * np.asarray(places)[None, :]
    return np.cos(turns), np.sin(turns)


def fourier_tables(rows, taps):
    long, short = 2 * rows, 2 * rows // PACK
    cos, sin = wave(np.arange(3 * rows) - rows, long)
    analyse = np.concatenate([cos, -sin], axis=0)
    cos_s, sin_s = wave(np.arange(rows), short)
    pack = lambda table: np.tile(table, (PACK, 1))
    analyse_short = np.concatenate([pack(cos_s), pack(-sin_s)], axis=0)
    near = (np.arange(taps) < short // 2)[None, :]
    lag_cos, lag_sin = wave(np.arange(taps), long)
    near_cos, near_sin = [pack(table * near) for table in wave(np.arange(taps), short)]
    causal = np.concatenate([lag_cos, -lag_sin, near_cos, -near_sin], axis=0)
    anti = np.concatenate([lag_cos, lag_sin, near_cos, near_sin], axis=0)
    forward = causal.T.copy()
    backward = anti.T.copy()
    for table in (forward, backward):
        table[:, : 2 * rows] *= 2.0 / long
        table[:, 2 * rows :] *= 2.0 / short
    rebuild = analyse[:, rows : 2 * rows].T * (2.0 / long)
    rebuild_short = analyse_short.T * (2.0 / short)
    return (
        analyse.astype(BF16),
        analyse_short.astype(BF16),
        rebuild.astype(BF16),
        rebuild_short.astype(BF16),
        *split_bf16(causal),
        *split_bf16(anti),
        *split_bf16(forward),
        *split_bf16(backward),
    )


def mm(a, b):
    return jnp.dot(a, b, preferred_element_type=F32)


def mm_t(a, b):
    return lax.dot_general(a, b, (((1,), (1,)), ((), ())), preferred_element_type=F32)


def mm_fine(hi, lo, x):
    x_hi = x.astype(BF16)
    x_lo = (x - x_hi.astype(F32)).astype(BF16)
    return mm(hi, x_hi) + mm(hi, x_lo) + mm(lo, x_hi)


def product_of(a, b):
    return (a.astype(F32) * b.astype(F32)).astype(BF16)


def flag(mask):
    return mask.astype(F32).astype(BF16)


def times(a, x):
    half = a.shape[0] // 2
    a_re, a_im, x_re, x_im = a[:half], a[half:], x[:half], x[half:]
    return a_re * x_re - a_im * x_im, a_re * x_im + a_im * x_re


def times_conj(a, x):
    half = a.shape[0] // 2
    a_re, a_im, x_re, x_im = a[:half], a[half:], x[:half], x[half:]
    return a_re * x_re + a_im * x_im, a_re * x_im - a_im * x_re


def remote(src, dst, sems, index, device):
    return pltpu.make_async_remote_copy(
        src_ref=src, dst_ref=dst, send_sem=sems[0].at[index], recv_sem=sems[1].at[index],
        device_id=device, device_id_type=pl.DeviceIdType.MESH,
    )


def announce(devices):
    barrier = pltpu.get_barrier_semaphore()
    for device in devices:
        pl.semaphore_signal(barrier, inc=1, device_id=device, device_id_type=pl.DeviceIdType.MESH)


def gathered_in(devices):
    pl.semaphore_wait(pltpu.get_barrier_semaphore(), len(devices))


def pick_partners(complement, landed, ch, channels):
    mine = lax.axis_index("ch")
    owner = sum((complement >= k * channels).astype(jnp.int32) for k in range(1, ch)) + jnp.zeros_like(complement)
    step = mine - owner
    step = jnp.where(step < 0, step + ch, step)
    local = complement - owner * channels
    blocks = channels // LANES
    block = step * blocks + lax.shift_right_logical(local, 7)
    within = lax.bitwise_and(local, LANES - 1)
    sublane = lax.broadcasted_iota(jnp.int32, (LANES, channels), 0)
    chosen = flag(sublane == within)
    stacked = jnp.concatenate(
        [landed[s, :, b * LANES : (b + 1) * LANES] for s in range(ch) for b in range(blocks)], axis=0
    )
    spread_out = mm(stacked, chosen)
    height = landed.shape[1]
    total = jnp.zeros((height, channels), F32)
    for b in range(ch * blocks):
        total = total + jnp.where(block == b, spread_out[b * height : (b + 1) * height], 0.0)
    return total


def survey(lens, rows, first_place):
    limit = rows // PACK
    lane3 = lax.broadcasted_iota(jnp.int32, (1, 3 * rows), 1) - rows
    lane = lax.broadcasted_iota(jnp.int32, (1, rows), 1)
    column = lax.broadcasted_iota(jnp.int32, (rows, 1), 0)
    low = -first_place
    found, base, last = jnp.int32(0), jnp.int32(0), jnp.int32(0)
    seen = jnp.zeros_like(lane3)
    seen_column = jnp.zeros_like(column)
    long_lane, short_lane = jnp.zeros_like(lane), jnp.zeros_like(lane)
    long_column, short_column = jnp.zeros_like(column), jnp.zeros_like(column)
    for d in range(lens.shape[0]):
        high = low + lens[d]
        own = jnp.minimum(high, rows) - jnp.maximum(low, 0)
        is_long = jnp.where(own > limit, 1, 0)
        found = found + is_long
        long_code = is_long * found
        short_code = (1 - is_long) * (d + 1)
        inside = (lane >= low) & (lane < high)
        long_lane = jnp.where(inside, long_code, long_lane)
        short_lane = jnp.where(inside, short_code, short_lane)
        inside = (column >= low) & (column < high)
        long_column = jnp.where(inside, long_code, long_column)
        short_column = jnp.where(inside, short_code, short_column)
        seen = seen + jnp.where(lane3 >= low, 1, 0)
        seen_column = seen_column + jnp.where(column >= low, 1, 0)
        base = base + jnp.where(low <= 0, 1, 0)
        last = last + jnp.where(low <= rows - 1, 1, 0)
        low = high
    seen = seen + jnp.where(lane3 >= low, 1, 0)
    return long_lane, short_lane, long_column, short_column, seen, seen_column, base, last


def mixer_kernel(
    ctx, ch, groups, block, relay,
    lens, query, key, value, cot, filters, complement,
    analyse, analyse_short, rebuild, rebuild_short,
    causal_hi, causal_lo, anti_hi, anti_lo, fwd_hi, fwd_lo, bwd_hi, bwd_lo,
    mixer_out, grad_query, grad_key, grad_value, grad,
    u, r, halos, via, landed, picked, partner, outs, pieces, arrived, sent,
    masked, back, outer, back_outer, own_ends,
    ahead, behind, both, u_hat, o_hat, ends_hat, acc_g, z_ref, q_ref, acc_y, acc_p, acc_t,
    halo_send, halo_recv, via_send, via_recv, ch_send, ch_recv, mate_send, mate_recv,
    sum_send, sum_recv, back_send, back_recv, local,
):
    me, mine = lax.axis_index("ctx"), lax.axis_index("ch")
    rows, channels = query.shape
    taps = filters.shape[1]
    size = 2 * rows
    chunks = channels // block
    slots = masked.shape[0]
    longs = PACK - 1
    after, before = {"ctx": (me + 1) % ctx}, {"ctx": (me + ctx - 1) % ctx}
    group, octet = me % groups, me - me % groups
    height = taps // groups
    share = grad.shape[0]
    others = [{"ctx": (me + step) % ctx} for step in range(1, ctx)]
    peers = [{"ch": (mine + step) % ch} for step in range(1, ch)]
    mates = [{"ctx": octet + (group + step) % groups} for step in range(1, groups)]
    announce(others + peers)

    row = lax.broadcasted_iota(jnp.int32, (height, taps), 0)
    tap = lax.broadcasted_iota(jnp.int32, (height, taps), 1)
    landed[0] = mm_t(flag(tap == row + group * height), filters[...]).astype(BF16)
    u[...] = product_of(key[...], value[...])
    r[...] = product_of(cot[...], query[...])

    gathered_in(others + peers)
    along = [
        remote(landed.at[0], landed.at[step], (ch_send, ch_recv), step - 1, peers[step - 1])
        for step in range(1, ch)
    ]
    for copy in along[::-1]:
        copy.start()
    has_next, has_prev = me < ctx - 1, me > 0
    middle = ctx // 2 - 1
    at_middle = (me == middle) | (me == middle + 1)
    end = jnp.where(me == middle, ctx - 1, 0)
    starts, send_waits, recv_waits, forwards = [], [], [], []
    for c in range(chunks):
        lanes = pl.ds(c * block, block)
        for kind, field in enumerate((u, r)):
            index = c * 2 + kind
            detour = relay and index >= chunks
            to_next = remote(field.at[:, lanes], halos.at[kind, :, lanes],
                             (halo_send, halo_recv), c * 4 + kind, after)
            to_prev = remote(field.at[:, lanes], halos.at[2 + kind, :, lanes],
                             (halo_send, halo_recv), c * 4 + 2 + kind, before)
            starts.append([(has_next & (me != middle) if detour else has_next, to_next),
                           (has_prev & (me != middle + 1) if detour else has_prev, to_prev)])
            send_waits += starts[-1]
            recv_waits.append([(has_prev, to_next), (has_next, to_prev)])
            if detour:
                away = remote(field.at[:, lanes], via.at[kind, :, lanes], (via_send, via_recv), index, {"ctx": end})
                starts[-1].append((at_middle, away))
                send_waits.append((at_middle, away))
                from_last = remote(via.at[kind, :, lanes], halos.at[kind, :, lanes],
                                   (halo_send, halo_recv), c * 4 + kind, {"ctx": middle + 1})
                from_first = remote(via.at[kind, :, lanes], halos.at[2 + kind, :, lanes],
                                    (halo_send, halo_recv), c * 4 + 2 + kind, {"ctx": middle})
                forwards.append((away, from_last, from_first))

    def start_halos(chunk):
        for condition, copy in starts[2 * chunk] + starts[2 * chunk + 1]:
            pl.when(condition)(copy.start)

    start_halos(0)

    @pl.when(jnp.logical_not(has_prev))
    def _():
        halos[0:2] = jnp.zeros((2, rows, channels), BF16)

    @pl.when(jnp.logical_not(has_next))
    def _():
        halos[2:4] = jnp.zeros((2, rows, channels), BF16)

    long_lane, short_lane, long_column, short_column, seen, seen_column, base, last = survey(
        lens, rows, me * rows
    )
    quarter = rows // PACK
    packed_row = (lax.broadcasted_iota(jnp.int32, (size, 1), 0) % rows) // quarter
    packed_lane = (lax.broadcasted_iota(jnp.int32, (1, size), 1) % rows) // quarter
    for s in range(slots):
        cols = pl.ds(s * size, size)
        if s < longs:
            masked[s] = analyse[:, rows : 2 * rows] * flag(long_lane == s + 1)
            back[:, cols] = rebuild[...] * flag(long_column == s + 1)
        else:
            first = (s - longs) * PACK + 1
            masked[s] = analyse_short[...] * flag(short_lane == first + packed_row)
            back[:, cols] = rebuild_short[...] * flag(short_column == first + packed_lane)
    for e, code in enumerate((base, last)):
        section = slice(2 * e * rows, (2 * e + 1) * rows)
        outer[e] = analyse[:, section] * flag(seen[:, section] == code)
        own_ends[e] = analyse[:, rows : 2 * rows] * flag(seen[:, rows : 2 * rows] == code)
        back_outer[:, pl.ds(e * size, size)] = rebuild[...] * flag(seen_column == code)

    ahead[...] = mm_t(causal_hi[...], filters[...]) + mm_t(causal_lo[...], filters[...])

    def analysis(c, carry):
        lanes = pl.ds(pl.multiple_of(c * block, LANES), block)
        u_own, r_own = u[:, lanes], r[:, lanes]
        for s in range(slots):
            u_now, o_now = mm(masked[s], u_own), mm(masked[s], r_own)
            u_hat[s, :, lanes] = u_now
            o_hat[s, :, lanes] = o_now
            g_re, g_im = times_conj(u_now, o_now)
            kind = 0 if s < longs else 1
            if s == 0 or s == longs:
                acc_g[kind, :rows, lanes] = g_re
                acc_g[kind, rows:, lanes] = g_im
            else:
                acc_g[kind, :rows, lanes] += g_re
                acc_g[kind, rows:, lanes] += g_im
        for e in range(2):
            ends_hat[e, :, lanes] = mm(own_ends[e], r_own)
        own = jnp.concatenate([acc_g[0, :, lanes], acc_g[1, :, lanes]], axis=0)
        acc_t[0, :, lanes] = mm_fine(fwd_hi[...], fwd_lo[...], own)
        acc_t[1, :, lanes] = mm_fine(bwd_hi[...], bwd_lo[...], own)
        return carry

    analysis(0, 0)

    for copy in along:
        copy.wait()
    picked[...] = pick_partners(complement[...].reshape(1, channels), landed, ch, channels).astype(BF16)
    shared = [
        remote(picked, partner.at[group], (mate_send, mate_recv), step - 1, mates[step - 1])
        for step in range(1, groups)
    ]
    for copy in shared:
        copy.start()
    keep = pltpu.make_async_copy(picked, partner.at[group], local.at[0])
    keep.start()
    for chunk in range(1, chunks):
        start_halos(chunk)
    lax.fori_loop(1, chunks, analysis, 0)
    for copy in shared:
        copy.wait()
    keep.wait()
    for arriving, from_last, from_first in forwards:
        @pl.when(me == ctx - 1)
        def _():
            arriving.wait_recv()
            from_last.start()

        @pl.when(me == 0)
        def _():
            arriving.wait_recv()
            from_first.start()

    g = partner[...].reshape(taps, channels)
    behind[...] = mm(anti_hi[...], g) + mm(anti_lo[...], g)
    both[...] = ahead[...] + behind[...]

    def filtering(c, carry):
        lanes = pl.ds(pl.multiple_of(c * block, LANES), block)
        for s in range(slots):
            kind = 0 if s < longs else 1
            h = both[kind * size : (kind + 1) * size, lanes]
            z_re, z_im = times(h, u_hat[s, :, lanes])
            q_re, q_im = times_conj(h, o_hat[s, :, lanes])
            z_ref[s * size : s * size + rows] = z_re.astype(BF16)
            z_ref[s * size + rows : (s + 1) * size] = z_im.astype(BF16)
            q_ref[s * size : s * size + rows] = q_re.astype(BF16)
            q_ref[s * size + rows : (s + 1) * size] = q_im.astype(BF16)
        acc_y[:, lanes] = mm(back[...], z_ref[...])
        acc_p[:, lanes] = mm(back[...], q_ref[...])
        return carry

    sums, stores = [], []
    for c in range(chunks):
        lanes = pl.ds(c * block, block)
        filtering(c, 0)
        for condition, copy in recv_waits[2 * c] + recv_waits[2 * c + 1]:
            pl.when(condition)(copy.wait_recv)
        for e in range(2):
            u_far = mm(outer[e], halos[2 * e, :, lanes])
            r_far = mm(outer[e], halos[2 * e + 1, :, lanes])
            for_u, for_r = (ahead, behind) if e == 0 else (behind, ahead)
            z_re, z_im = times(for_u[:size, lanes], u_far)
            q_re, q_im = times_conj(for_r[:size, lanes], r_far)
            z_ref[e * size : e * size + rows] = z_re.astype(BF16)
            z_ref[e * size + rows : (e + 1) * size] = z_im.astype(BF16)
            q_ref[e * size : e * size + rows] = q_re.astype(BF16)
            q_ref[e * size + rows : (e + 1) * size] = q_im.astype(BF16)
            g_re, g_im = times_conj(u_far, ends_hat[e, :, lanes])
            hi, lo = (fwd_hi, fwd_lo) if e == 0 else (bwd_hi, bwd_lo)
            far = jnp.concatenate([g_re, g_im], axis=0)
            tap_sums = acc_t[e, :, lanes] + mm_fine(hi[:, :size], lo[:, :size], far)
            for i in range(ctx):
                pieces[e, i, :, lanes] = tap_sums[i * share : (i + 1) * share].astype(BF16)
        for step in range(1, ctx):
            copy = remote(pieces.at[:, (me + step) % ctx, :, lanes], arrived.at[step, :, :, lanes],
                          (sum_send, sum_recv), c * (ctx - 1) + step - 1, others[step - 1])
            copy.start()
            sums.append(copy)
        combined = acc_y[:, lanes] + mm(back_outer[...], z_ref[: 2 * size])
        grad_product = acc_p[:, lanes] + mm(back_outer[...], q_ref[: 2 * size])
        outs[0, :, lanes] = (query[:, lanes].astype(F32) * combined).astype(BF16)
        outs[1, :, lanes] = (cot[:, lanes].astype(F32) * combined).astype(BF16)
        outs[2, :, lanes] = (grad_product * value[:, lanes].astype(F32)).astype(BF16)
        outs[3, :, lanes] = (grad_product * key[:, lanes].astype(F32)).astype(BF16)
    for index, place in enumerate((mixer_out, grad_query, grad_key, grad_value)):
        copy = pltpu.make_async_copy(outs.at[index], place, local.at[1 + index])
        copy.start()
        stores.append(copy)

    if share < sent.shape[1]:
        sent[...] = jnp.zeros_like(sent)
    arrived[0] = pieces[:, me]
    across = []
    for c in range(chunks):
        lanes = pl.ds(c * block, block)
        for copy in sums[c * (ctx - 1) : (c + 1) * (ctx - 1)]:
            copy.wait()
        sent[0, :share, lanes] = sum(arrived[step, 1, :, lanes].astype(F32) for step in range(ctx)).astype(BF16)
        for step in range(1, ch):
            copy = remote(sent.at[0, :, lanes], sent.at[step, :, lanes],
                          (back_send, back_recv), c * (ch - 1) + step - 1, peers[step - 1])
            copy.start()
            across.append(copy)
    own = sum(arrived[step, 0].astype(F32) for step in range(ctx))
    for condition, copy in send_waits:
        pl.when(condition)(copy.wait_send)
    for _, from_last, from_first in forwards:
        pl.when(me == ctx - 1)(from_last.wait_send)
        pl.when(me == 0)(from_first.wait_send)
    for copy in across:
        copy.wait()
    grad[...] = own + pick_partners(complement[...].reshape(1, channels), sent, ch, channels)[:share]
    for copy in stores:
        copy.wait()


def channel_block(channels):
    for block in (384, 256, 128):
        if channels % block == 0:
            return block
    return channels


def hand_over_kernel(*refs):
    count = len(refs) // 2
    copies = [pltpu.make_async_copy(refs[i], refs[count + i], refs[-1].at[i]) for i in range(count)]
    for copy in copies:
        copy.start()
    for copy in copies:
        copy.wait()


def hand_over(*arrays):
    hbm = pl.BlockSpec(memory_space=pl.ANY)
    return pl.pallas_call(
        hand_over_kernel,
        in_specs=[hbm] * len(arrays),
        out_specs=[hbm] * len(arrays),
        out_shape=[jax.ShapeDtypeStruct(a.shape, a.dtype) for a in arrays],
        scratch_shapes=[pltpu.SemaphoreType.DMA((len(arrays),))],
        name="hand_over",
    )(*arrays)


def needs_relay(mesh):
    axis = mesh.axis_names.index("ctx")
    line = np.moveaxis(mesh.devices, axis, 0).reshape(mesh.shape["ctx"], -1)[:, 0]
    places = [getattr(device, "coords", None) for device in line]
    if any(place is None for place in places) or len(places) < 4:
        return False
    hops = lambda a, b: sum(abs(x - y) for x, y in zip(places[a], places[b]))
    middle, end = len(places) // 2 - 1, len(places) - 1
    return (
        hops(middle, middle + 1) == 2
        and hops(middle, end) == hops(end, middle + 1) == 1
        and hops(middle + 1, 0) == hops(0, middle) == 1
    )


def shards(relay, query_input, key_input, value_input, filters, complement, doc_lengths, cotangent):
    rows, channels = query_input.shape
    taps = filters.shape[1]
    ctx, ch = lax.axis_size("ctx"), lax.axis_size("ch")
    groups = min(ctx, taps // TILE)
    height, share, size = taps // groups, taps // ctx, 2 * rows
    block = channel_block(channels)
    chunks = channels // block
    slots = PACK - 1 + -(-doc_lengths.shape[0] // PACK)
    tables = fourier_tables(rows, taps)
    hbm = pl.BlockSpec(memory_space=pl.ANY)
    vmem = pl.BlockSpec(memory_space=pltpu.VMEM)
    dma = pltpu.SemaphoreType.DMA
    field = jax.ShapeDtypeStruct((rows, channels), BF16)
    *mixed, grad_filter = pl.pallas_call(
        functools.partial(mixer_kernel, ctx, ch, groups, block, relay),
        in_specs=[pl.BlockSpec(memory_space=pltpu.SMEM)] + [vmem] * (6 + len(tables)),
        out_specs=[hbm] * 4 + [vmem],
        out_shape=[field] * 4 + [jax.ShapeDtypeStruct((share, channels), F32)],
        scratch_shapes=[
            pltpu.VMEM((rows, channels), BF16),
            pltpu.VMEM((rows, channels), BF16),
            pltpu.VMEM((4, rows, channels), BF16),
            pltpu.VMEM((2, rows, channels), BF16),
            pltpu.VMEM((ch, height, channels), BF16),
            pltpu.VMEM((height, channels), BF16),
            pltpu.VMEM((groups, height, channels), BF16),
            pltpu.VMEM((4, rows, channels), BF16),
            pltpu.VMEM((2, ctx, share, channels), BF16),
            pltpu.VMEM((ctx, 2, share, channels), BF16),
            pltpu.VMEM((ch, -(-share // TILE) * TILE, channels), BF16),
            pltpu.VMEM((slots, size, rows), BF16),
            pltpu.VMEM((rows, slots * size), BF16),
            pltpu.VMEM((2, size, rows), BF16),
            pltpu.VMEM((rows, 2 * size), BF16),
            pltpu.VMEM((2, size, rows), BF16),
            pltpu.VMEM((2 * size, channels), F32),
            pltpu.VMEM((2 * size, channels), F32),
            pltpu.VMEM((2 * size, channels), F32),
            pltpu.VMEM((slots, size, channels), F32),
            pltpu.VMEM((slots, size, channels), F32),
            pltpu.VMEM((2, size, channels), F32),
            pltpu.VMEM((2, size, channels), F32),
            pltpu.VMEM((slots * size, block), BF16),
            pltpu.VMEM((slots * size, block), BF16),
            pltpu.VMEM((rows, channels), F32),
            pltpu.VMEM((rows, channels), F32),
            pltpu.VMEM((2, taps, channels), F32),
            dma((4 * chunks,)), dma((4 * chunks,)), dma((2 * chunks,)), dma((2 * chunks,)), dma((ch - 1,)), dma((ch - 1,)),
            dma((groups - 1,)), dma((groups - 1,)),
            dma(((ctx - 1) * chunks,)), dma(((ctx - 1) * chunks,)), dma(((ch - 1) * chunks,)), dma(((ch - 1) * chunks,)), dma((5,)),
        ],
        compiler_params=pltpu.CompilerParams(
            collective_id=0, has_side_effects=True, vmem_limit_bytes=VMEM_BYTES
        ),
        name="mixer",
    )(
        doc_lengths, query_input, key_input, value_input, cotangent, filters,
        complement, *[jnp.asarray(t) for t in tables],
    )
    *mixed, grad_filter = hand_over(*mixed, grad_filter)
    return (*mixed, grad_filter.T)


def solution(mesh):
    placed = (
        P("ctx", "ch"),
        P("ctx", "ch"),
        P("ctx", "ch"),
        P("ch", None),
        P("ch"),
        P(),
        P("ctx", "ch"),
    )
    return jax.shard_map(
        functools.partial(shards, needs_relay(mesh)),
        mesh=mesh,
        in_specs=placed,
        out_specs=(P("ctx", "ch"), P("ctx", "ch"), P("ctx", "ch"), P("ctx", "ch"), P("ch", "ctx")),
        check_vma=False,
    )
```

```python
import functools

import jax
import jax.numpy as jnp
import numpy as np
from jax import lax
from jax.experimental import pallas as pl
from jax.experimental.pallas import tpu as pltpu
from jax.sharding import PartitionSpec as P

F32, BF16 = jnp.float32, jnp.bfloat16
LANES, TILE, PACK = 128, 16, 4
VMEM_BYTES = 56 * 2**20


def split_bf16(table):
    high = table.astype(BF16)
    low = (table - high.astype(np.float64)).astype(BF16)
    return high, low


def wave(places, length):
    angle = 2.0 * np.pi * (np.arange(length // 2) + 0.5) / length
    turns = angle[:, None] * np.asarray(places)[None, :]
    return np.cos(turns), np.sin(turns)


def fourier_tables(rows, taps):
    long, short = 2 * rows, 2 * rows // PACK
    cos, sin = wave(np.arange(3 * rows) - rows, long)
    analyse = np.concatenate([cos, -sin], axis=0)
    cos_s, sin_s = wave(np.arange(rows), short)
    pack = lambda table: np.tile(table, (PACK, 1))
    analyse_short = np.concatenate([pack(cos_s), pack(-sin_s)], axis=0)
    near = (np.arange(taps) < short // 2)[None, :]
    lag_cos, lag_sin = wave(np.arange(taps), long)
    near_cos, near_sin = [pack(table * near) for table in wave(np.arange(taps), short)]
    causal = np.concatenate([lag_cos, -lag_sin, near_cos, -near_sin], axis=0)
    anti = np.concatenate([lag_cos, lag_sin, near_cos, near_sin], axis=0)
    forward = causal.T.copy()
    backward = anti.T.copy()
    for table in (forward, backward):
        table[:, : 2 * rows] *= 2.0 / long
        table[:, 2 * rows :] *= 2.0 / short
    rebuild = analyse[:, rows : 2 * rows].T * (2.0 / long)
    rebuild_short = analyse_short.T * (2.0 / short)
    return (
        analyse.astype(BF16),
        analyse_short.astype(BF16),
        rebuild.astype(BF16),
        rebuild_short.astype(BF16),
        *split_bf16(causal),
        *split_bf16(anti),
        *split_bf16(forward),
        *split_bf16(backward),
    )


def mm(a, b):
    return jnp.dot(a, b, preferred_element_type=F32)


def mm_t(a, b):
    return lax.dot_general(a, b, (((1,), (1,)), ((), ())), preferred_element_type=F32)


def mm_fine(hi, lo, x):
    x_hi = x.astype(BF16)
    x_lo = (x - x_hi.astype(F32)).astype(BF16)
    return mm(hi, x_hi) + mm(hi, x_lo) + mm(lo, x_hi)


def product_of(a, b):
    return (a.astype(F32) * b.astype(F32)).astype(BF16)


def flag(mask):
    return mask.astype(F32).astype(BF16)


def times(a, x):
    half = a.shape[0] // 2
    a_re, a_im, x_re, x_im = a[:half], a[half:], x[:half], x[half:]
    return a_re * x_re - a_im * x_im, a_re * x_im + a_im * x_re


def times_conj(a, x):
    half = a.shape[0] // 2
    a_re, a_im, x_re, x_im = a[:half], a[half:], x[:half], x[half:]
    return a_re * x_re + a_im * x_im, a_re * x_im - a_im * x_re


def remote(src, dst, sems, index, device):
    return pltpu.make_async_remote_copy(
        src_ref=src, dst_ref=dst, send_sem=sems[0].at[index], recv_sem=sems[1].at[index],
        device_id=device, device_id_type=pl.DeviceIdType.MESH,
    )


def announce(devices):
    barrier = pltpu.get_barrier_semaphore()
    for device in devices:
        pl.semaphore_signal(barrier, inc=1, device_id=device, device_id_type=pl.DeviceIdType.MESH)


def gathered_in(devices):
    pl.semaphore_wait(pltpu.get_barrier_semaphore(), len(devices))


def pick_partners(complement, landed, ch, channels):
    mine = lax.axis_index("ch")
    owner = sum((complement >= k * channels).astype(jnp.int32) for k in range(1, ch)) + jnp.zeros_like(complement)
    step = mine - owner
    step = jnp.where(step < 0, step + ch, step)
    local = complement - owner * channels
    blocks = channels // LANES
    block = step * blocks + lax.shift_right_logical(local, 7)
    within = lax.bitwise_and(local, LANES - 1)
    sublane = lax.broadcasted_iota(jnp.int32, (LANES, channels), 0)
    chosen = flag(sublane == within)
    stacked = jnp.concatenate(
        [landed[s, :, b * LANES : (b + 1) * LANES] for s in range(ch) for b in range(blocks)], axis=0
    )
    spread_out = mm(stacked, chosen)
    height = landed.shape[1]
    total = jnp.zeros((height, channels), F32)
    for b in range(ch * blocks):
        total = total + jnp.where(block == b, spread_out[b * height : (b + 1) * height], 0.0)
    return total


def survey(lens, rows, first_place):
    limit = rows // PACK
    lane3 = lax.broadcasted_iota(jnp.int32, (1, 3 * rows), 1) - rows
    lane = lax.broadcasted_iota(jnp.int32, (1, rows), 1)
    column = lax.broadcasted_iota(jnp.int32, (rows, 1), 0)
    low = -first_place
    found, base, last = jnp.int32(0), jnp.int32(0), jnp.int32(0)
    seen = jnp.zeros_like(lane3)
    seen_column = jnp.zeros_like(column)
    long_lane, short_lane = jnp.zeros_like(lane), jnp.zeros_like(lane)
    long_column, short_column = jnp.zeros_like(column), jnp.zeros_like(column)
    for d in range(lens.shape[0]):
        high = low + lens[d]
        own = jnp.minimum(high, rows) - jnp.maximum(low, 0)
        is_long = jnp.where(own > limit, 1, 0)
        found = found + is_long
        long_code = is_long * found
        short_code = (1 - is_long) * (d + 1)
        inside = (lane >= low) & (lane < high)
        long_lane = jnp.where(inside, long_code, long_lane)
        short_lane = jnp.where(inside, short_code, short_lane)
        inside = (column >= low) & (column < high)
        long_column = jnp.where(inside, long_code, long_column)
        short_column = jnp.where(inside, short_code, short_column)
        seen = seen + jnp.where(lane3 >= low, 1, 0)
        seen_column = seen_column + jnp.where(column >= low, 1, 0)
        base = base + jnp.where(low <= 0, 1, 0)
        last = last + jnp.where(low <= rows - 1, 1, 0)
        low = high
    seen = seen + jnp.where(lane3 >= low, 1, 0)
    return long_lane, short_lane, long_column, short_column, seen, seen_column, base, last


def mixer_kernel(
    ctx, ch, groups, block, relay,
    lens, query, key, value, cot, filters, complement,
    analyse, analyse_short, rebuild, rebuild_short,
    causal_hi, causal_lo, anti_hi, anti_lo, fwd_hi, fwd_lo, bwd_hi, bwd_lo,
    mixer_out, grad_query, grad_key, grad_value, grad,
    u, r, halos, via, landed, picked, partner, outs, pieces, arrived, sent,
    masked, back, outer, back_outer, own_ends,
    ahead, behind, both, u_hat, o_hat, ends_hat, acc_g, z_ref, q_ref, acc_y, acc_p, acc_t,
    halo_send, halo_recv, via_send, via_recv, ch_send, ch_recv, mate_send, mate_recv,
    sum_send, sum_recv, back_send, back_recv, local,
):
    me, mine = lax.axis_index("ctx"), lax.axis_index("ch")
    rows, channels = query.shape
    taps = filters.shape[1]
    size = 2 * rows
    chunks = channels // block
    slots = masked.shape[0]
    longs = PACK - 1
    after, before = {"ctx": (me + 1) % ctx}, {"ctx": (me + ctx - 1) % ctx}
    group, octet = me % groups, me - me % groups
    height = taps // groups
    share = grad.shape[0]
    others = [{"ctx": (me + step) % ctx} for step in range(1, ctx)]
    peers = [{"ch": (mine + step) % ch} for step in range(1, ch)]
    mates = [{"ctx": octet + (group + step) % groups} for step in range(1, groups)]
    announce(others + peers)

    row = lax.broadcasted_iota(jnp.int32, (height, taps), 0)
    tap = lax.broadcasted_iota(jnp.int32, (height, taps), 1)
    landed[0] = mm_t(flag(tap == row + group * height), filters[...]).astype(BF16)
    u[...] = product_of(key[...], value[...])
    r[...] = product_of(cot[...], query[...])

    gathered_in(others + peers)
    along = [
        remote(landed.at[0], landed.at[step], (ch_send, ch_recv), step - 1, peers[step - 1])
        for step in range(1, ch)
    ]
    for copy in along[::-1]:
        copy.start()
    has_next, has_prev = me < ctx - 1, me > 0
    middle = ctx // 2 - 1
    at_middle = (me == middle) | (me == middle + 1)
    end = jnp.where(me == middle, ctx - 1, 0)
    starts, send_waits, recv_waits, forwards = [], [], [], []
    for c in range(chunks):
        lanes = pl.ds(c * block, block)
        for kind, field in enumerate((u, r)):
            index = c * 2 + kind
            detour = relay and index >= chunks
            to_next = remote(field.at[:, lanes], halos.at[kind, :, lanes],
                             (halo_send, halo_recv), c * 4 + kind, after)
            to_prev = remote(field.at[:, lanes], halos.at[2 + kind, :, lanes],
                             (halo_send, halo_recv), c * 4 + 2 + kind, before)
            starts.append([(has_next & (me != middle) if detour else has_next, to_next),
                           (has_prev & (me != middle + 1) if detour else has_prev, to_prev)])
            send_waits += starts[-1]
            recv_waits.append([(has_prev, to_next), (has_next, to_prev)])
            if detour:
                away = remote(field.at[:, lanes], via.at[kind, :, lanes], (via_send, via_recv), index, {"ctx": end})
                starts[-1].append((at_middle, away))
                send_waits.append((at_middle, away))
                from_last = remote(via.at[kind, :, lanes], halos.at[kind, :, lanes],
                                   (halo_send, halo_recv), c * 4 + kind, {"ctx": middle + 1})
                from_first = remote(via.at[kind, :, lanes], halos.at[2 + kind, :, lanes],
                                    (halo_send, halo_recv), c * 4 + 2 + kind, {"ctx": middle})
                forwards.append((away, from_last, from_first))

    def start_halos(chunk):
        for condition, copy in starts[2 * chunk] + starts[2 * chunk + 1]:
            pl.when(condition)(copy.start)

    start_halos(0)

    @pl.when(jnp.logical_not(has_prev))
    def _():
        halos[0:2] = jnp.zeros((2, rows, channels), BF16)

    @pl.when(jnp.logical_not(has_next))
    def _():
        halos[2:4] = jnp.zeros((2, rows, channels), BF16)

    long_lane, short_lane, long_column, short_column, seen, seen_column, base, last = survey(
        lens, rows, me * rows
    )
    quarter = rows // PACK
    packed_row = (lax.broadcasted_iota(jnp.int32, (size, 1), 0) % rows) // quarter
    packed_lane = (lax.broadcasted_iota(jnp.int32, (1, size), 1) % rows) // quarter
    for s in range(slots):
        cols = pl.ds(s * size, size)
        if s < longs:
            masked[s] = analyse[:, rows : 2 * rows] * flag(long_lane == s + 1)
            back[:, cols] = rebuild[...] * flag(long_column == s + 1)
        else:
            first = (s - longs) * PACK + 1
            masked[s] = analyse_short[...] * flag(short_lane == first + packed_row)
            back[:, cols] = rebuild_short[...] * flag(short_column == first + packed_lane)
    for e, code in enumerate((base, last)):
        section = slice(2 * e * rows, (2 * e + 1) * rows)
        outer[e] = analyse[:, section] * flag(seen[:, section] == code)
        own_ends[e] = analyse[:, rows : 2 * rows] * flag(seen[:, rows : 2 * rows] == code)
        back_outer[:, pl.ds(e * size, size)] = rebuild[...] * flag(seen_column == code)

    ahead[...] = mm_t(causal_hi[...], filters[...]) + mm_t(causal_lo[...], filters[...])

    def analysis(c, carry):
        lanes = pl.ds(pl.multiple_of(c * block, LANES), block)
        u_own, r_own = u[:, lanes], r[:, lanes]
        for s in range(slots):
            u_now, o_now = mm(masked[s], u_own), mm(masked[s], r_own)
            u_hat[s, :, lanes] = u_now
            o_hat[s, :, lanes] = o_now
            g_re, g_im = times_conj(u_now, o_now)
            kind = 0 if s < longs else 1
            if s == 0 or s == longs:
                acc_g[kind, :rows, lanes] = g_re
                acc_g[kind, rows:, lanes] = g_im
            else:
                acc_g[kind, :rows, lanes] += g_re
                acc_g[kind, rows:, lanes] += g_im
        for e in range(2):
            ends_hat[e, :, lanes] = mm(own_ends[e], r_own)
        own = jnp.concatenate([acc_g[0, :, lanes], acc_g[1, :, lanes]], axis=0)
        acc_t[0, :, lanes] = mm_fine(fwd_hi[...], fwd_lo[...], own)
        acc_t[1, :, lanes] = mm_fine(bwd_hi[...], bwd_lo[...], own)
        return carry

    analysis(0, 0)

    for copy in along:
        copy.wait()
    picked[...] = pick_partners(complement[...].reshape(1, channels), landed, ch, channels).astype(BF16)
    shared = [
        remote(picked, partner.at[group], (mate_send, mate_recv), step - 1, mates[step - 1])
        for step in range(1, groups)
    ]
    for copy in shared:
        copy.start()
    keep = pltpu.make_async_copy(picked, partner.at[group], local.at[0])
    keep.start()
    for chunk in range(1, chunks):
        start_halos(chunk)
    lax.fori_loop(1, chunks, analysis, 0)
    for copy in shared:
        copy.wait()
    keep.wait()
    for arriving, from_last, from_first in forwards:
        @pl.when(me == ctx - 1)
        def _():
            arriving.wait_recv()
            from_last.start()

        @pl.when(me == 0)
        def _():
            arriving.wait_recv()
            from_first.start()

    g = partner[...].reshape(taps, channels)
    behind[...] = mm(anti_hi[...], g) + mm(anti_lo[...], g)
    both[...] = ahead[...] + behind[...]

    def filtering(c, carry):
        lanes = pl.ds(pl.multiple_of(c * block, LANES), block)
        for s in range(slots):
            kind = 0 if s < longs else 1
            h = both[kind * size : (kind + 1) * size, lanes]
            z_re, z_im = times(h, u_hat[s, :, lanes])
            q_re, q_im = times_conj(h, o_hat[s, :, lanes])
            z_ref[s * size : s * size + rows] = z_re.astype(BF16)
            z_ref[s * size + rows : (s + 1) * size] = z_im.astype(BF16)
            q_ref[s * size : s * size + rows] = q_re.astype(BF16)
            q_ref[s * size + rows : (s + 1) * size] = q_im.astype(BF16)
        acc_y[:, lanes] = mm(back[...], z_ref[...])
        acc_p[:, lanes] = mm(back[...], q_ref[...])
        return carry

    sums, stores = [], []
    for c in range(chunks):
        lanes = pl.ds(c * block, block)
        filtering(c, 0)
        for condition, copy in recv_waits[2 * c] + recv_waits[2 * c + 1]:
            pl.when(condition)(copy.wait_recv)
        for e in range(2):
            u_far = mm(outer[e], halos[2 * e, :, lanes])
            r_far = mm(outer[e], halos[2 * e + 1, :, lanes])
            for_u, for_r = (ahead, behind) if e == 0 else (behind, ahead)
            z_re, z_im = times(for_u[:size, lanes], u_far)
            q_re, q_im = times_conj(for_r[:size, lanes], r_far)
            z_ref[e * size : e * size + rows] = z_re.astype(BF16)
            z_ref[e * size + rows : (e + 1) * size] = z_im.astype(BF16)
            q_ref[e * size : e * size + rows] = q_re.astype(BF16)
            q_ref[e * size + rows : (e + 1) * size] = q_im.astype(BF16)
            g_re, g_im = times_conj(u_far, ends_hat[e, :, lanes])
            hi, lo = (fwd_hi, fwd_lo) if e == 0 else (bwd_hi, bwd_lo)
            far = jnp.concatenate([g_re, g_im], axis=0)
            tap_sums = acc_t[e, :, lanes] + mm_fine(hi[:, :size], lo[:, :size], far)
            for i in range(ctx):
                pieces[e, i, :, lanes] = tap_sums[i * share : (i + 1) * share].astype(BF16)
        for step in range(1, ctx):
            copy = remote(pieces.at[:, (me + step) % ctx, :, lanes], arrived.at[step, :, :, lanes],
                          (sum_send, sum_recv), c * (ctx - 1) + step - 1, others[step - 1])
            copy.start()
            sums.append(copy)
        combined = acc_y[:, lanes] + mm(back_outer[...], z_ref[: 2 * size])
        grad_product = acc_p[:, lanes] + mm(back_outer[...], q_ref[: 2 * size])
        outs[0, :, lanes] = (query[:, lanes].astype(F32) * combined).astype(BF16)
        outs[1, :, lanes] = (cot[:, lanes].astype(F32) * combined).astype(BF16)
        outs[2, :, lanes] = (grad_product * value[:, lanes].astype(F32)).astype(BF16)
        outs[3, :, lanes] = (grad_product * key[:, lanes].astype(F32)).astype(BF16)
    for index, place in enumerate((mixer_out, grad_query, grad_key, grad_value)):
        copy = pltpu.make_async_copy(outs.at[index], place, local.at[1 + index])
        copy.start()
        stores.append(copy)

    if share < sent.shape[1]:
        sent[...] = jnp.zeros_like(sent)
    arrived[0] = pieces[:, me]
    across = []
    for c in range(chunks):
        lanes = pl.ds(c * block, block)
        for copy in sums[c * (ctx - 1) : (c + 1) * (ctx - 1)]:
            copy.wait()
        sent[0, :share, lanes] = sum(arrived[step, 1, :, lanes].astype(F32) for step in range(ctx)).astype(BF16)
        for step in range(1, ch):
            copy = remote(sent.at[0, :, lanes], sent.at[step, :, lanes],
                          (back_send, back_recv), c * (ch - 1) + step - 1, peers[step - 1])
            copy.start()
            across.append(copy)
    own = sum(arrived[step, 0].astype(F32) for step in range(ctx))
    for condition, copy in send_waits:
        pl.when(condition)(copy.wait_send)
    for _, from_last, from_first in forwards:
        pl.when(me == ctx - 1)(from_last.wait_send)
        pl.when(me == 0)(from_first.wait_send)
    for copy in across:
        copy.wait()
    grad[...] = own + pick_partners(complement[...].reshape(1, channels), sent, ch, channels)[:share]
    for copy in stores:
        copy.wait()


def channel_block(channels):
    for block in (384, 256, 128):
        if channels % block == 0:
            return block
    return channels


def hand_over_kernel(*refs):
    count = (len(refs) - 2) // 3
    given, taken, held, (read, written) = refs[:count], refs[count : 2 * count], refs[2 * count : -2], refs[-2:]
    loads = [pltpu.make_async_copy(given[i], held[i], read.at[i]) for i in range(count)]
    stores = [pltpu.make_async_copy(held[i], taken[i], written.at[i]) for i in range(count)]
    for copy in loads:
        copy.start()
    for load, store in zip(loads, stores):
        load.wait()
        store.start()
    for copy in stores:
        copy.wait()


def hand_over(*arrays):
    hbm = pl.BlockSpec(memory_space=pl.ANY)
    return pl.pallas_call(
        hand_over_kernel,
        in_specs=[hbm] * len(arrays),
        out_specs=[hbm] * len(arrays),
        out_shape=[jax.ShapeDtypeStruct(a.shape, a.dtype) for a in arrays],
        scratch_shapes=[pltpu.VMEM(a.shape, a.dtype) for a in arrays]
        + [pltpu.SemaphoreType.DMA((len(arrays),))] * 2,
        name="hand_over",
    )(*arrays)


def needs_relay(mesh):
    axis = mesh.axis_names.index("ctx")
    line = np.moveaxis(mesh.devices, axis, 0).reshape(mesh.shape["ctx"], -1)[:, 0]
    places = [getattr(device, "coords", None) for device in line]
    if any(place is None for place in places) or len(places) < 4:
        return False
    hops = lambda a, b: sum(abs(x - y) for x, y in zip(places[a], places[b]))
    middle, end = len(places) // 2 - 1, len(places) - 1
    return (
        hops(middle, middle + 1) == 2
        and hops(middle, end) == hops(end, middle + 1) == 1
        and hops(middle + 1, 0) == hops(0, middle) == 1
    )


def shards(relay, query_input, key_input, value_input, filters, complement, doc_lengths, cotangent):
    rows, channels = query_input.shape
    taps = filters.shape[1]
    ctx, ch = lax.axis_size("ctx"), lax.axis_size("ch")
    groups = min(ctx, taps // TILE)
    height, share, size = taps // groups, taps // ctx, 2 * rows
    block = channel_block(channels)
    chunks = channels // block
    slots = PACK - 1 + -(-doc_lengths.shape[0] // PACK)
    tables = fourier_tables(rows, taps)
    hbm = pl.BlockSpec(memory_space=pl.ANY)
    vmem = pl.BlockSpec(memory_space=pltpu.VMEM)
    dma = pltpu.SemaphoreType.DMA
    field = jax.ShapeDtypeStruct((rows, channels), BF16)
    *mixed, grad_filter = pl.pallas_call(
        functools.partial(mixer_kernel, ctx, ch, groups, block, relay),
        in_specs=[pl.BlockSpec(memory_space=pltpu.SMEM)] + [vmem] * (6 + len(tables)),
        out_specs=[hbm] * 4 + [vmem],
        out_shape=[field] * 4 + [jax.ShapeDtypeStruct((share, channels), F32)],
        scratch_shapes=[
            pltpu.VMEM((rows, channels), BF16),
            pltpu.VMEM((rows, channels), BF16),
            pltpu.VMEM((4, rows, channels), BF16),
            pltpu.VMEM((2, rows, channels), BF16),
            pltpu.VMEM((ch, height, channels), BF16),
            pltpu.VMEM((height, channels), BF16),
            pltpu.VMEM((groups, height, channels), BF16),
            pltpu.VMEM((4, rows, channels), BF16),
            pltpu.VMEM((2, ctx, share, channels), BF16),
            pltpu.VMEM((ctx, 2, share, channels), BF16),
            pltpu.VMEM((ch, -(-share // TILE) * TILE, channels), BF16),
            pltpu.VMEM((slots, size, rows), BF16),
            pltpu.VMEM((rows, slots * size), BF16),
            pltpu.VMEM((2, size, rows), BF16),
            pltpu.VMEM((rows, 2 * size), BF16),
            pltpu.VMEM((2, size, rows), BF16),
            pltpu.VMEM((2 * size, channels), F32),
            pltpu.VMEM((2 * size, channels), F32),
            pltpu.VMEM((2 * size, channels), F32),
            pltpu.VMEM((slots, size, channels), F32),
            pltpu.VMEM((slots, size, channels), F32),
            pltpu.VMEM((2, size, channels), F32),
            pltpu.VMEM((2, size, channels), F32),
            pltpu.VMEM((slots * size, block), BF16),
            pltpu.VMEM((slots * size, block), BF16),
            pltpu.VMEM((rows, channels), F32),
            pltpu.VMEM((rows, channels), F32),
            pltpu.VMEM((2, taps, channels), F32),
            dma((4 * chunks,)), dma((4 * chunks,)), dma((2 * chunks,)), dma((2 * chunks,)), dma((ch - 1,)), dma((ch - 1,)),
            dma((groups - 1,)), dma((groups - 1,)),
            dma(((ctx - 1) * chunks,)), dma(((ctx - 1) * chunks,)), dma(((ch - 1) * chunks,)), dma(((ch - 1) * chunks,)), dma((5,)),
        ],
        compiler_params=pltpu.CompilerParams(
            collective_id=0, has_side_effects=True, vmem_limit_bytes=VMEM_BYTES
        ),
        name="mixer",
    )(
        doc_lengths, query_input, key_input, value_input, cotangent, filters,
        complement, *[jnp.asarray(t) for t in tables],
    )
    *mixed, grad_filter = hand_over(*mixed, grad_filter)
    return (*mixed, grad_filter.T)


def solution(mesh):
    placed = (
        P("ctx", "ch"),
        P("ctx", "ch"),
        P("ctx", "ch"),
        P("ch", None),
        P("ch"),
        P(),
        P("ctx", "ch"),
    )
    return jax.shard_map(
        functools.partial(shards, needs_relay(mesh)),
        mesh=mesh,
        in_specs=placed,
        out_specs=(P("ctx", "ch"), P("ctx", "ch"), P("ctx", "ch"), P("ctx", "ch"), P("ch", "ctx")),
        check_vma=False,
    )
```

```python
import functools

import jax
import jax.numpy as jnp
import numpy as np
from jax import lax
from jax.experimental import pallas as pl
from jax.experimental.pallas import tpu as pltpu
from jax.sharding import PartitionSpec as P

F32, BF16 = jnp.float32, jnp.bfloat16
LANES, TILE, PACK = 128, 16, 4
VMEM_BYTES = 56 * 2**20


def split_bf16(table):
    high = table.astype(BF16)
    low = (table - high.astype(np.float64)).astype(BF16)
    return high, low


def wave(places, length):
    angle = 2.0 * np.pi * (np.arange(length // 2) + 0.5) / length
    turns = angle[:, None] * np.asarray(places)[None, :]
    return np.cos(turns), np.sin(turns)


def fourier_tables(rows, taps):
    long, short = 2 * rows, 2 * rows // PACK
    cos, sin = wave(np.arange(3 * rows) - rows, long)
    analyse = np.concatenate([cos, -sin], axis=0)
    cos_s, sin_s = wave(np.arange(rows), short)
    pack = lambda table: np.tile(table, (PACK, 1))
    analyse_short = np.concatenate([pack(cos_s), pack(-sin_s)], axis=0)
    near = (np.arange(taps) < short // 2)[None, :]
    lag_cos, lag_sin = wave(np.arange(taps), long)
    near_cos, near_sin = [pack(table * near) for table in wave(np.arange(taps), short)]
    causal = np.concatenate([lag_cos, -lag_sin, near_cos, -near_sin], axis=0)
    anti = np.concatenate([lag_cos, lag_sin, near_cos, near_sin], axis=0)
    forward = causal.T.copy()
    backward = anti.T.copy()
    for table in (forward, backward):
        table[:, : 2 * rows] *= 2.0 / long
        table[:, 2 * rows :] *= 2.0 / short
    rebuild = analyse[:, rows : 2 * rows].T * (2.0 / long)
    rebuild_short = analyse_short.T * (2.0 / short)
    return (
        analyse.astype(BF16),
        analyse_short.astype(BF16),
        rebuild.astype(BF16),
        rebuild_short.astype(BF16),
        *split_bf16(causal),
        *split_bf16(anti),
        *split_bf16(forward),
        *split_bf16(backward),
    )


def mm(a, b):
    return jnp.dot(a, b, preferred_element_type=F32)


def mm_t(a, b):
    return lax.dot_general(a, b, (((1,), (1,)), ((), ())), preferred_element_type=F32)


def mm_fine(hi, lo, x):
    x_hi = x.astype(BF16)
    x_lo = (x - x_hi.astype(F32)).astype(BF16)
    return mm(hi, x_hi) + mm(hi, x_lo) + mm(lo, x_hi)


def product_of(a, b):
    return (a.astype(F32) * b.astype(F32)).astype(BF16)


def flag(mask):
    return mask.astype(F32).astype(BF16)


def times(a, x):
    half = a.shape[0] // 2
    a_re, a_im, x_re, x_im = a[:half], a[half:], x[:half], x[half:]
    return a_re * x_re - a_im * x_im, a_re * x_im + a_im * x_re


def times_conj(a, x):
    half = a.shape[0] // 2
    a_re, a_im, x_re, x_im = a[:half], a[half:], x[:half], x[half:]
    return a_re * x_re + a_im * x_im, a_re * x_im - a_im * x_re


def remote(src, dst, sems, index, device):
    return pltpu.make_async_remote_copy(
        src_ref=src, dst_ref=dst, send_sem=sems[0].at[index], recv_sem=sems[1].at[index],
        device_id=device, device_id_type=pl.DeviceIdType.MESH,
    )


def announce(devices):
    barrier = pltpu.get_barrier_semaphore()
    for device in devices:
        pl.semaphore_signal(barrier, inc=1, device_id=device, device_id_type=pl.DeviceIdType.MESH)


def gathered_in(devices):
    pl.semaphore_wait(pltpu.get_barrier_semaphore(), len(devices))


def pick_partners(complement, landed, ch, channels):
    mine = lax.axis_index("ch")
    owner = sum((complement >= k * channels).astype(jnp.int32) for k in range(1, ch)) + jnp.zeros_like(complement)
    step = mine - owner
    step = jnp.where(step < 0, step + ch, step)
    local = complement - owner * channels
    blocks = channels // LANES
    block = step * blocks + lax.shift_right_logical(local, 7)
    within = lax.bitwise_and(local, LANES - 1)
    sublane = lax.broadcasted_iota(jnp.int32, (LANES, channels), 0)
    chosen = flag(sublane == within)
    stacked = jnp.concatenate(
        [landed[s, :, b * LANES : (b + 1) * LANES] for s in range(ch) for b in range(blocks)], axis=0
    )
    spread_out = mm(stacked, chosen)
    height = landed.shape[1]
    total = jnp.zeros((height, channels), F32)
    for b in range(ch * blocks):
        total = total + jnp.where(block == b, spread_out[b * height : (b + 1) * height], 0.0)
    return total


def survey(lens, rows, first_place):
    limit = rows // PACK
    lane3 = lax.broadcasted_iota(jnp.int32, (1, 3 * rows), 1) - rows
    lane = lax.broadcasted_iota(jnp.int32, (1, rows), 1)
    column = lax.broadcasted_iota(jnp.int32, (rows, 1), 0)
    low = -first_place
    found, base, last = jnp.int32(0), jnp.int32(0), jnp.int32(0)
    seen = jnp.zeros_like(lane3)
    seen_column = jnp.zeros_like(column)
    long_lane, short_lane = jnp.zeros_like(lane), jnp.zeros_like(lane)
    long_column, short_column = jnp.zeros_like(column), jnp.zeros_like(column)
    for d in range(lens.shape[0]):
        high = low + lens[d]
        own = jnp.minimum(high, rows) - jnp.maximum(low, 0)
        is_long = jnp.where(own > limit, 1, 0)
        found = found + is_long
        long_code = is_long * found
        short_code = (1 - is_long) * (d + 1)
        inside = (lane >= low) & (lane < high)
        long_lane = jnp.where(inside, long_code, long_lane)
        short_lane = jnp.where(inside, short_code, short_lane)
        inside = (column >= low) & (column < high)
        long_column = jnp.where(inside, long_code, long_column)
        short_column = jnp.where(inside, short_code, short_column)
        seen = seen + jnp.where(lane3 >= low, 1, 0)
        seen_column = seen_column + jnp.where(column >= low, 1, 0)
        base = base + jnp.where(low <= 0, 1, 0)
        last = last + jnp.where(low <= rows - 1, 1, 0)
        low = high
    seen = seen + jnp.where(lane3 >= low, 1, 0)
    return long_lane, short_lane, long_column, short_column, seen, seen_column, base, last


def mixer_kernel(
    ctx, ch, groups, block, relay, fetches,
    lens, query, key, value, cot, filters, complement,
    analyse, analyse_short, rebuild, rebuild_short,
    causal_hi, causal_lo, anti_hi, anti_lo, fwd_hi, fwd_lo, bwd_hi, bwd_lo,
    mixer_out, grad_query, grad_key, grad_value, grad,
    u, r, halos, via, landed, picked, partner, outs, pieces, arrived, sent,
    masked, back, outer, own_ends,
    ahead, behind, both, u_hat, o_hat, far_hat, ends_hat, acc_g, z_ref, q_ref, acc_t,
    halo_send, halo_recv, via_send, via_recv, ch_send, ch_recv, mate_send, mate_recv,
    sum_send, sum_recv, back_send, back_recv, local,
):
    me, mine = lax.axis_index("ctx"), lax.axis_index("ch")
    rows, channels = query.shape
    taps = filters.shape[1]
    size = 2 * rows
    chunks = channels // block
    slots = masked.shape[0]
    longs = PACK - 1
    after, before = {"ctx": (me + 1) % ctx}, {"ctx": (me + ctx - 1) % ctx}
    group, octet = me % groups, me - me % groups
    height = taps // groups
    share = grad.shape[0]
    others = [{"ctx": (me + step) % ctx} for step in range(1, ctx)]
    peers = [{"ch": (mine + step) % ch} for step in range(1, ch)]
    mates = [{"ctx": octet + (group + step) % groups} for step in range(1, groups)]
    announce(others + peers)
    for copy in fetches:
        copy.start()
    for copy in fetches[:5]:
        copy.wait()

    row = lax.broadcasted_iota(jnp.int32, (height, taps), 0)
    tap = lax.broadcasted_iota(jnp.int32, (height, taps), 1)
    landed[0] = mm_t(flag(tap == row + group * height), filters[...]).astype(BF16)
    u[...] = product_of(key[...], value[...])
    r[...] = product_of(cot[...], query[...])

    gathered_in(others + peers)
    along = [
        remote(landed.at[0], landed.at[step], (ch_send, ch_recv), step - 1, peers[step - 1])
        for step in range(1, ch)
    ]
    for copy in along[::-1]:
        copy.start()
    has_next, has_prev = me < ctx - 1, me > 0
    middle = ctx // 2 - 1
    at_middle = (me == middle) | (me == middle + 1)
    end = jnp.where(me == middle, ctx - 1, 0)
    starts, send_waits, recv_waits, forwards = [], [], [], []
    for c in range(chunks):
        lanes = pl.ds(c * block, block)
        for kind, field in enumerate((u, r)):
            index = c * 2 + kind
            detour = relay and index >= chunks
            to_next = remote(field.at[:, lanes], halos.at[kind, :, lanes],
                             (halo_send, halo_recv), c * 4 + kind, after)
            to_prev = remote(field.at[:, lanes], halos.at[2 + kind, :, lanes],
                             (halo_send, halo_recv), c * 4 + 2 + kind, before)
            starts.append([(has_next & (me != middle) if detour else has_next, to_next),
                           (has_prev & (me != middle + 1) if detour else has_prev, to_prev)])
            send_waits += starts[-1]
            recv_waits.append([(has_prev, to_next), (has_next, to_prev)])
            if detour:
                away = remote(field.at[:, lanes], via.at[kind, :, lanes], (via_send, via_recv), index, {"ctx": end})
                starts[-1].append((at_middle, away))
                send_waits.append((at_middle, away))
                from_last = remote(via.at[kind, :, lanes], halos.at[kind, :, lanes],
                                   (halo_send, halo_recv), c * 4 + kind, {"ctx": middle + 1})
                from_first = remote(via.at[kind, :, lanes], halos.at[2 + kind, :, lanes],
                                    (halo_send, halo_recv), c * 4 + 2 + kind, {"ctx": middle})
                forwards.append((away, from_last, from_first))

    def start_halos(chunk):
        for condition, copy in starts[2 * chunk] + starts[2 * chunk + 1]:
            pl.when(condition)(copy.start)

    for chunk in range(chunks - 1):
        start_halos(chunk)

    @pl.when(jnp.logical_not(has_prev))
    def _():
        halos[0:2] = jnp.zeros((2, rows, channels), BF16)

    @pl.when(jnp.logical_not(has_next))
    def _():
        halos[2:4] = jnp.zeros((2, rows, channels), BF16)

    long_lane, short_lane, long_column, short_column, seen, seen_column, base, last = survey(
        lens, rows, me * rows
    )
    for copy in fetches[5:]:
        copy.wait()
    quarter = rows // PACK
    packed_row = (lax.broadcasted_iota(jnp.int32, (size, 1), 0) % rows) // quarter
    packed_lane = (lax.broadcasted_iota(jnp.int32, (1, size), 1) % rows) // quarter
    for s in range(slots):
        cols = pl.ds(s * size, size)
        if s < longs:
            masked[s] = analyse[:, rows : 2 * rows] * flag(long_lane == s + 1)
            back[:, cols] = rebuild[...] * flag(long_column == s + 1)
        else:
            first = (s - longs) * PACK + 1
            masked[s] = analyse_short[...] * flag(short_lane == first + packed_row)
            back[:, cols] = rebuild_short[...] * flag(short_column == first + packed_lane)
    for e, code in enumerate((base, last)):
        section = slice(2 * e * rows, (2 * e + 1) * rows)
        outer[e] = analyse[:, section] * flag(seen[:, section] == code)
        own_ends[e] = analyse[:, rows : 2 * rows] * flag(seen[:, rows : 2 * rows] == code)
        back[:, pl.ds((slots + e) * size, size)] = rebuild[...] * flag(seen_column == code)

    ahead[...] = mm_t(causal_hi[...], filters[...]) + mm_t(causal_lo[...], filters[...])

    def analysis(c, carry):
        lanes = pl.ds(pl.multiple_of(c * block, LANES), block)
        u_own, r_own = u[:, lanes], r[:, lanes]
        for s in range(slots):
            u_now, o_now = mm(masked[s], u_own), mm(masked[s], r_own)
            u_hat[s, :, lanes] = u_now
            o_hat[s, :, lanes] = o_now
            g_re, g_im = times_conj(u_now, o_now)
            kind = 0 if s < longs else 1
            if s == 0 or s == longs:
                acc_g[kind, :rows, lanes] = g_re
                acc_g[kind, rows:, lanes] = g_im
            else:
                acc_g[kind, :rows, lanes] += g_re
                acc_g[kind, rows:, lanes] += g_im
        for e in range(2):
            ends_hat[e, :, lanes] = mm(own_ends[e], r_own)
        own = jnp.concatenate([acc_g[0, :, lanes], acc_g[1, :, lanes]], axis=0)
        acc_t[0, :, lanes] = mm_fine(fwd_hi[...], fwd_lo[...], own)
        acc_t[1, :, lanes] = mm_fine(bwd_hi[...], bwd_lo[...], own)
        return carry

    lax.fori_loop(0, chunks, analysis, 0)

    for copy in along:
        copy.wait()
    picked[...] = pick_partners(complement[...].reshape(1, channels), landed, ch, channels).astype(BF16)
    shared = [
        remote(picked, partner.at[group], (mate_send, mate_recv), step - 1, mates[step - 1])
        for step in range(1, groups)
    ]
    for copy in shared:
        copy.start()
    keep = pltpu.make_async_copy(picked, partner.at[group], local.at[0])
    keep.start()
    start_halos(chunks - 1)
    for arriving, from_last, from_first in forwards:
        @pl.when(me == ctx - 1)
        def _():
            arriving.wait_recv()
            from_last.start()

        @pl.when(me == 0)
        def _():
            arriving.wait_recv()
            from_first.start()

    sums = []

    def send_taps(c):
        lanes = pl.ds(c * block, block)
        for condition, copy in recv_waits[2 * c] + recv_waits[2 * c + 1]:
            pl.when(condition)(copy.wait_recv)
        for e in range(2):
            u_far = mm(outer[e], halos[2 * e, :, lanes])
            far_hat[e, 0, :, lanes] = u_far
            far_hat[e, 1, :, lanes] = mm(outer[e], halos[2 * e + 1, :, lanes])
            g_re, g_im = times_conj(u_far, ends_hat[e, :, lanes])
            hi, lo = (fwd_hi, fwd_lo) if e == 0 else (bwd_hi, bwd_lo)
            far = jnp.concatenate([g_re, g_im], axis=0)
            tap_sums = acc_t[e, :, lanes] + mm_fine(hi[:, :size], lo[:, :size], far)
            for i in range(ctx):
                pieces[e, i, :, lanes] = tap_sums[i * share : (i + 1) * share].astype(BF16)
        for step in range(1, ctx):
            copy = remote(pieces.at[:, (me + step) % ctx, :, lanes], arrived.at[step, :, :, lanes],
                          (sum_send, sum_recv), c * (ctx - 1) + step - 1, others[step - 1])
            copy.start()
            sums.append(copy)

    def filtering(c):
        lanes = pl.ds(c * block, block)

        def keep_products(s, z, q):
            z_ref[s * size : s * size + rows] = z[0].astype(BF16)
            z_ref[s * size + rows : (s + 1) * size] = z[1].astype(BF16)
            q_ref[s * size : s * size + rows] = q[0].astype(BF16)
            q_ref[s * size + rows : (s + 1) * size] = q[1].astype(BF16)

        for s in range(slots):
            kind = 0 if s < longs else 1
            h = both[kind * size : (kind + 1) * size, lanes]
            keep_products(s, times(h, u_hat[s, :, lanes]), times_conj(h, o_hat[s, :, lanes]))
        for e in range(2):
            for_u, for_r = (ahead, behind) if e == 0 else (behind, ahead)
            keep_products(
                slots + e,
                times(for_u[:size, lanes], far_hat[e, 0, :, lanes]),
                times_conj(for_r[:size, lanes], far_hat[e, 1, :, lanes]),
            )
        combined = mm(back[...], z_ref[...])
        grad_product = mm(back[...], q_ref[...])
        outs[0, :, lanes] = (query[:, lanes].astype(F32) * combined).astype(BF16)
        outs[1, :, lanes] = (cot[:, lanes].astype(F32) * combined).astype(BF16)
        outs[2, :, lanes] = (grad_product * value[:, lanes].astype(F32)).astype(BF16)
        outs[3, :, lanes] = (grad_product * key[:, lanes].astype(F32)).astype(BF16)

    across = []

    def send_mirrored(c):
        lanes = pl.ds(c * block, block)
        for copy in sums[c * (ctx - 1) : (c + 1) * (ctx - 1)]:
            copy.wait()
        total = sum(arrived[step, 1, :, lanes].astype(F32) for step in range(1, ctx))
        sent[0, :share, lanes] = (total + pieces[1, me, :, lanes].astype(F32)).astype(BF16)
        for step in range(1, ch):
            copy = remote(sent.at[0, :, lanes], sent.at[step, :, lanes],
                          (back_send, back_recv), c * (ch - 1) + step - 1, peers[step - 1])
            copy.start()
            across.append(copy)

    if share < sent.shape[1]:
        sent[...] = jnp.zeros_like(sent)
    for c in range(chunks - 1):
        send_taps(c)
    for copy in shared:
        copy.wait()
    keep.wait()
    g = partner[...].reshape(taps, channels)
    behind[...] = mm(anti_hi[...], g) + mm(anti_lo[...], g)
    both[...] = ahead[...] + behind[...]
    if chunks > 1:
        filtering(0)
    send_taps(chunks - 1)
    for c in range(chunks):
        if c > 0 or chunks == 1:
            filtering(c)
        if c < chunks - 1:
            send_mirrored(c)
    stores = []
    for index, place in enumerate((mixer_out, grad_query, grad_key, grad_value)):
        copy = pltpu.make_async_copy(outs.at[index], place, local.at[1 + index])
        copy.start()
        stores.append(copy)

    send_mirrored(chunks - 1)
    own = pieces[0, me].astype(F32) + sum(arrived[step, 0].astype(F32) for step in range(1, ctx))
    for condition, copy in send_waits:
        pl.when(condition)(copy.wait_send)
    for _, from_last, from_first in forwards:
        pl.when(me == ctx - 1)(from_last.wait_send)
        pl.when(me == 0)(from_first.wait_send)
    for copy in across:
        copy.wait()
    grad[...] = own + pick_partners(complement[...].reshape(1, channels), sent, ch, channels)[:share]
    for copy in stores:
        copy.wait()


def entry_kernel(ctx, ch, groups, block, relay, count, lens, complement, *refs):
    given, results, held, fetch = refs[:count], refs[count : count + 5], refs[count + 5 : 2 * count + 5], refs[2 * count + 5]
    fetches = [pltpu.make_async_copy(given[i], held[i], fetch.at[i]) for i in range(count)]
    mixer_kernel(
        ctx, ch, groups, block, relay, fetches,
        lens, *held[:5], complement, *held[5:], *results, *refs[2 * count + 6 :],
    )


def channel_block(channels):
    for block in (384, 256, 128):
        if channels % block == 0:
            return block
    return channels


def hand_over_kernel(*refs):
    count = (len(refs) - 2) // 3
    given, taken, held, (read, written) = refs[:count], refs[count : 2 * count], refs[2 * count : -2], refs[-2:]
    loads = [pltpu.make_async_copy(given[i], held[i], read.at[i]) for i in range(count)]
    stores = [pltpu.make_async_copy(held[i], taken[i], written.at[i]) for i in range(count)]
    for copy in loads:
        copy.start()
    for load, store in zip(loads, stores):
        load.wait()
        store.start()
    for copy in stores:
        copy.wait()


def hand_over(*arrays):
    hbm = pl.BlockSpec(memory_space=pl.ANY)
    return pl.pallas_call(
        hand_over_kernel,
        in_specs=[hbm] * len(arrays),
        out_specs=[hbm] * len(arrays),
        out_shape=[jax.ShapeDtypeStruct(a.shape, a.dtype) for a in arrays],
        scratch_shapes=[pltpu.VMEM(a.shape, a.dtype) for a in arrays]
        + [pltpu.SemaphoreType.DMA((len(arrays),))] * 2,
        name="hand_over",
    )(*arrays)


def needs_relay(mesh):
    axis = mesh.axis_names.index("ctx")
    line = np.moveaxis(mesh.devices, axis, 0).reshape(mesh.shape["ctx"], -1)[:, 0]
    places = [getattr(device, "coords", None) for device in line]
    if any(place is None for place in places) or len(places) < 4:
        return False
    hops = lambda a, b: sum(abs(x - y) for x, y in zip(places[a], places[b]))
    middle, end = len(places) // 2 - 1, len(places) - 1
    return (
        hops(middle, middle + 1) == 2
        and hops(middle, end) == hops(end, middle + 1) == 1
        and hops(middle + 1, 0) == hops(0, middle) == 1
    )


def shards(relay, query_input, key_input, value_input, filters, complement, doc_lengths, cotangent):
    rows, channels = query_input.shape
    taps = filters.shape[1]
    ctx, ch = lax.axis_size("ctx"), lax.axis_size("ch")
    groups = min(ctx, taps // TILE)
    height, share, size = taps // groups, taps // ctx, 2 * rows
    block = channel_block(channels)
    chunks = channels // block
    slots = PACK - 1 + -(-doc_lengths.shape[0] // PACK)
    tables = [jnp.asarray(table) for table in fourier_tables(rows, taps)]
    fetched = [query_input, key_input, value_input, cotangent, filters, *tables]
    hbm = pl.BlockSpec(memory_space=pl.ANY)
    vmem = pl.BlockSpec(memory_space=pltpu.VMEM)
    dma = pltpu.SemaphoreType.DMA
    field = jax.ShapeDtypeStruct((rows, channels), BF16)
    *mixed, grad_filter = pl.pallas_call(
        functools.partial(entry_kernel, ctx, ch, groups, block, relay, len(fetched)),
        in_specs=[pl.BlockSpec(memory_space=pltpu.SMEM), vmem] + [hbm] * len(fetched),
        out_specs=[hbm] * 4 + [vmem],
        out_shape=[field] * 4 + [jax.ShapeDtypeStruct((share, channels), F32)],
        scratch_shapes=[pltpu.VMEM(a.shape, a.dtype) for a in fetched]
        + [
            dma((len(fetched),)),
            pltpu.VMEM((rows, channels), BF16),
            pltpu.VMEM((rows, channels), BF16),
            pltpu.VMEM((4, rows, channels), BF16),
            pltpu.VMEM((2, rows, channels), BF16),
            pltpu.VMEM((ch, height, channels), BF16),
            pltpu.VMEM((height, channels), BF16),
            pltpu.VMEM((groups, height, channels), BF16),
            pltpu.VMEM((4, rows, channels), BF16),
            pltpu.VMEM((2, ctx, share, channels), BF16),
            pltpu.VMEM((ctx, 2, share, channels), BF16),
            pltpu.VMEM((ch, -(-share // TILE) * TILE, channels), BF16),
            pltpu.VMEM((slots, size, rows), BF16),
            pltpu.VMEM((rows, (slots + 2) * size), BF16),
            pltpu.VMEM((2, size, rows), BF16),
            pltpu.VMEM((2, size, rows), BF16),
            pltpu.VMEM((2 * size, channels), F32),
            pltpu.VMEM((2 * size, channels), F32),
            pltpu.VMEM((2 * size, channels), F32),
            pltpu.VMEM((slots, size, channels), F32),
            pltpu.VMEM((slots, size, channels), F32),
            pltpu.VMEM((2, 2, size, channels), F32),
            pltpu.VMEM((2, size, channels), F32),
            pltpu.VMEM((2, size, channels), F32),
            pltpu.VMEM(((slots + 2) * size, block), BF16),
            pltpu.VMEM(((slots + 2) * size, block), BF16),
            pltpu.VMEM((2, taps, channels), F32),
            dma((4 * chunks,)), dma((4 * chunks,)), dma((2 * chunks,)), dma((2 * chunks,)), dma((ch - 1,)), dma((ch - 1,)),
            dma((groups - 1,)), dma((groups - 1,)),
            dma(((ctx - 1) * chunks,)), dma(((ctx - 1) * chunks,)), dma(((ch - 1) * chunks,)), dma(((ch - 1) * chunks,)), dma((5,)),
        ],
        compiler_params=pltpu.CompilerParams(
            collective_id=0, has_side_effects=True, vmem_limit_bytes=VMEM_BYTES
        ),
        name="mixer",
    )(doc_lengths, complement, *fetched)
    *mixed, grad_filter = hand_over(*mixed, grad_filter)
    return (*mixed, grad_filter.T)


def solution(mesh):
    placed = (
        P("ctx", "ch"),
        P("ctx", "ch"),
        P("ctx", "ch"),
        P("ch", None),
        P("ch"),
        P(),
        P("ctx", "ch"),
    )
    return jax.shard_map(
        functools.partial(shards, needs_relay(mesh)),
        mesh=mesh,
        in_specs=placed,
        out_specs=(P("ctx", "ch"), P("ctx", "ch"), P("ctx", "ch"), P("ctx", "ch"), P("ch", "ctx")),
        check_vma=False,
    )
```

```python
import functools

import jax
import jax.numpy as jnp
import numpy as np
from jax import lax
from jax.experimental import pallas as pl
from jax.experimental.pallas import tpu as pltpu
from jax.sharding import PartitionSpec as P

F32, BF16 = jnp.float32, jnp.bfloat16
LANES, TILE, PACK = 128, 16, 4
VMEM_BYTES = 56 * 2**20


def split_bf16(table):
    high = table.astype(BF16)
    low = (table - high.astype(np.float64)).astype(BF16)
    return high, low


def wave(places, length):
    angle = 2.0 * np.pi * (np.arange(length // 2) + 0.5) / length
    turns = angle[:, None] * np.asarray(places)[None, :]
    return np.cos(turns), np.sin(turns)


def fourier_tables(rows, taps):
    long, short = 2 * rows, 2 * rows // PACK
    cos, sin = wave(np.arange(3 * rows) - rows, long)
    analyse = np.concatenate([cos, -sin], axis=0)
    cos_s, sin_s = wave(np.arange(rows), short)
    pack = lambda table: np.tile(table, (PACK, 1))
    analyse_short = np.concatenate([pack(cos_s), pack(-sin_s)], axis=0)
    near = (np.arange(taps) < short // 2)[None, :]
    lag_cos, lag_sin = wave(np.arange(taps), long)
    near_cos, near_sin = [pack(table * near) for table in wave(np.arange(taps), short)]
    causal = np.concatenate([lag_cos, -lag_sin, near_cos, -near_sin], axis=0)
    anti = np.concatenate([lag_cos, lag_sin, near_cos, near_sin], axis=0)
    forward = causal.T.copy()
    backward = anti.T.copy()
    for table in (forward, backward):
        table[:, : 2 * rows] *= 2.0 / long
        table[:, 2 * rows :] *= 2.0 / short
    rebuild = analyse[:, rows : 2 * rows].T * (2.0 / long)
    rebuild_short = analyse_short.T * (2.0 / short)
    return (
        analyse.astype(BF16),
        analyse_short.astype(BF16),
        rebuild.astype(BF16),
        rebuild_short.astype(BF16),
        *split_bf16(causal),
        *split_bf16(anti),
        *split_bf16(forward),
        *split_bf16(backward),
    )


def mm(a, b):
    return jnp.dot(a, b, preferred_element_type=F32)


def mm_t(a, b):
    return lax.dot_general(a, b, (((1,), (1,)), ((), ())), preferred_element_type=F32)


def mm_fine(hi, lo, x):
    x_hi = x.astype(BF16)
    x_lo = (x - x_hi.astype(F32)).astype(BF16)
    return mm(hi, x_hi) + mm(hi, x_lo) + mm(lo, x_hi)


def product_of(a, b):
    return (a.astype(F32) * b.astype(F32)).astype(BF16)


def flag(mask):
    return mask.astype(F32).astype(BF16)


def times(a, x):
    half = a.shape[0] // 2
    a_re, a_im, x_re, x_im = a[:half], a[half:], x[:half], x[half:]
    return a_re * x_re - a_im * x_im, a_re * x_im + a_im * x_re


def times_conj(a, x):
    half = a.shape[0] // 2
    a_re, a_im, x_re, x_im = a[:half], a[half:], x[:half], x[half:]
    return a_re * x_re + a_im * x_im, a_re * x_im - a_im * x_re


def remote(src, dst, sems, index, device):
    return pltpu.make_async_remote_copy(
        src_ref=src, dst_ref=dst, send_sem=sems[0].at[index], recv_sem=sems[1].at[index],
        device_id=device, device_id_type=pl.DeviceIdType.MESH,
    )


def announce(devices):
    barrier = pltpu.get_barrier_semaphore()
    for device in devices:
        pl.semaphore_signal(barrier, inc=1, device_id=device, device_id_type=pl.DeviceIdType.MESH)


def gathered_in(devices):
    pl.semaphore_wait(pltpu.get_barrier_semaphore(), len(devices))


def pick_partners(complement, landed, ch, channels):
    mine = lax.axis_index("ch")
    owner = sum((complement >= k * channels).astype(jnp.int32) for k in range(1, ch)) + jnp.zeros_like(complement)
    step = mine - owner
    step = jnp.where(step < 0, step + ch, step)
    local = complement - owner * channels
    blocks = channels // LANES
    block = step * blocks + lax.shift_right_logical(local, 7)
    within = lax.bitwise_and(local, LANES - 1)
    sublane = lax.broadcasted_iota(jnp.int32, (LANES, channels), 0)
    chosen = flag(sublane == within)
    stacked = jnp.concatenate(
        [landed[s, :, b * LANES : (b + 1) * LANES] for s in range(ch) for b in range(blocks)], axis=0
    )
    spread_out = mm(stacked, chosen)
    height = landed.shape[1]
    total = jnp.zeros((height, channels), F32)
    for b in range(ch * blocks):
        total = total + jnp.where(block == b, spread_out[b * height : (b + 1) * height], 0.0)
    return total


def survey(lens, rows, first_place):
    limit = rows // PACK
    lane3 = lax.broadcasted_iota(jnp.int32, (1, 3 * rows), 1) - rows
    lane = lax.broadcasted_iota(jnp.int32, (1, rows), 1)
    column = lax.broadcasted_iota(jnp.int32, (rows, 1), 0)
    low = -first_place
    found, base, last = jnp.int32(0), jnp.int32(0), jnp.int32(0)
    seen = jnp.zeros_like(lane3)
    seen_column = jnp.zeros_like(column)
    long_lane, short_lane = jnp.zeros_like(lane), jnp.zeros_like(lane)
    long_column, short_column = jnp.zeros_like(column), jnp.zeros_like(column)
    for d in range(lens.shape[0]):
        high = low + lens[d]
        own = jnp.minimum(high, rows) - jnp.maximum(low, 0)
        is_long = jnp.where(own > limit, 1, 0)
        found = found + is_long
        long_code = is_long * found
        short_code = (1 - is_long) * (d + 1)
        inside = (lane >= low) & (lane < high)
        long_lane = jnp.where(inside, long_code, long_lane)
        short_lane = jnp.where(inside, short_code, short_lane)
        inside = (column >= low) & (column < high)
        long_column = jnp.where(inside, long_code, long_column)
        short_column = jnp.where(inside, short_code, short_column)
        seen = seen + jnp.where(lane3 >= low, 1, 0)
        seen_column = seen_column + jnp.where(column >= low, 1, 0)
        base = base + jnp.where(low <= 0, 1, 0)
        last = last + jnp.where(low <= rows - 1, 1, 0)
        low = high
    seen = seen + jnp.where(lane3 >= low, 1, 0)
    return long_lane, short_lane, long_column, short_column, seen, seen_column, base, last


def mixer_kernel(
    ctx, ch, groups, block, relay, fetches,
    lens, query, key, value, cot, filters, complement,
    analyse, analyse_short, rebuild, rebuild_short,
    causal_hi, causal_lo, anti_hi, anti_lo, fwd_hi, fwd_lo, bwd_hi, bwd_lo,
    mixer_out, grad_query, grad_key, grad_value, grad,
    u, r, halos, via, landed, picked, partner, outs, pieces, twins, joined, arrived, sent,
    masked, back, outer, own_ends,
    ahead, behind, both, u_hat, o_hat, far_hat, ends_hat, acc_g, z_ref, q_ref, acc_t,
    halo_send, halo_recv, via_send, via_recv, ch_send, ch_recv, mate_send, mate_recv,
    twin_send, twin_recv, sum_send, sum_recv, back_send, back_recv, local,
):
    me, mine = lax.axis_index("ctx"), lax.axis_index("ch")
    rows, channels = query.shape
    taps = filters.shape[1]
    size = 2 * rows
    chunks = channels // block
    slots = masked.shape[0]
    longs = PACK - 1
    after, before = {"ctx": (me + 1) % ctx}, {"ctx": (me + ctx - 1) % ctx}
    group, octet = me % groups, me - me % groups
    height = taps // groups
    share = grad.shape[0]
    others = [{"ctx": (me + step) % ctx} for step in range(1, ctx)]
    peers = [{"ch": (mine + step) % ch} for step in range(1, ch)]
    mates = [{"ctx": octet + (group + step) % groups} for step in range(1, groups)]
    announce(others + peers)
    for copy in fetches:
        copy.start()
    for copy in fetches[:5]:
        copy.wait()

    row = lax.broadcasted_iota(jnp.int32, (height, taps), 0)
    tap = lax.broadcasted_iota(jnp.int32, (height, taps), 1)
    landed[0] = mm_t(flag(tap == row + group * height), filters[...]).astype(BF16)
    u[...] = product_of(key[...], value[...])
    r[...] = product_of(cot[...], query[...])

    gathered_in(others + peers)
    along = [
        remote(landed.at[0], landed.at[step], (ch_send, ch_recv), step - 1, peers[step - 1])
        for step in range(1, ch)
    ]
    for copy in along[::-1]:
        copy.start()
    has_next, has_prev = me < ctx - 1, me > 0
    middle = ctx // 2 - 1
    at_middle = (me == middle) | (me == middle + 1)
    end = jnp.where(me == middle, ctx - 1, 0)
    starts, send_waits, recv_waits, forwards = [], [], [], []
    for c in range(chunks):
        lanes = pl.ds(c * block, block)
        for kind, field in enumerate((u, r)):
            index = c * 2 + kind
            detour = relay and index >= chunks
            to_next = remote(field.at[:, lanes], halos.at[kind, :, lanes],
                             (halo_send, halo_recv), c * 4 + kind, after)
            to_prev = remote(field.at[:, lanes], halos.at[2 + kind, :, lanes],
                             (halo_send, halo_recv), c * 4 + 2 + kind, before)
            starts.append([(has_next & (me != middle) if detour else has_next, to_next),
                           (has_prev & (me != middle + 1) if detour else has_prev, to_prev)])
            send_waits += starts[-1]
            recv_waits.append([(has_prev, to_next), (has_next, to_prev)])
            if detour:
                away = remote(field.at[:, lanes], via.at[kind, :, lanes], (via_send, via_recv), index, {"ctx": end})
                starts[-1].append((at_middle, away))
                send_waits.append((at_middle, away))
                from_last = remote(via.at[kind, :, lanes], halos.at[kind, :, lanes],
                                   (halo_send, halo_recv), c * 4 + kind, {"ctx": middle + 1})
                from_first = remote(via.at[kind, :, lanes], halos.at[2 + kind, :, lanes],
                                    (halo_send, halo_recv), c * 4 + 2 + kind, {"ctx": middle})
                forwards.append((away, from_last, from_first))

    def start_halos(chunk):
        for condition, copy in starts[2 * chunk] + starts[2 * chunk + 1]:
            pl.when(condition)(copy.start)

    for chunk in range(chunks - 1):
        start_halos(chunk)

    @pl.when(jnp.logical_not(has_prev))
    def _():
        halos[0:2] = jnp.zeros((2, rows, channels), BF16)

    @pl.when(jnp.logical_not(has_next))
    def _():
        halos[2:4] = jnp.zeros((2, rows, channels), BF16)

    long_lane, short_lane, long_column, short_column, seen, seen_column, base, last = survey(
        lens, rows, me * rows
    )
    for copy in fetches[5:]:
        copy.wait()
    quarter = rows // PACK
    packed_row = (lax.broadcasted_iota(jnp.int32, (size, 1), 0) % rows) // quarter
    packed_lane = (lax.broadcasted_iota(jnp.int32, (1, size), 1) % rows) // quarter
    for s in range(slots):
        cols = pl.ds(s * size, size)
        if s < longs:
            masked[s] = analyse[:, rows : 2 * rows] * flag(long_lane == s + 1)
            back[:, cols] = rebuild[...] * flag(long_column == s + 1)
        else:
            first = (s - longs) * PACK + 1
            masked[s] = analyse_short[...] * flag(short_lane == first + packed_row)
            back[:, cols] = rebuild_short[...] * flag(short_column == first + packed_lane)
    for e, code in enumerate((base, last)):
        section = slice(2 * e * rows, (2 * e + 1) * rows)
        outer[e] = analyse[:, section] * flag(seen[:, section] == code)
        own_ends[e] = analyse[:, rows : 2 * rows] * flag(seen[:, rows : 2 * rows] == code)
        back[:, pl.ds((slots + e) * size, size)] = rebuild[...] * flag(seen_column == code)

    ahead[...] = mm_t(causal_hi[...], filters[...]) + mm_t(causal_lo[...], filters[...])

    def analysis(c, carry):
        lanes = pl.ds(pl.multiple_of(c * block, LANES), block)
        u_own, r_own = u[:, lanes], r[:, lanes]
        for s in range(slots):
            u_now, o_now = mm(masked[s], u_own), mm(masked[s], r_own)
            u_hat[s, :, lanes] = u_now
            o_hat[s, :, lanes] = o_now
            g_re, g_im = times_conj(u_now, o_now)
            kind = 0 if s < longs else 1
            if s == 0 or s == longs:
                acc_g[kind, :rows, lanes] = g_re
                acc_g[kind, rows:, lanes] = g_im
            else:
                acc_g[kind, :rows, lanes] += g_re
                acc_g[kind, rows:, lanes] += g_im
        for e in range(2):
            ends_hat[e, :, lanes] = mm(own_ends[e], r_own)
        own = jnp.concatenate([acc_g[0, :, lanes], acc_g[1, :, lanes]], axis=0)
        acc_t[0, :, lanes] = mm_fine(fwd_hi[...], fwd_lo[...], own)
        acc_t[1, :, lanes] = mm_fine(bwd_hi[...], bwd_lo[...], own)
        return carry

    lax.fori_loop(0, chunks, analysis, 0)

    for copy in along:
        copy.wait()
    picked[...] = pick_partners(complement[...].reshape(1, channels), landed, ch, channels).astype(BF16)
    shared = [
        remote(picked, partner.at[group], (mate_send, mate_recv), step - 1, mates[step - 1])
        for step in range(1, groups)
    ]
    for copy in shared:
        copy.start()
    keep = pltpu.make_async_copy(picked, partner.at[group], local.at[0])
    keep.start()
    start_halos(chunks - 1)
    for arriving, from_last, from_first in forwards:
        @pl.when(me == ctx - 1)
        def _():
            arriving.wait_recv()
            from_last.start()

        @pl.when(me == 0)
        def _():
            arriving.wait_recv()
            from_first.start()

    core, chip, chips = me % 2, me // 2, ctx // 2
    swaps, sums = [], []

    def send_taps(c):
        lanes = pl.ds(c * block, block)
        for condition, copy in recv_waits[2 * c] + recv_waits[2 * c + 1]:
            pl.when(condition)(copy.wait_recv)
        for e in range(2):
            u_far = mm(outer[e], halos[2 * e, :, lanes])
            far_hat[e, 0, :, lanes] = u_far
            far_hat[e, 1, :, lanes] = mm(outer[e], halos[2 * e + 1, :, lanes])
            g_re, g_im = times_conj(u_far, ends_hat[e, :, lanes])
            hi, lo = (fwd_hi, fwd_lo) if e == 0 else (bwd_hi, bwd_lo)
            far = jnp.concatenate([g_re, g_im], axis=0)
            tap_sums = acc_t[e, :, lanes] + mm_fine(hi[:, :size], lo[:, :size], far)
            for i in range(ctx):
                pieces[i % 2, e, i // 2, :, lanes] = tap_sums[i * share : (i + 1) * share].astype(BF16)
        copy = remote(pieces.at[1 - core, :, :, :, lanes], twins.at[:, :, :, lanes],
                      (twin_send, twin_recv), c, {"ctx": me + 1 - 2 * core})
        copy.start()
        swaps.append(copy)

    def join_taps(c):
        lanes = pl.ds(c * block, block)
        swaps[c].wait()
        joined[:, :, :, lanes] = (
            pieces[core, :, :, :, lanes].astype(F32) + twins[:, :, :, lanes].astype(F32)
        ).astype(BF16)
        for step in range(1, chips):
            copy = remote(joined.at[:, (chip + step) % chips, :, lanes], arrived.at[step - 1, :, :, lanes],
                          (sum_send, sum_recv), c * (chips - 1) + step - 1, {"ctx": (me + 2 * step) % ctx})
            copy.start()
            sums.append(copy)

    def filtering(c):
        lanes = pl.ds(c * block, block)

        def keep_products(s, z, q):
            z_ref[s * size : s * size + rows] = z[0].astype(BF16)
            z_ref[s * size + rows : (s + 1) * size] = z[1].astype(BF16)
            q_ref[s * size : s * size + rows] = q[0].astype(BF16)
            q_ref[s * size + rows : (s + 1) * size] = q[1].astype(BF16)

        for s in range(slots):
            kind = 0 if s < longs else 1
            h = both[kind * size : (kind + 1) * size, lanes]
            keep_products(s, times(h, u_hat[s, :, lanes]), times_conj(h, o_hat[s, :, lanes]))
        for e in range(2):
            for_u, for_r = (ahead, behind) if e == 0 else (behind, ahead)
            keep_products(
                slots + e,
                times(for_u[:size, lanes], far_hat[e, 0, :, lanes]),
                times_conj(for_r[:size, lanes], far_hat[e, 1, :, lanes]),
            )
        combined = mm(back[...], z_ref[...])
        grad_product = mm(back[...], q_ref[...])
        outs[0, :, lanes] = (query[:, lanes].astype(F32) * combined).astype(BF16)
        outs[1, :, lanes] = (cot[:, lanes].astype(F32) * combined).astype(BF16)
        outs[2, :, lanes] = (grad_product * value[:, lanes].astype(F32)).astype(BF16)
        outs[3, :, lanes] = (grad_product * key[:, lanes].astype(F32)).astype(BF16)

    across = []

    def send_mirrored(c):
        lanes = pl.ds(c * block, block)
        for copy in sums[c * (chips - 1) : (c + 1) * (chips - 1)]:
            copy.wait()
        total = sum(arrived[step, 1, :, lanes].astype(F32) for step in range(chips - 1))
        sent[0, :share, lanes] = (total + joined[1, chip, :, lanes].astype(F32)).astype(BF16)
        for step in range(1, ch):
            copy = remote(sent.at[0, :, lanes], sent.at[step, :, lanes],
                          (back_send, back_recv), c * (ch - 1) + step - 1, peers[step - 1])
            copy.start()
            across.append(copy)

    if share < sent.shape[1]:
        sent[...] = jnp.zeros_like(sent)
    for c in range(chunks - 1):
        send_taps(c)
    for c in range(chunks - 1):
        join_taps(c)
    for copy in shared:
        copy.wait()
    keep.wait()
    g = partner[...].reshape(taps, channels)
    behind[...] = mm(anti_hi[...], g) + mm(anti_lo[...], g)
    both[...] = ahead[...] + behind[...]
    early = max(chunks - 2, 0)
    for c in range(early):
        filtering(c)
    send_taps(chunks - 1)
    for c in range(early, chunks - 1):
        filtering(c)
    join_taps(chunks - 1)
    for c in range(chunks - 1):
        send_mirrored(c)
    filtering(chunks - 1)
    stores = []
    for index, place in enumerate((mixer_out, grad_query, grad_key, grad_value)):
        copy = pltpu.make_async_copy(outs.at[index], place, local.at[1 + index])
        copy.start()
        stores.append(copy)

    send_mirrored(chunks - 1)
    own = joined[0, chip].astype(F32) + sum(arrived[step, 0].astype(F32) for step in range(chips - 1))
    for condition, copy in send_waits:
        pl.when(condition)(copy.wait_send)
    for _, from_last, from_first in forwards:
        pl.when(me == ctx - 1)(from_last.wait_send)
        pl.when(me == 0)(from_first.wait_send)
    for copy in across:
        copy.wait()
    grad[...] = own + pick_partners(complement[...].reshape(1, channels), sent, ch, channels)[:share]
    for copy in stores:
        copy.wait()


def entry_kernel(ctx, ch, groups, block, relay, count, lens, complement, *refs):
    given, results, held, fetch = refs[:count], refs[count : count + 5], refs[count + 5 : 2 * count + 5], refs[2 * count + 5]
    fetches = [pltpu.make_async_copy(given[i], held[i], fetch.at[i]) for i in range(count)]
    mixer_kernel(
        ctx, ch, groups, block, relay, fetches,
        lens, *held[:5], complement, *held[5:], *results, *refs[2 * count + 6 :],
    )


def channel_block(channels):
    for block in (384, 256, 128):
        if channels % block == 0:
            return block
    return channels


def hand_over_kernel(*refs):
    count = (len(refs) - 2) // 3
    given, taken, held, (read, written) = refs[:count], refs[count : 2 * count], refs[2 * count : -2], refs[-2:]
    loads = [pltpu.make_async_copy(given[i], held[i], read.at[i]) for i in range(count)]
    stores = [pltpu.make_async_copy(held[i], taken[i], written.at[i]) for i in range(count)]
    for copy in loads:
        copy.start()
    for load, store in zip(loads, stores):
        load.wait()
        store.start()
    for copy in stores:
        copy.wait()


def hand_over(*arrays):
    hbm = pl.BlockSpec(memory_space=pl.ANY)
    return pl.pallas_call(
        hand_over_kernel,
        in_specs=[hbm] * len(arrays),
        out_specs=[hbm] * len(arrays),
        out_shape=[jax.ShapeDtypeStruct(a.shape, a.dtype) for a in arrays],
        scratch_shapes=[pltpu.VMEM(a.shape, a.dtype) for a in arrays]
        + [pltpu.SemaphoreType.DMA((len(arrays),))] * 2,
        name="hand_over",
    )(*arrays)


def needs_relay(mesh):
    axis = mesh.axis_names.index("ctx")
    line = np.moveaxis(mesh.devices, axis, 0).reshape(mesh.shape["ctx"], -1)[:, 0]
    places = [getattr(device, "coords", None) for device in line]
    if any(place is None for place in places) or len(places) < 4:
        return False
    hops = lambda a, b: sum(abs(x - y) for x, y in zip(places[a], places[b]))
    middle, end = len(places) // 2 - 1, len(places) - 1
    return (
        hops(middle, middle + 1) == 2
        and hops(middle, end) == hops(end, middle + 1) == 1
        and hops(middle + 1, 0) == hops(0, middle) == 1
    )


def shards(relay, query_input, key_input, value_input, filters, complement, doc_lengths, cotangent):
    rows, channels = query_input.shape
    taps = filters.shape[1]
    ctx, ch = lax.axis_size("ctx"), lax.axis_size("ch")
    groups = min(ctx, taps // TILE)
    height, share, size = taps // groups, taps // ctx, 2 * rows
    block = channel_block(channels)
    chunks = channels // block
    slots = PACK - 1 + -(-doc_lengths.shape[0] // PACK)
    tables = [jnp.asarray(table) for table in fourier_tables(rows, taps)]
    fetched = [query_input, key_input, value_input, cotangent, filters, *tables]
    hbm = pl.BlockSpec(memory_space=pl.ANY)
    vmem = pl.BlockSpec(memory_space=pltpu.VMEM)
    dma = pltpu.SemaphoreType.DMA
    field = jax.ShapeDtypeStruct((rows, channels), BF16)
    *mixed, grad_filter = pl.pallas_call(
        functools.partial(entry_kernel, ctx, ch, groups, block, relay, len(fetched)),
        in_specs=[pl.BlockSpec(memory_space=pltpu.SMEM), vmem] + [hbm] * len(fetched),
        out_specs=[hbm] * 4 + [vmem],
        out_shape=[field] * 4 + [jax.ShapeDtypeStruct((share, channels), F32)],
        scratch_shapes=[pltpu.VMEM(a.shape, a.dtype) for a in fetched]
        + [
            dma((len(fetched),)),
            pltpu.VMEM((rows, channels), BF16),
            pltpu.VMEM((rows, channels), BF16),
            pltpu.VMEM((4, rows, channels), BF16),
            pltpu.VMEM((2, rows, channels), BF16),
            pltpu.VMEM((ch, height, channels), BF16),
            pltpu.VMEM((height, channels), BF16),
            pltpu.VMEM((groups, height, channels), BF16),
            pltpu.VMEM((4, rows, channels), BF16),
            pltpu.VMEM((2, 2, ctx // 2, share, channels), BF16),
            pltpu.VMEM((2, ctx // 2, share, channels), BF16),
            pltpu.VMEM((2, ctx // 2, share, channels), BF16),
            pltpu.VMEM((ctx // 2 - 1, 2, share, channels), BF16),
            pltpu.VMEM((ch, -(-share // TILE) * TILE, channels), BF16),
            pltpu.VMEM((slots, size, rows), BF16),
            pltpu.VMEM((rows, (slots + 2) * size), BF16),
            pltpu.VMEM((2, size, rows), BF16),
            pltpu.VMEM((2, size, rows), BF16),
            pltpu.VMEM((2 * size, channels), F32),
            pltpu.VMEM((2 * size, channels), F32),
            pltpu.VMEM((2 * size, channels), F32),
            pltpu.VMEM((slots, size, channels), F32),
            pltpu.VMEM((slots, size, channels), F32),
            pltpu.VMEM((2, 2, size, channels), F32),
            pltpu.VMEM((2, size, channels), F32),
            pltpu.VMEM((2, size, channels), F32),
            pltpu.VMEM(((slots + 2) * size, block), BF16),
            pltpu.VMEM(((slots + 2) * size, block), BF16),
            pltpu.VMEM((2, taps, channels), F32),
            dma((4 * chunks,)), dma((4 * chunks,)), dma((2 * chunks,)), dma((2 * chunks,)), dma((ch - 1,)), dma((ch - 1,)),
            dma((groups - 1,)), dma((groups - 1,)),
            dma((chunks,)), dma((chunks,)),
            dma(((ctx // 2 - 1) * chunks,)), dma(((ctx // 2 - 1) * chunks,)), dma(((ch - 1) * chunks,)), dma(((ch - 1) * chunks,)), dma((5,)),
        ],
        compiler_params=pltpu.CompilerParams(
            collective_id=0, has_side_effects=True, vmem_limit_bytes=VMEM_BYTES
        ),
        name="mixer",
    )(doc_lengths, complement, *fetched)
    *mixed, grad_filter = hand_over(*mixed, grad_filter)
    return (*mixed, grad_filter.T)


def solution(mesh):
    placed = (
        P("ctx", "ch"),
        P("ctx", "ch"),
        P("ctx", "ch"),
        P("ch", None),
        P("ch"),
        P(),
        P("ctx", "ch"),
    )
    return jax.shard_map(
        functools.partial(shards, needs_relay(mesh)),
        mesh=mesh,
        in_specs=placed,
        out_specs=(P("ctx", "ch"), P("ctx", "ch"), P("ctx", "ch"), P("ctx", "ch"), P("ch", "ctx")),
        check_vma=False,
    )
```

```python
import functools

import jax
import jax.numpy as jnp
import numpy as np
from jax import lax
from jax.experimental import pallas as pl
from jax.experimental.pallas import tpu as pltpu
from jax.sharding import PartitionSpec as P

F32, BF16 = jnp.float32, jnp.bfloat16
LANES, TILE, PACK = 128, 16, 4
VMEM_BYTES = 56 * 2**20


def split_bf16(table):
    high = table.astype(BF16)
    low = (table - high.astype(np.float64)).astype(BF16)
    return high, low


def wave(places, length):
    angle = 2.0 * np.pi * (np.arange(length // 2) + 0.5) / length
    turns = angle[:, None] * np.asarray(places)[None, :]
    return np.cos(turns), np.sin(turns)


def fourier_tables(rows, taps):
    long, short = 2 * rows, 2 * rows // PACK
    cos, sin = wave(np.arange(3 * rows) - rows, long)
    analyse = np.concatenate([cos, -sin], axis=0)
    cos_s, sin_s = wave(np.arange(rows), short)
    pack = lambda table: np.tile(table, (PACK, 1))
    analyse_short = np.concatenate([pack(cos_s), pack(-sin_s)], axis=0)
    near = (np.arange(taps) < short // 2)[None, :]
    lag_cos, lag_sin = wave(np.arange(taps), long)
    near_cos, near_sin = [pack(table * near) for table in wave(np.arange(taps), short)]
    causal = np.concatenate([lag_cos, -lag_sin, near_cos, -near_sin], axis=0)
    anti = np.concatenate([lag_cos, lag_sin, near_cos, near_sin], axis=0)
    forward = causal.T.copy()
    backward = anti.T.copy()
    for table in (forward, backward):
        table[:, : 2 * rows] *= 2.0 / long
        table[:, 2 * rows :] *= 2.0 / short
    rebuild = analyse[:, rows : 2 * rows].T * (2.0 / long)
    rebuild_short = analyse_short.T * (2.0 / short)
    return (
        analyse.astype(BF16),
        analyse_short.astype(BF16),
        rebuild.astype(BF16),
        rebuild_short.astype(BF16),
        *split_bf16(causal),
        *split_bf16(anti),
        *split_bf16(forward),
        *split_bf16(backward),
    )


def mm(a, b):
    return jnp.dot(a, b, preferred_element_type=F32)


def mm_t(a, b):
    return lax.dot_general(a, b, (((1,), (1,)), ((), ())), preferred_element_type=F32)


def mm_fine(hi, lo, x):
    x_hi = x.astype(BF16)
    x_lo = (x - x_hi.astype(F32)).astype(BF16)
    return mm(hi, x_hi) + mm(hi, x_lo) + mm(lo, x_hi)


def product_of(a, b):
    return (a.astype(F32) * b.astype(F32)).astype(BF16)


def flag(mask):
    return mask.astype(F32).astype(BF16)


def times(a, x):
    half = a.shape[0] // 2
    a_re, a_im, x_re, x_im = a[:half], a[half:], x[:half], x[half:]
    return a_re * x_re - a_im * x_im, a_re * x_im + a_im * x_re


def times_conj(a, x):
    half = a.shape[0] // 2
    a_re, a_im, x_re, x_im = a[:half], a[half:], x[:half], x[half:]
    return a_re * x_re + a_im * x_im, a_re * x_im - a_im * x_re


def remote(src, dst, sems, index, device):
    return pltpu.make_async_remote_copy(
        src_ref=src, dst_ref=dst, send_sem=sems[0].at[index], recv_sem=sems[1].at[index],
        device_id=device, device_id_type=pl.DeviceIdType.MESH,
    )


def announce(devices):
    barrier = pltpu.get_barrier_semaphore()
    for device in devices:
        pl.semaphore_signal(barrier, inc=1, device_id=device, device_id_type=pl.DeviceIdType.MESH)


def gathered_in(devices):
    pl.semaphore_wait(pltpu.get_barrier_semaphore(), len(devices))


def pick_partners(complement, landed, ch, channels):
    mine = lax.axis_index("ch")
    owner = sum((complement >= k * channels).astype(jnp.int32) for k in range(1, ch)) + jnp.zeros_like(complement)
    step = mine - owner
    step = jnp.where(step < 0, step + ch, step)
    local = complement - owner * channels
    blocks = channels // LANES
    block = step * blocks + lax.shift_right_logical(local, 7)
    within = lax.bitwise_and(local, LANES - 1)
    sublane = lax.broadcasted_iota(jnp.int32, (LANES, channels), 0)
    chosen = flag(sublane == within)
    stacked = jnp.concatenate(
        [landed[s, :, b * LANES : (b + 1) * LANES] for s in range(ch) for b in range(blocks)], axis=0
    )
    spread_out = mm(stacked, chosen)
    height = landed.shape[1]
    total = jnp.zeros((height, channels), F32)
    for b in range(ch * blocks):
        total = total + jnp.where(block == b, spread_out[b * height : (b + 1) * height], 0.0)
    return total


def survey(lens, rows, first_place):
    limit = rows // PACK
    lane3 = lax.broadcasted_iota(jnp.int32, (1, 3 * rows), 1) - rows
    lane = lax.broadcasted_iota(jnp.int32, (1, rows), 1)
    column = lax.broadcasted_iota(jnp.int32, (rows, 1), 0)
    low = -first_place
    found, base, last = jnp.int32(0), jnp.int32(0), jnp.int32(0)
    seen = jnp.zeros_like(lane3)
    seen_column = jnp.zeros_like(column)
    long_lane, short_lane = jnp.zeros_like(lane), jnp.zeros_like(lane)
    long_column, short_column = jnp.zeros_like(column), jnp.zeros_like(column)
    for d in range(lens.shape[0]):
        high = low + lens[d]
        own = jnp.minimum(high, rows) - jnp.maximum(low, 0)
        is_long = jnp.where(own > limit, 1, 0)
        found = found + is_long
        long_code = is_long * found
        short_code = (1 - is_long) * (d + 1)
        inside = (lane >= low) & (lane < high)
        long_lane = jnp.where(inside, long_code, long_lane)
        short_lane = jnp.where(inside, short_code, short_lane)
        inside = (column >= low) & (column < high)
        long_column = jnp.where(inside, long_code, long_column)
        short_column = jnp.where(inside, short_code, short_column)
        seen = seen + jnp.where(lane3 >= low, 1, 0)
        seen_column = seen_column + jnp.where(column >= low, 1, 0)
        base = base + jnp.where(low <= 0, 1, 0)
        last = last + jnp.where(low <= rows - 1, 1, 0)
        low = high
    seen = seen + jnp.where(lane3 >= low, 1, 0)
    return long_lane, short_lane, long_column, short_column, seen, seen_column, base, last


def mixer_kernel(
    ctx, ch, groups, block, relay, fetches,
    lens, query, key, value, cot, filters, complement,
    analyse, analyse_short, rebuild, rebuild_short,
    causal_hi, causal_lo, anti_hi, anti_lo, fwd_hi, fwd_lo, bwd_hi, bwd_lo,
    mixer_out, grad_query, grad_key, grad_value, grad,
    u, r, halos, via, landed, picked, partner, outs, pieces, twins, joined, arrived, sent,
    masked, back, outer, own_ends,
    ahead, behind, both, u_hat, o_hat, far_hat, ends_hat, acc_g, z_ref, q_ref, acc_t,
    halo_send, halo_recv, via_send, via_recv, ch_send, ch_recv, mate_send, mate_recv,
    twin_send, twin_recv, sum_send, sum_recv, back_send, back_recv, local,
):
    me, mine = lax.axis_index("ctx"), lax.axis_index("ch")
    rows, channels = query.shape
    taps = filters.shape[1]
    size = 2 * rows
    chunks = channels // block
    slots = masked.shape[0]
    longs = PACK - 1
    after, before = {"ctx": (me + 1) % ctx}, {"ctx": (me + ctx - 1) % ctx}
    group, octet = me % groups, me - me % groups
    height = taps // groups
    share = grad.shape[0]
    others = [{"ctx": (me + step) % ctx} for step in range(1, ctx)]
    peers = [{"ch": (mine + step) % ch} for step in range(1, ch)]
    mates = [{"ctx": octet + (group + step) % groups} for step in range(1, groups)]
    announce(others + peers)
    for copy in fetches:
        copy.start()
    for copy in fetches[:5]:
        copy.wait()

    row = lax.broadcasted_iota(jnp.int32, (height, taps), 0)
    tap = lax.broadcasted_iota(jnp.int32, (height, taps), 1)
    landed[0] = mm_t(flag(tap == row + group * height), filters[...]).astype(BF16)
    u[...] = product_of(key[...], value[...])
    r[...] = product_of(cot[...], query[...])

    gathered_in(others + peers)
    along = [
        remote(landed.at[0], landed.at[step], (ch_send, ch_recv), step - 1, peers[step - 1])
        for step in range(1, ch)
    ]
    for copy in along[::-1]:
        copy.start()
    has_next, has_prev = me < ctx - 1, me > 0
    middle = ctx // 2 - 1
    at_middle = (me == middle) | (me == middle + 1)
    end = jnp.where(me == middle, ctx - 1, 0)
    starts, send_waits, recv_waits, forwards = [], [], [], []
    for c in range(chunks):
        lanes = pl.ds(c * block, block)
        for kind, field in enumerate((u, r)):
            index = c * 2 + kind
            detour = relay and index >= chunks
            to_next = remote(field.at[:, lanes], halos.at[kind, :, lanes],
                             (halo_send, halo_recv), c * 4 + kind, after)
            to_prev = remote(field.at[:, lanes], halos.at[2 + kind, :, lanes],
                             (halo_send, halo_recv), c * 4 + 2 + kind, before)
            starts.append([(has_next & (me != middle) if detour else has_next, to_next),
                           (has_prev & (me != middle + 1) if detour else has_prev, to_prev)])
            send_waits += starts[-1]
            recv_waits.append([(has_prev, to_next), (has_next, to_prev)])
            if detour:
                away = remote(field.at[:, lanes], via.at[kind, :, lanes], (via_send, via_recv), index, {"ctx": end})
                starts[-1].append((at_middle, away))
                send_waits.append((at_middle, away))
                from_last = remote(via.at[kind, :, lanes], halos.at[kind, :, lanes],
                                   (halo_send, halo_recv), c * 4 + kind, {"ctx": middle + 1})
                from_first = remote(via.at[kind, :, lanes], halos.at[2 + kind, :, lanes],
                                    (halo_send, halo_recv), c * 4 + 2 + kind, {"ctx": middle})
                forwards.append((away, from_last, from_first))

    def start_halos(chunk):
        for condition, copy in starts[2 * chunk] + starts[2 * chunk + 1]:
            pl.when(condition)(copy.start)

    for chunk in range(chunks):
        start_halos(chunk)

    @pl.when(jnp.logical_not(has_prev))
    def _():
        halos[0:2] = jnp.zeros((2, rows, channels), BF16)

    @pl.when(jnp.logical_not(has_next))
    def _():
        halos[2:4] = jnp.zeros((2, rows, channels), BF16)

    long_lane, short_lane, long_column, short_column, seen, seen_column, base, last = survey(
        lens, rows, me * rows
    )
    for copy in fetches[5:]:
        copy.wait()
    quarter = rows // PACK
    packed_row = (lax.broadcasted_iota(jnp.int32, (size, 1), 0) % rows) // quarter
    packed_lane = (lax.broadcasted_iota(jnp.int32, (1, size), 1) % rows) // quarter
    for s in range(slots):
        cols = pl.ds(s * size, size)
        if s < longs:
            masked[s] = analyse[:, rows : 2 * rows] * flag(long_lane == s + 1)
            back[:, cols] = rebuild[...] * flag(long_column == s + 1)
        else:
            first = (s - longs) * PACK + 1
            masked[s] = analyse_short[...] * flag(short_lane == first + packed_row)
            back[:, cols] = rebuild_short[...] * flag(short_column == first + packed_lane)
    for e, code in enumerate((base, last)):
        section = slice(2 * e * rows, (2 * e + 1) * rows)
        outer[e] = analyse[:, section] * flag(seen[:, section] == code)
        own_ends[e] = analyse[:, rows : 2 * rows] * flag(seen[:, rows : 2 * rows] == code)
        back[:, pl.ds((slots + e) * size, size)] = rebuild[...] * flag(seen_column == code)

    ahead[...] = mm_t(causal_hi[...], filters[...]) + mm_t(causal_lo[...], filters[...])

    def analysis(c, carry):
        lanes = pl.ds(pl.multiple_of(c * block, LANES), block)
        u_own, r_own = u[:, lanes], r[:, lanes]
        for s in range(slots):
            u_now, o_now = mm(masked[s], u_own), mm(masked[s], r_own)
            u_hat[s, :, lanes] = u_now
            o_hat[s, :, lanes] = o_now
            g_re, g_im = times_conj(u_now, o_now)
            kind = 0 if s < longs else 1
            if s == 0 or s == longs:
                acc_g[kind, :rows, lanes] = g_re
                acc_g[kind, rows:, lanes] = g_im
            else:
                acc_g[kind, :rows, lanes] += g_re
                acc_g[kind, rows:, lanes] += g_im
        for e in range(2):
            ends_hat[e, :, lanes] = mm(own_ends[e], r_own)
        own = jnp.concatenate([acc_g[0, :, lanes], acc_g[1, :, lanes]], axis=0)
        acc_t[0, :, lanes] = mm_fine(fwd_hi[...], fwd_lo[...], own)
        acc_t[1, :, lanes] = mm_fine(bwd_hi[...], bwd_lo[...], own)
        return carry

    lax.fori_loop(0, chunks, analysis, 0)

    for arriving, from_last, from_first in forwards:
        @pl.when(me == ctx - 1)
        def _():
            arriving.wait_recv()
            from_last.start()

        @pl.when(me == 0)
        def _():
            arriving.wait_recv()
            from_first.start()


    for copy in along:
        copy.wait()
    picked[...] = pick_partners(complement[...].reshape(1, channels), landed, ch, channels).astype(BF16)
    shared = [
        remote(picked, partner.at[group], (mate_send, mate_recv), step - 1, mates[step - 1])
        for step in range(1, groups)
    ]
    for copy in shared:
        copy.start()
    keep = pltpu.make_async_copy(picked, partner.at[group], local.at[0])
    keep.start()
    core, chip, chips = me % 2, me // 2, ctx // 2
    swaps, sums = [], []

    def send_taps(c):
        lanes = pl.ds(c * block, block)
        for condition, copy in recv_waits[2 * c] + recv_waits[2 * c + 1]:
            pl.when(condition)(copy.wait_recv)
        for e in range(2):
            u_far = mm(outer[e], halos[2 * e, :, lanes])
            far_hat[e, 0, :, lanes] = u_far
            far_hat[e, 1, :, lanes] = mm(outer[e], halos[2 * e + 1, :, lanes])
            g_re, g_im = times_conj(u_far, ends_hat[e, :, lanes])
            hi, lo = (fwd_hi, fwd_lo) if e == 0 else (bwd_hi, bwd_lo)
            far = jnp.concatenate([g_re, g_im], axis=0)
            tap_sums = acc_t[e, :, lanes] + mm_fine(hi[:, :size], lo[:, :size], far)
            for i in range(ctx):
                pieces[i % 2, e, i // 2, :, lanes] = tap_sums[i * share : (i + 1) * share].astype(BF16)
        copy = remote(pieces.at[1 - core, :, :, :, lanes], twins.at[:, :, :, lanes],
                      (twin_send, twin_recv), c, {"ctx": me + 1 - 2 * core})
        copy.start()
        swaps.append(copy)

    def join_taps(c):
        lanes = pl.ds(c * block, block)
        swaps[c].wait()
        joined[:, :, :, lanes] = (
            pieces[core, :, :, :, lanes].astype(F32) + twins[:, :, :, lanes].astype(F32)
        ).astype(BF16)
        for step in range(1, chips):
            copy = remote(joined.at[:, (chip + step) % chips, :, lanes], arrived.at[step - 1, :, :, lanes],
                          (sum_send, sum_recv), c * (chips - 1) + step - 1, {"ctx": (me + 2 * step) % ctx})
            copy.start()
            sums.append(copy)

    def filtering(c):
        lanes = pl.ds(c * block, block)

        def keep_products(s, z, q):
            z_ref[s * size : s * size + rows] = z[0].astype(BF16)
            z_ref[s * size + rows : (s + 1) * size] = z[1].astype(BF16)
            q_ref[s * size : s * size + rows] = q[0].astype(BF16)
            q_ref[s * size + rows : (s + 1) * size] = q[1].astype(BF16)

        for s in range(slots):
            kind = 0 if s < longs else 1
            h = both[kind * size : (kind + 1) * size, lanes]
            keep_products(s, times(h, u_hat[s, :, lanes]), times_conj(h, o_hat[s, :, lanes]))
        for e in range(2):
            for_u, for_r = (ahead, behind) if e == 0 else (behind, ahead)
            keep_products(
                slots + e,
                times(for_u[:size, lanes], far_hat[e, 0, :, lanes]),
                times_conj(for_r[:size, lanes], far_hat[e, 1, :, lanes]),
            )
        combined = mm(back[...], z_ref[...])
        grad_product = mm(back[...], q_ref[...])
        outs[0, :, lanes] = (query[:, lanes].astype(F32) * combined).astype(BF16)
        outs[1, :, lanes] = (cot[:, lanes].astype(F32) * combined).astype(BF16)
        outs[2, :, lanes] = (grad_product * value[:, lanes].astype(F32)).astype(BF16)
        outs[3, :, lanes] = (grad_product * key[:, lanes].astype(F32)).astype(BF16)
        for index, place in enumerate((mixer_out, grad_query, grad_key, grad_value)):
            copy = pltpu.make_async_copy(outs.at[index, :, lanes], place.at[:, lanes], local.at[1 + c * 4 + index])
            copy.start()
            stores.append(copy)

    across, stores = [], []

    def send_mirrored(c):
        lanes = pl.ds(c * block, block)
        for copy in sums[c * (chips - 1) : (c + 1) * (chips - 1)]:
            copy.wait()
        total = sum(arrived[step, 1, :, lanes].astype(F32) for step in range(chips - 1))
        sent[0, :share, lanes] = (total + joined[1, chip, :, lanes].astype(F32)).astype(BF16)
        for step in range(1, ch):
            copy = remote(sent.at[0, :, lanes], sent.at[step, :, lanes],
                          (back_send, back_recv), c * (ch - 1) + step - 1, peers[step - 1])
            copy.start()
            across.append(copy)

    if share < sent.shape[1]:
        sent[...] = jnp.zeros_like(sent)
    for c in range(chunks):
        send_taps(c)
        if c > 0:
            join_taps(c - 1)
    join_taps(chunks - 1)
    for copy in shared:
        copy.wait()
    keep.wait()
    g = partner[...].reshape(taps, channels)
    behind[...] = mm(anti_hi[...], g) + mm(anti_lo[...], g)
    both[...] = ahead[...] + behind[...]
    filtering(0)
    for c in range(chunks):
        send_mirrored(c)
    for c in range(1, chunks):
        filtering(c)
    own = joined[0, chip].astype(F32) + sum(arrived[step, 0].astype(F32) for step in range(chips - 1))
    for condition, copy in send_waits:
        pl.when(condition)(copy.wait_send)
    for _, from_last, from_first in forwards:
        pl.when(me == ctx - 1)(from_last.wait_send)
        pl.when(me == 0)(from_first.wait_send)
    for copy in across:
        copy.wait()
    grad[...] = own + pick_partners(complement[...].reshape(1, channels), sent, ch, channels)[:share]
    for copy in stores:
        copy.wait()


def entry_kernel(ctx, ch, groups, block, relay, count, lens, complement, *refs):
    given, results, held, fetch = refs[:count], refs[count : count + 5], refs[count + 5 : 2 * count + 5], refs[2 * count + 5]
    fetches = [pltpu.make_async_copy(given[i], held[i], fetch.at[i]) for i in range(count)]
    mixer_kernel(
        ctx, ch, groups, block, relay, fetches,
        lens, *held[:5], complement, *held[5:], *results, *refs[2 * count + 6 :],
    )


def channel_block(channels):
    for block in (384, 256, 128):
        if channels % block == 0:
            return block
    return channels


def hand_over_kernel(*refs):
    count = (len(refs) - 2) // 3
    given, taken, held, (read, written) = refs[:count], refs[count : 2 * count], refs[2 * count : -2], refs[-2:]
    loads = [pltpu.make_async_copy(given[i], held[i], read.at[i]) for i in range(count)]
    stores = [pltpu.make_async_copy(held[i], taken[i], written.at[i]) for i in range(count)]
    for copy in loads:
        copy.start()
    for load, store in zip(loads, stores):
        load.wait()
        store.start()
    for copy in stores:
        copy.wait()


def hand_over(*arrays):
    hbm = pl.BlockSpec(memory_space=pl.ANY)
    return pl.pallas_call(
        hand_over_kernel,
        in_specs=[hbm] * len(arrays),
        out_specs=[hbm] * len(arrays),
        out_shape=[jax.ShapeDtypeStruct(a.shape, a.dtype) for a in arrays],
        scratch_shapes=[pltpu.VMEM(a.shape, a.dtype) for a in arrays]
        + [pltpu.SemaphoreType.DMA((len(arrays),))] * 2,
        name="hand_over",
    )(*arrays)


def needs_relay(mesh):
    axis = mesh.axis_names.index("ctx")
    line = np.moveaxis(mesh.devices, axis, 0).reshape(mesh.shape["ctx"], -1)[:, 0]
    places = [getattr(device, "coords", None) for device in line]
    if any(place is None for place in places) or len(places) < 4:
        return False
    hops = lambda a, b: sum(abs(x - y) for x, y in zip(places[a], places[b]))
    middle, end = len(places) // 2 - 1, len(places) - 1
    return (
        hops(middle, middle + 1) == 2
        and hops(middle, end) == hops(end, middle + 1) == 1
        and hops(middle + 1, 0) == hops(0, middle) == 1
    )


def shards(relay, query_input, key_input, value_input, filters, complement, doc_lengths, cotangent):
    rows, channels = query_input.shape
    taps = filters.shape[1]
    ctx, ch = lax.axis_size("ctx"), lax.axis_size("ch")
    groups = min(ctx, taps // TILE)
    height, share, size = taps // groups, taps // ctx, 2 * rows
    block = channel_block(channels)
    chunks = channels // block
    slots = PACK - 1 + -(-doc_lengths.shape[0] // PACK)
    tables = [jnp.asarray(table) for table in fourier_tables(rows, taps)]
    fetched = [query_input, key_input, value_input, cotangent, filters, *tables]
    hbm = pl.BlockSpec(memory_space=pl.ANY)
    vmem = pl.BlockSpec(memory_space=pltpu.VMEM)
    dma = pltpu.SemaphoreType.DMA
    field = jax.ShapeDtypeStruct((rows, channels), BF16)
    *mixed, grad_filter = pl.pallas_call(
        functools.partial(entry_kernel, ctx, ch, groups, block, relay, len(fetched)),
        in_specs=[pl.BlockSpec(memory_space=pltpu.SMEM), vmem] + [hbm] * len(fetched),
        out_specs=[hbm] * 4 + [vmem],
        out_shape=[field] * 4 + [jax.ShapeDtypeStruct((share, channels), F32)],
        scratch_shapes=[pltpu.VMEM(a.shape, a.dtype) for a in fetched]
        + [
            dma((len(fetched),)),
            pltpu.VMEM((rows, channels), BF16),
            pltpu.VMEM((rows, channels), BF16),
            pltpu.VMEM((4, rows, channels), BF16),
            pltpu.VMEM((2, rows, channels), BF16),
            pltpu.VMEM((ch, height, channels), BF16),
            pltpu.VMEM((height, channels), BF16),
            pltpu.VMEM((groups, height, channels), BF16),
            pltpu.VMEM((4, rows, channels), BF16),
            pltpu.VMEM((2, 2, ctx // 2, share, channels), BF16),
            pltpu.VMEM((2, ctx // 2, share, channels), BF16),
            pltpu.VMEM((2, ctx // 2, share, channels), BF16),
            pltpu.VMEM((ctx // 2 - 1, 2, share, channels), BF16),
            pltpu.VMEM((ch, -(-share // TILE) * TILE, channels), BF16),
            pltpu.VMEM((slots, size, rows), BF16),
            pltpu.VMEM((rows, (slots + 2) * size), BF16),
            pltpu.VMEM((2, size, rows), BF16),
            pltpu.VMEM((2, size, rows), BF16),
            pltpu.VMEM((2 * size, channels), F32),
            pltpu.VMEM((2 * size, channels), F32),
            pltpu.VMEM((2 * size, channels), F32),
            pltpu.VMEM((slots, size, channels), F32),
            pltpu.VMEM((slots, size, channels), F32),
            pltpu.VMEM((2, 2, size, channels), F32),
            pltpu.VMEM((2, size, channels), F32),
            pltpu.VMEM((2, size, channels), F32),
            pltpu.VMEM(((slots + 2) * size, block), BF16),
            pltpu.VMEM(((slots + 2) * size, block), BF16),
            pltpu.VMEM((2, taps, channels), F32),
            dma((4 * chunks,)), dma((4 * chunks,)), dma((2 * chunks,)), dma((2 * chunks,)), dma((ch - 1,)), dma((ch - 1,)),
            dma((groups - 1,)), dma((groups - 1,)),
            dma((chunks,)), dma((chunks,)),
            dma(((ctx // 2 - 1) * chunks,)), dma(((ctx // 2 - 1) * chunks,)), dma(((ch - 1) * chunks,)), dma(((ch - 1) * chunks,)), dma((1 + 4 * chunks,)),
        ],
        compiler_params=pltpu.CompilerParams(
            collective_id=0, has_side_effects=True, vmem_limit_bytes=VMEM_BYTES
        ),
        name="mixer",
    )(doc_lengths, complement, *fetched)
    *mixed, grad_filter = hand_over(*mixed, grad_filter)
    return (*mixed, grad_filter.T)


def solution(mesh):
    placed = (
        P("ctx", "ch"),
        P("ctx", "ch"),
        P("ctx", "ch"),
        P("ch", None),
        P("ch"),
        P(),
        P("ctx", "ch"),
    )
    return jax.shard_map(
        functools.partial(shards, needs_relay(mesh)),
        mesh=mesh,
        in_specs=placed,
        out_specs=(P("ctx", "ch"), P("ctx", "ch"), P("ctx", "ch"), P("ctx", "ch"), P("ch", "ctx")),
        check_vma=False,
    )
```

```python
import functools

import jax
import jax.numpy as jnp
import numpy as np
from jax import lax
from jax.experimental import pallas as pl
from jax.experimental.pallas import tpu as pltpu
from jax.sharding import PartitionSpec as P

F32, BF16 = jnp.float32, jnp.bfloat16
LANES, TILE, PACK = 128, 16, 4
VMEM_BYTES = 56 * 2**20


def split_bf16(table):
    high = table.astype(BF16)
    low = (table - high.astype(np.float64)).astype(BF16)
    return high, low


def wave(places, length):
    angle = 2.0 * np.pi * (np.arange(length // 2) + 0.5) / length
    turns = angle[:, None] * np.asarray(places)[None, :]
    return np.cos(turns), np.sin(turns)


def fourier_tables(rows, taps):
    long, short = 2 * rows, 2 * rows // PACK
    cos, sin = wave(np.arange(3 * rows) - rows, long)
    analyse = np.concatenate([cos, -sin], axis=0)
    cos_s, sin_s = wave(np.arange(rows), short)
    pack = lambda table: np.tile(table, (PACK, 1))
    analyse_short = np.concatenate([pack(cos_s), pack(-sin_s)], axis=0)
    near = (np.arange(taps) < short // 2)[None, :]
    lag_cos, lag_sin = wave(np.arange(taps), long)
    near_cos, near_sin = [pack(table * near) for table in wave(np.arange(taps), short)]
    causal = np.concatenate([lag_cos, -lag_sin, near_cos, -near_sin], axis=0)
    anti = np.concatenate([lag_cos, lag_sin, near_cos, near_sin], axis=0)
    forward = causal.T.copy()
    backward = anti.T.copy()
    for table in (forward, backward):
        table[:, : 2 * rows] *= 2.0 / long
        table[:, 2 * rows :] *= 2.0 / short
    rebuild = analyse[:, rows : 2 * rows].T * (2.0 / long)
    rebuild_short = analyse_short.T * (2.0 / short)
    return (
        analyse.astype(BF16),
        analyse_short.astype(BF16),
        rebuild.astype(BF16),
        rebuild_short.astype(BF16),
        *split_bf16(causal),
        *split_bf16(anti),
        *split_bf16(forward),
        *split_bf16(backward),
    )


def mm(a, b):
    return jnp.dot(a, b, preferred_element_type=F32)


def mm_t(a, b):
    return lax.dot_general(a, b, (((1,), (1,)), ((), ())), preferred_element_type=F32)


def mm_fine(hi, lo, x):
    x_hi = x.astype(BF16)
    x_lo = (x - x_hi.astype(F32)).astype(BF16)
    return mm(hi, x_hi) + mm(hi, x_lo) + mm(lo, x_hi)


def product_of(a, b):
    return (a.astype(F32) * b.astype(F32)).astype(BF16)


def flag(mask):
    return mask.astype(F32).astype(BF16)


def times(a, x):
    half = a.shape[0] // 2
    a_re, a_im, x_re, x_im = a[:half], a[half:], x[:half], x[half:]
    return a_re * x_re - a_im * x_im, a_re * x_im + a_im * x_re


def times_conj(a, x):
    half = a.shape[0] // 2
    a_re, a_im, x_re, x_im = a[:half], a[half:], x[:half], x[half:]
    return a_re * x_re + a_im * x_im, a_re * x_im - a_im * x_re


def remote(src, dst, sems, index, device):
    return pltpu.make_async_remote_copy(
        src_ref=src, dst_ref=dst, send_sem=sems[0].at[index], recv_sem=sems[1].at[index],
        device_id=device, device_id_type=pl.DeviceIdType.MESH,
    )


def announce(devices):
    barrier = pltpu.get_barrier_semaphore()
    for device in devices:
        pl.semaphore_signal(barrier, inc=1, device_id=device, device_id_type=pl.DeviceIdType.MESH)


def gathered_in(devices):
    pl.semaphore_wait(pltpu.get_barrier_semaphore(), len(devices))


def pick_partners(complement, landed, ch, channels):
    mine = lax.axis_index("ch")
    owner = sum((complement >= k * channels).astype(jnp.int32) for k in range(1, ch)) + jnp.zeros_like(complement)
    step = mine - owner
    step = jnp.where(step < 0, step + ch, step)
    local = complement - owner * channels
    blocks = channels // LANES
    block = step * blocks + lax.shift_right_logical(local, 7)
    within = lax.bitwise_and(local, LANES - 1)
    sublane = lax.broadcasted_iota(jnp.int32, (LANES, channels), 0)
    chosen = flag(sublane == within)
    stacked = jnp.concatenate(
        [landed[s, :, b * LANES : (b + 1) * LANES] for s in range(ch) for b in range(blocks)], axis=0
    )
    spread_out = mm(stacked, chosen)
    height = landed.shape[1]
    total = jnp.zeros((height, channels), F32)
    for b in range(ch * blocks):
        total = total + jnp.where(block == b, spread_out[b * height : (b + 1) * height], 0.0)
    return total


def survey(lens, rows, first_place):
    limit = rows // PACK
    lane3 = lax.broadcasted_iota(jnp.int32, (1, 3 * rows), 1) - rows
    lane = lax.broadcasted_iota(jnp.int32, (1, rows), 1)
    column = lax.broadcasted_iota(jnp.int32, (rows, 1), 0)
    low = -first_place
    found, base, last = jnp.int32(0), jnp.int32(0), jnp.int32(0)
    seen = jnp.zeros_like(lane3)
    seen_column = jnp.zeros_like(column)
    long_lane, short_lane = jnp.zeros_like(lane), jnp.zeros_like(lane)
    long_column, short_column = jnp.zeros_like(column), jnp.zeros_like(column)
    for d in range(lens.shape[0]):
        high = low + lens[d]
        own = jnp.minimum(high, rows) - jnp.maximum(low, 0)
        is_long = jnp.where(own > limit, 1, 0)
        found = found + is_long
        long_code = is_long * found
        short_code = (1 - is_long) * (d + 1)
        inside = (lane >= low) & (lane < high)
        long_lane = jnp.where(inside, long_code, long_lane)
        short_lane = jnp.where(inside, short_code, short_lane)
        inside = (column >= low) & (column < high)
        long_column = jnp.where(inside, long_code, long_column)
        short_column = jnp.where(inside, short_code, short_column)
        seen = seen + jnp.where(lane3 >= low, 1, 0)
        seen_column = seen_column + jnp.where(column >= low, 1, 0)
        base = base + jnp.where(low <= 0, 1, 0)
        last = last + jnp.where(low <= rows - 1, 1, 0)
        low = high
    seen = seen + jnp.where(lane3 >= low, 1, 0)
    return long_lane, short_lane, long_column, short_column, seen, seen_column, base, last


def mixer_kernel(
    ctx, ch, groups, block, relay, fetches,
    lens, query, key, value, cot, filters, complement,
    analyse, analyse_short, rebuild, rebuild_short,
    causal_hi, causal_lo, anti_hi, anti_lo, fwd_hi, fwd_lo, bwd_hi, bwd_lo,
    mixer_out, grad_query, grad_key, grad_value, grad,
    u, r, halos, via, landed, picked, partner, pieces, twins, joined, arrived, sent,
    masked, back, outer, own_ends,
    ahead, behind, both, u_hat, o_hat, far_hat, ends_hat, acc_g, z_ref, q_ref, acc_t,
    halo_send, halo_recv, via_send, via_recv, ch_send, ch_recv, mate_send, mate_recv,
    twin_send, twin_recv, sum_send, sum_recv, back_send, back_recv, local,
):
    me, mine = lax.axis_index("ctx"), lax.axis_index("ch")
    rows, channels = query.shape
    taps = filters.shape[1]
    size = 2 * rows
    chunks = channels // block
    slots = masked.shape[0]
    longs = PACK - 1
    after, before = {"ctx": (me + 1) % ctx}, {"ctx": (me + ctx - 1) % ctx}
    core, half = me % 2, groups // 2
    spot, octet = (me % groups) // 2, me - me % groups
    group = core * half + spot
    height = taps // groups
    share = grad.shape[0]
    others = [{"ctx": (me + step) % ctx} for step in range(1, ctx)]
    peers = [{"ch": (mine + step) % ch} for step in range(1, ch)]
    mates = [{"ctx": octet + 2 * ((spot + step) % half) + core} for step in range(1, half)]
    announce(others + peers)
    for copy in fetches:
        copy.start()
    for copy in fetches[:5]:
        copy.wait()

    row = lax.broadcasted_iota(jnp.int32, (height, taps), 0)
    tap = lax.broadcasted_iota(jnp.int32, (height, taps), 1)
    landed[0] = mm_t(flag(tap == row + group * height), filters[...]).astype(BF16)
    u[...] = product_of(key[...], value[...])
    r[...] = product_of(cot[...], query[...])

    gathered_in(others + peers)
    along = [
        remote(landed.at[0], landed.at[step], (ch_send, ch_recv), step - 1, peers[step - 1])
        for step in range(1, ch)
    ]
    for copy in along[::-1]:
        copy.start()
    has_next, has_prev = me < ctx - 1, me > 0
    middle = ctx // 2 - 1
    at_middle = (me == middle) | (me == middle + 1)
    end = jnp.where(me == middle, ctx - 1, 0)
    starts, send_waits, recv_waits, forwards = [], [], [], []
    for c in range(chunks):
        lanes = pl.ds(c * block, block)
        for kind, field in enumerate((u, r)):
            index = c * 2 + kind
            detour = relay and index >= chunks
            to_next = remote(field.at[:, lanes], halos.at[kind, :, lanes],
                             (halo_send, halo_recv), c * 4 + kind, after)
            to_prev = remote(field.at[:, lanes], halos.at[2 + kind, :, lanes],
                             (halo_send, halo_recv), c * 4 + 2 + kind, before)
            starts.append([(has_next & (me != middle) if detour else has_next, to_next),
                           (has_prev & (me != middle + 1) if detour else has_prev, to_prev)])
            send_waits += starts[-1]
            recv_waits.append([(has_prev, to_next), (has_next, to_prev)])
            if detour:
                away = remote(field.at[:, lanes], via.at[kind, :, lanes], (via_send, via_recv), index, {"ctx": end})
                starts[-1].append((at_middle, away))
                send_waits.append((at_middle, away))
                from_last = remote(via.at[kind, :, lanes], halos.at[kind, :, lanes],
                                   (halo_send, halo_recv), c * 4 + kind, {"ctx": middle + 1})
                from_first = remote(via.at[kind, :, lanes], halos.at[2 + kind, :, lanes],
                                    (halo_send, halo_recv), c * 4 + 2 + kind, {"ctx": middle})
                forwards.append((away, from_last, from_first))

    def start_halos(chunk):
        for condition, copy in starts[2 * chunk] + starts[2 * chunk + 1]:
            pl.when(condition)(copy.start)

    for chunk in range(chunks):
        start_halos(chunk)

    @pl.when(jnp.logical_not(has_prev))
    def _():
        halos[0:2] = jnp.zeros((2, rows, channels), BF16)

    @pl.when(jnp.logical_not(has_next))
    def _():
        halos[2:4] = jnp.zeros((2, rows, channels), BF16)

    long_lane, short_lane, long_column, short_column, seen, seen_column, base, last = survey(
        lens, rows, me * rows
    )
    for copy in fetches[5:]:
        copy.wait()
    quarter = rows // PACK
    packed_row = (lax.broadcasted_iota(jnp.int32, (size, 1), 0) % rows) // quarter
    packed_lane = (lax.broadcasted_iota(jnp.int32, (1, size), 1) % rows) // quarter
    for s in range(slots):
        cols = pl.ds(s * size, size)
        if s < longs:
            masked[s] = analyse[:, rows : 2 * rows] * flag(long_lane == s + 1)
            back[:, cols] = rebuild[...] * flag(long_column == s + 1)
        else:
            first = (s - longs) * PACK + 1
            masked[s] = analyse_short[...] * flag(short_lane == first + packed_row)
            back[:, cols] = rebuild_short[...] * flag(short_column == first + packed_lane)
    for e, code in enumerate((base, last)):
        section = slice(2 * e * rows, (2 * e + 1) * rows)
        outer[e] = analyse[:, section] * flag(seen[:, section] == code)
        own_ends[e] = analyse[:, rows : 2 * rows] * flag(seen[:, rows : 2 * rows] == code)
        back[:, pl.ds((slots + e) * size, size)] = rebuild[...] * flag(seen_column == code)

    ahead[...] = mm_t(causal_hi[...], filters[...]) + mm_t(causal_lo[...], filters[...])

    def analysis(c, carry):
        lanes = pl.ds(pl.multiple_of(c * block, LANES), block)
        u_own, r_own = u[:, lanes], r[:, lanes]
        for s in range(slots):
            u_now, o_now = mm(masked[s], u_own), mm(masked[s], r_own)
            u_hat[s, :, lanes] = u_now
            o_hat[s, :, lanes] = o_now
            g_re, g_im = times_conj(u_now, o_now)
            kind = 0 if s < longs else 1
            if s == 0 or s == longs:
                acc_g[kind, :rows, lanes] = g_re
                acc_g[kind, rows:, lanes] = g_im
            else:
                acc_g[kind, :rows, lanes] += g_re
                acc_g[kind, rows:, lanes] += g_im
        for e in range(2):
            ends_hat[e, :, lanes] = mm(own_ends[e], r_own)
        own = jnp.concatenate([acc_g[0, :, lanes], acc_g[1, :, lanes]], axis=0)
        acc_t[0, :, lanes] = mm_fine(fwd_hi[...], fwd_lo[...], own)
        acc_t[1, :, lanes] = mm_fine(bwd_hi[...], bwd_lo[...], own)
        return carry

    lax.fori_loop(0, chunks, analysis, 0)

    for arriving, from_last, from_first in forwards:
        @pl.when(me == ctx - 1)
        def _():
            arriving.wait_recv()
            from_last.start()

        @pl.when(me == 0)
        def _():
            arriving.wait_recv()
            from_first.start()


    for copy in along:
        copy.wait()
    picked[...] = pick_partners(complement[...].reshape(1, channels), landed, ch, channels).astype(BF16)
    shared = [
        remote(picked, partner.at[group], (mate_send, mate_recv), step - 1, mates[step - 1])
        for step in range(1, half)
    ]
    for copy in shared:
        copy.start()
    keep = pltpu.make_async_copy(picked, partner.at[group], local.at[0])
    keep.start()
    chip, chips = me // 2, ctx // 2
    swaps, sums = [], []

    def send_taps(c):
        lanes = pl.ds(c * block, block)
        for condition, copy in recv_waits[2 * c] + recv_waits[2 * c + 1]:
            pl.when(condition)(copy.wait_recv)
        for e in range(2):
            u_far = mm(outer[e], halos[2 * e, :, lanes])
            far_hat[e, 0, :, lanes] = u_far
            far_hat[e, 1, :, lanes] = mm(outer[e], halos[2 * e + 1, :, lanes])
            g_re, g_im = times_conj(u_far, ends_hat[e, :, lanes])
            hi, lo = (fwd_hi, fwd_lo) if e == 0 else (bwd_hi, bwd_lo)
            far = jnp.concatenate([g_re, g_im], axis=0)
            tap_sums = acc_t[e, :, lanes] + mm_fine(hi[:, :size], lo[:, :size], far)
            for i in range(ctx):
                pieces[i % 2, e, i // 2, :, lanes] = tap_sums[i * share : (i + 1) * share].astype(BF16)
        copy = remote(pieces.at[1 - core, :, :, :, lanes], twins.at[:, :, :, lanes],
                      (twin_send, twin_recv), c, {"ctx": me + 1 - 2 * core})
        copy.start()
        swaps.append(copy)

    def join_taps(c):
        lanes = pl.ds(c * block, block)
        swaps[c].wait()
        joined[:, :, :, lanes] = (
            pieces[core, :, :, :, lanes].astype(F32) + twins[:, :, :, lanes].astype(F32)
        ).astype(BF16)
        for step in range(1, chips):
            copy = remote(joined.at[:, (chip + step) % chips, :, lanes], arrived.at[step - 1, :, :, lanes],
                          (sum_send, sum_recv), c * (chips - 1) + step - 1, {"ctx": (me + 2 * step) % ctx})
            copy.start()
            sums.append(copy)

    def filtering(c):
        lanes = pl.ds(c * block, block)

        def keep_products(s, z, q):
            z_ref[s * size : s * size + rows] = z[0].astype(BF16)
            z_ref[s * size + rows : (s + 1) * size] = z[1].astype(BF16)
            q_ref[s * size : s * size + rows] = q[0].astype(BF16)
            q_ref[s * size + rows : (s + 1) * size] = q[1].astype(BF16)

        for s in range(slots):
            kind = 0 if s < longs else 1
            h = both[kind * size : (kind + 1) * size, lanes]
            keep_products(s, times(h, u_hat[s, :, lanes]), times_conj(h, o_hat[s, :, lanes]))
        for e in range(2):
            for_u, for_r = (ahead, behind) if e == 0 else (behind, ahead)
            keep_products(
                slots + e,
                times(for_u[:size, lanes], far_hat[e, 0, :, lanes]),
                times_conj(for_r[:size, lanes], far_hat[e, 1, :, lanes]),
            )
        combined = mm(back[...], z_ref[...])
        grad_product = mm(back[...], q_ref[...])
        mixer_out[:, lanes] = (query[:, lanes].astype(F32) * combined).astype(BF16)
        grad_query[:, lanes] = (cot[:, lanes].astype(F32) * combined).astype(BF16)
        grad_key[:, lanes] = (grad_product * value[:, lanes].astype(F32)).astype(BF16)
        grad_value[:, lanes] = (grad_product * key[:, lanes].astype(F32)).astype(BF16)

    across = []

    def send_mirrored(c):
        lanes = pl.ds(c * block, block)
        for copy in sums[c * (chips - 1) : (c + 1) * (chips - 1)]:
            copy.wait()
        total = sum(arrived[step, 1, :, lanes].astype(F32) for step in range(chips - 1))
        sent[0, :share, lanes] = (total + joined[1, chip, :, lanes].astype(F32)).astype(BF16)
        for step in range(1, ch):
            copy = remote(sent.at[0, :, lanes], sent.at[step, :, lanes],
                          (back_send, back_recv), c * (ch - 1) + step - 1, peers[step - 1])
            copy.start()
            across.append(copy)

    if share < sent.shape[1]:
        sent[...] = jnp.zeros_like(sent)
    for c in range(chunks):
        send_taps(c)
        if c > 0:
            join_taps(c - 1)
    for copy in shared:
        copy.wait()
    keep.wait()
    side = partner.at[pl.ds(core * half, half)]
    handed = remote(side, side, (mate_send, mate_recv), half - 1, {"ctx": me + 1 - 2 * core})
    handed.start()
    join_taps(chunks - 1)
    handed.wait()
    g = partner[...].reshape(taps, channels)
    behind[...] = mm(anti_hi[...], g) + mm(anti_lo[...], g)
    both[...] = ahead[...] + behind[...]
    filtering(0)
    for c in range(chunks):
        send_mirrored(c)
    for c in range(1, chunks):
        filtering(c)
    own = joined[0, chip].astype(F32) + sum(arrived[step, 0].astype(F32) for step in range(chips - 1))
    for condition, copy in send_waits:
        pl.when(condition)(copy.wait_send)
    for _, from_last, from_first in forwards:
        pl.when(me == ctx - 1)(from_last.wait_send)
        pl.when(me == 0)(from_first.wait_send)
    for copy in across:
        copy.wait()
    grad[...] = own + pick_partners(complement[...].reshape(1, channels), sent, ch, channels)[:share]


def entry_kernel(ctx, ch, groups, block, relay, count, lens, complement, *refs):
    given, results, held, fetch = refs[:count], refs[count : count + 5], refs[count + 5 : 2 * count + 5], refs[2 * count + 5]
    fetches = [pltpu.make_async_copy(given[i], held[i], fetch.at[i]) for i in range(count)]
    mixer_kernel(
        ctx, ch, groups, block, relay, fetches,
        lens, *held[:5], complement, *held[5:], *results, *refs[2 * count + 6 :],
    )


def channel_block(channels):
    for block in (384, 256, 128):
        if channels % block == 0:
            return block
    return channels


def hand_over_kernel(*refs):
    count = len(refs) // 2
    copies = [pltpu.make_async_copy(refs[i], refs[count + i], refs[-1].at[i]) for i in range(count)]
    for copy in copies:
        copy.start()
    for copy in copies:
        copy.wait()


def hand_over(*arrays):
    hbm = pl.BlockSpec(memory_space=pl.ANY)
    return pl.pallas_call(
        hand_over_kernel,
        in_specs=[pl.BlockSpec(memory_space=pltpu.VMEM)] * len(arrays),
        out_specs=[hbm] * len(arrays),
        out_shape=[jax.ShapeDtypeStruct(a.shape, a.dtype) for a in arrays],
        scratch_shapes=[pltpu.SemaphoreType.DMA((len(arrays),))],
        name="hand_over",
    )(*[pltpu.with_memory_space_constraint(a, pltpu.VMEM) for a in arrays])


def needs_relay(mesh):
    axis = mesh.axis_names.index("ctx")
    line = np.moveaxis(mesh.devices, axis, 0).reshape(mesh.shape["ctx"], -1)[:, 0]
    places = [getattr(device, "coords", None) for device in line]
    if any(place is None for place in places) or len(places) < 4:
        return False
    hops = lambda a, b: sum(abs(x - y) for x, y in zip(places[a], places[b]))
    middle, end = len(places) // 2 - 1, len(places) - 1
    return (
        hops(middle, middle + 1) == 2
        and hops(middle, end) == hops(end, middle + 1) == 1
        and hops(middle + 1, 0) == hops(0, middle) == 1
    )


def shards(relay, query_input, key_input, value_input, filters, complement, doc_lengths, cotangent):
    rows, channels = query_input.shape
    taps = filters.shape[1]
    ctx, ch = lax.axis_size("ctx"), lax.axis_size("ch")
    groups = min(ctx, taps // TILE)
    height, share, size = taps // groups, taps // ctx, 2 * rows
    block = channel_block(channels)
    chunks = channels // block
    slots = PACK - 1 + -(-doc_lengths.shape[0] // PACK)
    tables = [jnp.asarray(table) for table in fourier_tables(rows, taps)]
    fetched = [query_input, key_input, value_input, cotangent, filters, *tables]
    hbm = pl.BlockSpec(memory_space=pl.ANY)
    vmem = pl.BlockSpec(memory_space=pltpu.VMEM)
    dma = pltpu.SemaphoreType.DMA
    *mixed, grad_filter = pl.pallas_call(
        functools.partial(entry_kernel, ctx, ch, groups, block, relay, len(fetched)),
        in_specs=[pl.BlockSpec(memory_space=pltpu.SMEM), vmem] + [hbm] * len(fetched),
        out_specs=[vmem] * 5,
        out_shape=[pltpu.VMEM((rows, channels), BF16)] * 4 + [pltpu.VMEM((share, channels), F32)],
        scratch_shapes=[pltpu.VMEM(a.shape, a.dtype) for a in fetched]
        + [
            dma((len(fetched),)),
            pltpu.VMEM((rows, channels), BF16),
            pltpu.VMEM((rows, channels), BF16),
            pltpu.VMEM((4, rows, channels), BF16),
            pltpu.VMEM((2, rows, channels), BF16),
            pltpu.VMEM((ch, height, channels), BF16),
            pltpu.VMEM((height, channels), BF16),
            pltpu.VMEM((groups, height, channels), BF16),
            pltpu.VMEM((2, 2, ctx // 2, share, channels), BF16),
            pltpu.VMEM((2, ctx // 2, share, channels), BF16),
            pltpu.VMEM((2, ctx // 2, share, channels), BF16),
            pltpu.VMEM((ctx // 2 - 1, 2, share, channels), BF16),
            pltpu.VMEM((ch, -(-share // TILE) * TILE, channels), BF16),
            pltpu.VMEM((slots, size, rows), BF16),
            pltpu.VMEM((rows, (slots + 2) * size), BF16),
            pltpu.VMEM((2, size, rows), BF16),
            pltpu.VMEM((2, size, rows), BF16),
            pltpu.VMEM((2 * size, channels), F32),
            pltpu.VMEM((2 * size, channels), F32),
            pltpu.VMEM((2 * size, channels), F32),
            pltpu.VMEM((slots, size, channels), F32),
            pltpu.VMEM((slots, size, channels), F32),
            pltpu.VMEM((2, 2, size, channels), F32),
            pltpu.VMEM((2, size, channels), F32),
            pltpu.VMEM((2, size, channels), F32),
            pltpu.VMEM(((slots + 2) * size, block), BF16),
            pltpu.VMEM(((slots + 2) * size, block), BF16),
            pltpu.VMEM((2, taps, channels), F32),
            dma((4 * chunks,)), dma((4 * chunks,)), dma((2 * chunks,)), dma((2 * chunks,)), dma((ch - 1,)), dma((ch - 1,)),
            dma((groups // 2,)), dma((groups // 2,)),
            dma((chunks,)), dma((chunks,)),
            dma(((ctx // 2 - 1) * chunks,)), dma(((ctx // 2 - 1) * chunks,)), dma(((ch - 1) * chunks,)), dma(((ch - 1) * chunks,)), dma((1,)),
        ],
        compiler_params=pltpu.CompilerParams(
            collective_id=0, has_side_effects=True, vmem_limit_bytes=VMEM_BYTES
        ),
        name="mixer",
    )(doc_lengths, complement, *fetched)
    *mixed, grad_filter = hand_over(*mixed, grad_filter)
    return (*mixed, grad_filter.T)


def solution(mesh):
    placed = (
        P("ctx", "ch"),
        P("ctx", "ch"),
        P("ctx", "ch"),
        P("ch", None),
        P("ch"),
        P(),
        P("ctx", "ch"),
    )
    return jax.shard_map(
        functools.partial(shards, needs_relay(mesh)),
        mesh=mesh,
        in_specs=placed,
        out_specs=(P("ctx", "ch"), P("ctx", "ch"), P("ctx", "ch"), P("ctx", "ch"), P("ch", "ctx")),
        check_vma=False,
    )
```

```python
import functools

import jax
import jax.numpy as jnp
import numpy as np
from jax import lax
from jax.experimental import pallas as pl
from jax.experimental.pallas import tpu as pltpu
from jax.sharding import PartitionSpec as P

F32, BF16 = jnp.float32, jnp.bfloat16
LANES, TILE, PACK = 128, 16, 4
VMEM_BYTES = 56 * 2**20


def split_bf16(table):
    high = table.astype(BF16)
    low = (table - high.astype(np.float64)).astype(BF16)
    return high, low


def wave(places, length):
    angle = 2.0 * np.pi * (np.arange(length // 2) + 0.5) / length
    turns = angle[:, None] * np.asarray(places)[None, :]
    return np.cos(turns), np.sin(turns)


def fourier_tables(rows, taps):
    long, short = 2 * rows, 2 * rows // PACK
    cos, sin = wave(np.arange(3 * rows) - rows, long)
    analyse = np.concatenate([cos, -sin], axis=0)
    cos_s, sin_s = wave(np.arange(rows), short)
    pack = lambda table: np.tile(table, (PACK, 1))
    analyse_short = np.concatenate([pack(cos_s), pack(-sin_s)], axis=0)
    near = (np.arange(taps) < short // 2)[None, :]
    lag_cos, lag_sin = wave(np.arange(taps), long)
    near_cos, near_sin = [pack(table * near) for table in wave(np.arange(taps), short)]
    causal = np.concatenate([lag_cos, -lag_sin, near_cos, -near_sin], axis=0)
    anti = np.concatenate([lag_cos, lag_sin, near_cos, near_sin], axis=0)
    forward = causal.T.copy()
    backward = anti.T.copy()
    for table in (forward, backward):
        table[:, : 2 * rows] *= 2.0 / long
        table[:, 2 * rows :] *= 2.0 / short
    rebuild = analyse[:, rows : 2 * rows].T * (2.0 / long)
    rebuild_short = analyse_short.T * (2.0 / short)
    return (
        analyse.astype(BF16),
        analyse_short.astype(BF16),
        rebuild.astype(BF16),
        rebuild_short.astype(BF16),
        *split_bf16(causal),
        *split_bf16(anti),
        *split_bf16(forward),
        *split_bf16(backward),
    )


def mm(a, b):
    return jnp.dot(a, b, preferred_element_type=F32)


def mm_t(a, b):
    return lax.dot_general(a, b, (((1,), (1,)), ((), ())), preferred_element_type=F32)


def mm_fine(hi, lo, x):
    x_hi = x.astype(BF16)
    x_lo = (x - x_hi.astype(F32)).astype(BF16)
    return mm(hi, x_hi) + mm(hi, x_lo) + mm(lo, x_hi)


def product_of(a, b):
    return (a.astype(F32) * b.astype(F32)).astype(BF16)


def flag(mask):
    return mask.astype(F32).astype(BF16)


def times(a, x):
    half = a.shape[0] // 2
    a_re, a_im, x_re, x_im = a[:half], a[half:], x[:half], x[half:]
    return a_re * x_re - a_im * x_im, a_re * x_im + a_im * x_re


def times_conj(a, x):
    half = a.shape[0] // 2
    a_re, a_im, x_re, x_im = a[:half], a[half:], x[:half], x[half:]
    return a_re * x_re + a_im * x_im, a_re * x_im - a_im * x_re


def remote(src, dst, sems, index, device):
    return pltpu.make_async_remote_copy(
        src_ref=src, dst_ref=dst, send_sem=sems[0].at[index], recv_sem=sems[1].at[index],
        device_id=device, device_id_type=pl.DeviceIdType.MESH,
    )


def announce(devices):
    barrier = pltpu.get_barrier_semaphore()
    for device in devices:
        pl.semaphore_signal(barrier, inc=1, device_id=device, device_id_type=pl.DeviceIdType.MESH)


def gathered_in(devices):
    pl.semaphore_wait(pltpu.get_barrier_semaphore(), len(devices))


def partner_places(complement, ch, channels):
    mine = lax.axis_index("ch")
    owner = sum((complement >= k * channels).astype(jnp.int32) for k in range(1, ch)) + jnp.zeros_like(complement)
    step = mine - owner
    step = jnp.where(step < 0, step + ch, step)
    local = complement - owner * channels
    block = step * (channels // LANES) + lax.shift_right_logical(local, 7)
    return block, lax.bitwise_and(local, LANES - 1)


def pick_partners(block, chosen, landed, first, last):
    ch, height, channels = landed.shape
    places = [(s, b) for s in range(ch) for b in range(first, last)]
    stacked = jnp.concatenate([landed[s, :, b * LANES : (b + 1) * LANES] for s, b in places], axis=0)
    spread_out = mm(stacked, chosen[...])
    total = jnp.zeros((height, channels), F32)
    for i, (s, b) in enumerate(places):
        wanted = block == s * (channels // LANES) + b
        total = total + jnp.where(wanted, spread_out[i * height : (i + 1) * height], 0.0)
    return total


def survey(lens, rows, first_place):
    limit = rows // PACK
    lane3 = lax.broadcasted_iota(jnp.int32, (1, 3 * rows), 1) - rows
    lane = lax.broadcasted_iota(jnp.int32, (1, rows), 1)
    column = lax.broadcasted_iota(jnp.int32, (rows, 1), 0)
    low = -first_place
    found, base, last = jnp.int32(0), jnp.int32(0), jnp.int32(0)
    seen = jnp.zeros_like(lane3)
    seen_column = jnp.zeros_like(column)
    long_lane, short_lane = jnp.zeros_like(lane), jnp.zeros_like(lane)
    long_column, short_column = jnp.zeros_like(column), jnp.zeros_like(column)
    for d in range(lens.shape[0]):
        high = low + lens[d]
        own = jnp.minimum(high, rows) - jnp.maximum(low, 0)
        is_long = jnp.where(own > limit, 1, 0)
        found = found + is_long
        long_code = is_long * found
        short_code = (1 - is_long) * (d + 1)
        inside = (lane >= low) & (lane < high)
        long_lane = jnp.where(inside, long_code, long_lane)
        short_lane = jnp.where(inside, short_code, short_lane)
        inside = (column >= low) & (column < high)
        long_column = jnp.where(inside, long_code, long_column)
        short_column = jnp.where(inside, short_code, short_column)
        seen = seen + jnp.where(lane3 >= low, 1, 0)
        seen_column = seen_column + jnp.where(column >= low, 1, 0)
        base = base + jnp.where(low <= 0, 1, 0)
        last = last + jnp.where(low <= rows - 1, 1, 0)
        low = high
    seen = seen + jnp.where(lane3 >= low, 1, 0)
    return long_lane, short_lane, long_column, short_column, seen, seen_column, base, last


def mixer_kernel(
    ctx, ch, groups, widths, relay, fetches,
    lens, query, key, value, cot, filters, complement,
    analyse, analyse_short, rebuild, rebuild_short,
    causal_hi, causal_lo, anti_hi, anti_lo, fwd_hi, fwd_lo, bwd_hi, bwd_lo,
    mixer_out, grad_query, grad_key, grad_value, grad,
    u, r, halos, via, landed, picked, chosen, partner, pieces, twins, joined, arrived, sent,
    masked, back, outer, own_ends,
    ahead, behind, both, u_hat, o_hat, far_hat, ends_hat, acc_g, z_ref, q_ref, acc_t,
    halo_send, halo_recv, via_send, via_recv, ch_send, ch_recv, mate_send, mate_recv,
    twin_send, twin_recv, sum_send, sum_recv, back_send, back_recv, local,
):
    me, mine = lax.axis_index("ctx"), lax.axis_index("ch")
    rows, channels = query.shape
    taps = filters.shape[1]
    size = 2 * rows
    chunks = len(widths)
    offsets = [sum(widths[:c]) for c in range(chunks)]
    spans = [pl.ds(offset, width) for offset, width in zip(offsets, widths)]
    slots = masked.shape[0]
    longs = PACK - 1
    after, before = {"ctx": (me + 1) % ctx}, {"ctx": (me + ctx - 1) % ctx}
    core, half = me % 2, groups // 2
    spot, octet = (me % groups) // 2, me - me % groups
    group = core * half + spot
    height = taps // groups
    share = grad.shape[0]
    others = [{"ctx": (me + step) % ctx} for step in range(1, ctx)]
    peers = [{"ch": (mine + step) % ch} for step in range(1, ch)]
    mates = [{"ctx": octet + 2 * ((spot + step) % half) + core} for step in range(1, half)]
    announce(others + peers)
    for copy in fetches:
        copy.start()
    for copy in fetches[:5]:
        copy.wait()

    row = lax.broadcasted_iota(jnp.int32, (height, taps), 0)
    tap = lax.broadcasted_iota(jnp.int32, (height, taps), 1)
    landed[0] = mm_t(flag(tap == row + group * height), filters[...]).astype(BF16)

    def fields(c):
        lanes = spans[c]
        u[:, lanes] = product_of(key[:, lanes], value[:, lanes])
        r[:, lanes] = product_of(cot[:, lanes], query[:, lanes])

    fields(0)

    gathered_in(others + peers)
    along = [
        remote(landed.at[0], landed.at[step], (ch_send, ch_recv), step - 1, peers[step - 1])
        for step in range(1, ch)
    ]
    for copy in along[::-1]:
        copy.start()
    has_next, has_prev = me < ctx - 1, me > 0
    middle = ctx // 2 - 1
    at_middle = (me == middle) | (me == middle + 1)
    end = jnp.where(me == middle, ctx - 1, 0)
    starts, send_waits, recv_waits, forwards = [], [], [], []
    for c in range(chunks):
        lanes = spans[c]
        for kind, field in enumerate((u, r)):
            index = c * 2 + kind
            detour = relay and kind == 1
            to_next = remote(field.at[:, lanes], halos.at[kind, :, lanes],
                             (halo_send, halo_recv), c * 4 + kind, after)
            to_prev = remote(field.at[:, lanes], halos.at[2 + kind, :, lanes],
                             (halo_send, halo_recv), c * 4 + 2 + kind, before)
            starts.append([(has_next & (me != middle) if detour else has_next, to_next),
                           (has_prev & (me != middle + 1) if detour else has_prev, to_prev)])
            send_waits += starts[-1]
            recv_waits.append([(has_prev, to_next), (has_next, to_prev)])
            if detour:
                away = remote(field.at[:, lanes], via.at[kind, :, lanes], (via_send, via_recv), index, {"ctx": end})
                starts[-1].append((at_middle, away))
                send_waits.append((at_middle, away))
                from_last = remote(via.at[kind, :, lanes], halos.at[kind, :, lanes],
                                   (halo_send, halo_recv), c * 4 + kind, {"ctx": middle + 1})
                from_first = remote(via.at[kind, :, lanes], halos.at[2 + kind, :, lanes],
                                    (halo_send, halo_recv), c * 4 + 2 + kind, {"ctx": middle})
                forwards.append((away, from_last, from_first))

    def start_halos(chunk):
        for condition, copy in starts[2 * chunk] + starts[2 * chunk + 1]:
            pl.when(condition)(copy.start)

    for chunk in range(chunks):
        if chunk > 0:
            fields(chunk)
        start_halos(chunk)

    @pl.when(jnp.logical_not(has_prev))
    def _():
        halos[0:2] = jnp.zeros((2, rows, channels), BF16)

    @pl.when(jnp.logical_not(has_next))
    def _():
        halos[2:4] = jnp.zeros((2, rows, channels), BF16)

    long_lane, short_lane, long_column, short_column, seen, seen_column, base, last = survey(
        lens, rows, me * rows
    )
    for copy in fetches[5:]:
        copy.wait()
    quarter = rows // PACK
    packed_row = (lax.broadcasted_iota(jnp.int32, (size, 1), 0) % rows) // quarter
    packed_lane = (lax.broadcasted_iota(jnp.int32, (1, size), 1) % rows) // quarter
    for s in range(slots):
        cols = pl.ds(s * size, size)
        if s < longs:
            masked[s] = analyse[:, rows : 2 * rows] * flag(long_lane == s + 1)
            back[:, cols] = rebuild[...] * flag(long_column == s + 1)
        else:
            first = (s - longs) * PACK + 1
            masked[s] = analyse_short[...] * flag(short_lane == first + packed_row)
            back[:, cols] = rebuild_short[...] * flag(short_column == first + packed_lane)
    for e, code in enumerate((base, last)):
        section = slice(2 * e * rows, (2 * e + 1) * rows)
        outer[e] = analyse[:, section] * flag(seen[:, section] == code)
        own_ends[e] = analyse[:, rows : 2 * rows] * flag(seen[:, rows : 2 * rows] == code)
        back[:, pl.ds((slots + e) * size, size)] = rebuild[...] * flag(seen_column == code)

    ahead[...] = mm_t(causal_hi[...], filters[...]) + mm_t(causal_lo[...], filters[...])

    def analysis(c):
        lanes = spans[c]
        u_own, r_own = u[:, lanes], r[:, lanes]
        for s in range(slots):
            u_now, o_now = mm(masked[s], u_own), mm(masked[s], r_own)
            u_hat[s, :, lanes] = u_now
            o_hat[s, :, lanes] = o_now
            g_re, g_im = times_conj(u_now, o_now)
            kind = 0 if s < longs else 1
            if s == 0 or s == longs:
                acc_g[kind, :rows, lanes] = g_re
                acc_g[kind, rows:, lanes] = g_im
            else:
                acc_g[kind, :rows, lanes] += g_re
                acc_g[kind, rows:, lanes] += g_im
        for e in range(2):
            ends_hat[e, :, lanes] = mm(own_ends[e], r_own)
        own = jnp.concatenate([acc_g[0, :, lanes], acc_g[1, :, lanes]], axis=0)
        acc_t[0, :, lanes] = mm_fine(fwd_hi[...], fwd_lo[...], own)
        acc_t[1, :, lanes] = mm_fine(bwd_hi[...], bwd_lo[...], own)

    for c in range(chunks):
        analysis(c)
    partner_block, within = partner_places(complement[...].reshape(1, channels), ch, channels)
    chosen[...] = flag(lax.broadcasted_iota(jnp.int32, (LANES, channels), 0) == within)

    for arriving, from_last, from_first in forwards:
        @pl.when(me == ctx - 1)
        def _():
            arriving.wait_recv()
            from_last.start()

        @pl.when(me == 0)
        def _():
            arriving.wait_recv()
            from_first.start()


    for copy in along:
        copy.wait()
    picked[...] = pick_partners(partner_block, chosen, landed, 0, channels // LANES).astype(BF16)
    shared = [
        remote(picked, partner.at[group], (mate_send, mate_recv), step - 1, mates[step - 1])
        for step in range(1, half)
    ]
    for copy in shared:
        copy.start()
    keep = pltpu.make_async_copy(picked, partner.at[group], local.at[0])
    keep.start()
    chip, chips = me // 2, ctx // 2
    swaps, sums = [], []

    def send_taps(c):
        lanes = spans[c]
        for condition, copy in recv_waits[2 * c] + recv_waits[2 * c + 1]:
            pl.when(condition)(copy.wait_recv)
        for e in range(2):
            u_far = mm(outer[e], halos[2 * e, :, lanes])
            far_hat[e, 0, :, lanes] = u_far
            far_hat[e, 1, :, lanes] = mm(outer[e], halos[2 * e + 1, :, lanes])
            g_re, g_im = times_conj(u_far, ends_hat[e, :, lanes])
            hi, lo = (fwd_hi, fwd_lo) if e == 0 else (bwd_hi, bwd_lo)
            far = jnp.concatenate([g_re, g_im], axis=0)
            tap_sums = acc_t[e, :, lanes] + mm_fine(hi[:, :size], lo[:, :size], far)
            for i in range(ctx):
                pieces[i % 2, e, i // 2, :, lanes] = tap_sums[i * share : (i + 1) * share].astype(BF16)
        copy = remote(pieces.at[1 - core, :, :, :, lanes], twins.at[:, :, :, lanes],
                      (twin_send, twin_recv), c, {"ctx": me + 1 - 2 * core})
        copy.start()
        swaps.append(copy)

    def join_taps(c):
        lanes = spans[c]
        swaps[c].wait()
        joined[:, :, :, lanes] = (
            pieces[core, :, :, :, lanes].astype(F32) + twins[:, :, :, lanes].astype(F32)
        ).astype(BF16)
        for step in range(1, chips):
            copy = remote(joined.at[:, (chip + step) % chips, :, lanes], arrived.at[step - 1, :, :, lanes],
                          (sum_send, sum_recv), c * (chips - 1) + step - 1, {"ctx": (me + 2 * step) % ctx})
            copy.start()
            sums.append(copy)

    def filtering(c):
        lanes, width = spans[c], widths[c]

        def keep_products(s, z, q):
            z_ref[s * size : s * size + rows, :width] = z[0].astype(BF16)
            z_ref[s * size + rows : (s + 1) * size, :width] = z[1].astype(BF16)
            q_ref[s * size : s * size + rows, :width] = q[0].astype(BF16)
            q_ref[s * size + rows : (s + 1) * size, :width] = q[1].astype(BF16)

        for s in range(slots):
            kind = 0 if s < longs else 1
            h = both[kind * size : (kind + 1) * size, lanes]
            keep_products(s, times(h, u_hat[s, :, lanes]), times_conj(h, o_hat[s, :, lanes]))
        for e in range(2):
            for_u, for_r = (ahead, behind) if e == 0 else (behind, ahead)
            keep_products(
                slots + e,
                times(for_u[:size, lanes], far_hat[e, 0, :, lanes]),
                times_conj(for_r[:size, lanes], far_hat[e, 1, :, lanes]),
            )
        combined = mm(back[...], z_ref[:, :width])
        grad_product = mm(back[...], q_ref[:, :width])
        mixer_out[:, lanes] = (query[:, lanes].astype(F32) * combined).astype(BF16)
        grad_query[:, lanes] = (cot[:, lanes].astype(F32) * combined).astype(BF16)
        grad_key[:, lanes] = (grad_product * value[:, lanes].astype(F32)).astype(BF16)
        grad_value[:, lanes] = (grad_product * key[:, lanes].astype(F32)).astype(BF16)

    across = []

    def send_mirrored(c):
        lanes = spans[c]
        for copy in sums[c * (chips - 1) : (c + 1) * (chips - 1)]:
            copy.wait()
        total = sum(arrived[step, 1, :, lanes].astype(F32) for step in range(chips - 1))
        sent[0, :share, lanes] = (total + joined[1, chip, :, lanes].astype(F32)).astype(BF16)
        for step in range(1, ch):
            copy = remote(sent.at[0, :, lanes], sent.at[step, :, lanes],
                          (back_send, back_recv), c * (ch - 1) + step - 1, peers[step - 1])
            copy.start()
            across.append(copy)

    if share < sent.shape[1]:
        sent[...] = jnp.zeros_like(sent)
    for c in range(chunks):
        send_taps(c)
        if c > 0:
            join_taps(c - 1)
    for copy in shared:
        copy.wait()
    keep.wait()
    side = partner.at[pl.ds(core * half, half)]
    handed = remote(side, side, (mate_send, mate_recv), half - 1, {"ctx": me + 1 - 2 * core})
    handed.start()
    join_taps(chunks - 1)
    handed.wait()
    g = partner[...].reshape(taps, channels)
    behind[...] = mm(anti_hi[...], g) + mm(anti_lo[...], g)
    both[...] = ahead[...] + behind[...]
    filtering(0)
    for c in range(chunks):
        send_mirrored(c)
    for c in range(1, chunks):
        filtering(c)
    own = joined[0, chip].astype(F32) + sum(arrived[step, 0].astype(F32) for step in range(chips - 1))
    for condition, copy in send_waits:
        pl.when(condition)(copy.wait_send)
    for _, from_last, from_first in forwards:
        pl.when(me == ctx - 1)(from_last.wait_send)
        pl.when(me == 0)(from_first.wait_send)
    for c in range(chunks):
        for copy in across[c * (ch - 1) : (c + 1) * (ch - 1)]:
            copy.wait()
        first = offsets[c] // LANES
        last = first + widths[c] // LANES
        own = own + pick_partners(partner_block, chosen, sent, first, last)[:share]
    grad[...] = own


def entry_kernel(ctx, ch, groups, widths, relay, count, lens, complement, *refs):
    given, results, held, fetch = refs[:count], refs[count : count + 5], refs[count + 5 : 2 * count + 5], refs[2 * count + 5]
    fetches = [pltpu.make_async_copy(given[i], held[i], fetch.at[i]) for i in range(count)]
    mixer_kernel(
        ctx, ch, groups, widths, relay, fetches,
        lens, *held[:5], complement, *held[5:], *results, *refs[2 * count + 6 :],
    )


def channel_widths(channels):
    tiles = channels // LANES
    if tiles < 4 or channels % LANES:
        return (channels,)
    first = tiles // 2
    return (first * LANES, (tiles - 2 - first) * LANES, 2 * LANES)


def hand_over_kernel(*refs):
    count = len(refs) // 2
    copies = [pltpu.make_async_copy(refs[i], refs[count + i], refs[-1].at[i]) for i in range(count)]
    for copy in copies:
        copy.start()
    for copy in copies:
        copy.wait()


def hand_over(*arrays):
    hbm = pl.BlockSpec(memory_space=pl.ANY)
    return pl.pallas_call(
        hand_over_kernel,
        in_specs=[pl.BlockSpec(memory_space=pltpu.VMEM)] * len(arrays),
        out_specs=[hbm] * len(arrays),
        out_shape=[jax.ShapeDtypeStruct(a.shape, a.dtype) for a in arrays],
        scratch_shapes=[pltpu.SemaphoreType.DMA((len(arrays),))],
        name="hand_over",
    )(*[pltpu.with_memory_space_constraint(a, pltpu.VMEM) for a in arrays])


def needs_relay(mesh):
    axis = mesh.axis_names.index("ctx")
    line = np.moveaxis(mesh.devices, axis, 0).reshape(mesh.shape["ctx"], -1)[:, 0]
    places = [getattr(device, "coords", None) for device in line]
    if any(place is None for place in places) or len(places) < 4:
        return False
    hops = lambda a, b: sum(abs(x - y) for x, y in zip(places[a], places[b]))
    middle, end = len(places) // 2 - 1, len(places) - 1
    return (
        hops(middle, middle + 1) == 2
        and hops(middle, end) == hops(end, middle + 1) == 1
        and hops(middle + 1, 0) == hops(0, middle) == 1
    )


def shards(relay, query_input, key_input, value_input, filters, complement, doc_lengths, cotangent):
    rows, channels = query_input.shape
    taps = filters.shape[1]
    ctx, ch = lax.axis_size("ctx"), lax.axis_size("ch")
    groups = min(ctx, taps // TILE)
    height, share, size = taps // groups, taps // ctx, 2 * rows
    widths = channel_widths(channels)
    chunks, block = len(widths), max(widths)
    slots = PACK - 1 + -(-doc_lengths.shape[0] // PACK)
    tables = [jnp.asarray(table) for table in fourier_tables(rows, taps)]
    fetched = [query_input, key_input, value_input, cotangent, filters, *tables]
    hbm = pl.BlockSpec(memory_space=pl.ANY)
    vmem = pl.BlockSpec(memory_space=pltpu.VMEM)
    dma = pltpu.SemaphoreType.DMA
    *mixed, grad_filter = pl.pallas_call(
        functools.partial(entry_kernel, ctx, ch, groups, widths, relay, len(fetched)),
        in_specs=[pl.BlockSpec(memory_space=pltpu.SMEM), vmem] + [hbm] * len(fetched),
        out_specs=[vmem] * 5,
        out_shape=[pltpu.VMEM((rows, channels), BF16)] * 4 + [pltpu.VMEM((share, channels), F32)],
        scratch_shapes=[pltpu.VMEM(a.shape, a.dtype) for a in fetched]
        + [
            dma((len(fetched),)),
            pltpu.VMEM((rows, channels), BF16),
            pltpu.VMEM((rows, channels), BF16),
            pltpu.VMEM((4, rows, channels), BF16),
            pltpu.VMEM((2, rows, channels), BF16),
            pltpu.VMEM((ch, height, channels), BF16),
            pltpu.VMEM((height, channels), BF16),
            pltpu.VMEM((LANES, channels), BF16),
            pltpu.VMEM((groups, height, channels), BF16),
            pltpu.VMEM((2, 2, ctx // 2, share, channels), BF16),
            pltpu.VMEM((2, ctx // 2, share, channels), BF16),
            pltpu.VMEM((2, ctx // 2, share, channels), BF16),
            pltpu.VMEM((ctx // 2 - 1, 2, share, channels), BF16),
            pltpu.VMEM((ch, -(-share // TILE) * TILE, channels), BF16),
            pltpu.VMEM((slots, size, rows), BF16),
            pltpu.VMEM((rows, (slots + 2) * size), BF16),
            pltpu.VMEM((2, size, rows), BF16),
            pltpu.VMEM((2, size, rows), BF16),
            pltpu.VMEM((2 * size, channels), F32),
            pltpu.VMEM((2 * size, channels), F32),
            pltpu.VMEM((2 * size, channels), F32),
            pltpu.VMEM((slots, size, channels), F32),
            pltpu.VMEM((slots, size, channels), F32),
            pltpu.VMEM((2, 2, size, channels), F32),
            pltpu.VMEM((2, size, channels), F32),
            pltpu.VMEM((2, size, channels), F32),
            pltpu.VMEM(((slots + 2) * size, block), BF16),
            pltpu.VMEM(((slots + 2) * size, block), BF16),
            pltpu.VMEM((2, taps, channels), F32),
            dma((4 * chunks,)), dma((4 * chunks,)), dma((2 * chunks,)), dma((2 * chunks,)), dma((ch - 1,)), dma((ch - 1,)),
            dma((groups // 2,)), dma((groups // 2,)),
            dma((chunks,)), dma((chunks,)),
            dma(((ctx // 2 - 1) * chunks,)), dma(((ctx // 2 - 1) * chunks,)), dma(((ch - 1) * chunks,)), dma(((ch - 1) * chunks,)), dma((1,)),
        ],
        compiler_params=pltpu.CompilerParams(
            collective_id=0, has_side_effects=True, vmem_limit_bytes=VMEM_BYTES
        ),
        name="mixer",
    )(doc_lengths, complement, *fetched)
    *mixed, grad_filter = hand_over(*mixed, grad_filter)
    return (*mixed, grad_filter.T)


def solution(mesh):
    placed = (
        P("ctx", "ch"),
        P("ctx", "ch"),
        P("ctx", "ch"),
        P("ch", None),
        P("ch"),
        P(),
        P("ctx", "ch"),
    )
    return jax.shard_map(
        functools.partial(shards, needs_relay(mesh)),
        mesh=mesh,
        in_specs=placed,
        out_specs=(P("ctx", "ch"), P("ctx", "ch"), P("ctx", "ch"), P("ctx", "ch"), P("ch", "ctx")),
        check_vma=False,
    )
```

```python
import functools

import jax
import jax.numpy as jnp
import numpy as np
from jax import lax
from jax.experimental import pallas as pl
from jax.experimental.pallas import tpu as pltpu
from jax.sharding import PartitionSpec as P

F32, BF16 = jnp.float32, jnp.bfloat16
LANES, TILE, PACK = 128, 16, 4
VMEM_BYTES = 56 * 2**20


def split_bf16(table):
    high = table.astype(BF16)
    low = (table - high.astype(np.float64)).astype(BF16)
    return high, low


def wave(places, length):
    angle = 2.0 * np.pi * (np.arange(length // 2) + 0.5) / length
    turns = angle[:, None] * np.asarray(places)[None, :]
    return np.cos(turns), np.sin(turns)


def fourier_tables(rows, taps):
    long, short = 2 * rows, 2 * rows // PACK
    cos, sin = wave(np.arange(3 * rows) - rows, long)
    analyse = np.concatenate([cos, -sin], axis=0)
    cos_s, sin_s = wave(np.arange(rows), short)
    pack = lambda table: np.tile(table, (PACK, 1))
    analyse_short = np.concatenate([pack(cos_s), pack(-sin_s)], axis=0)
    near = (np.arange(taps) < short // 2)[None, :]
    lag_cos, lag_sin = wave(np.arange(taps), long)
    near_cos, near_sin = [pack(table * near) for table in wave(np.arange(taps), short)]
    causal = np.concatenate([lag_cos, -lag_sin, near_cos, -near_sin], axis=0)
    anti = np.concatenate([lag_cos, lag_sin, near_cos, near_sin], axis=0)
    forward = causal.T.copy()
    backward = anti.T.copy()
    for table in (forward, backward):
        table[:, : 2 * rows] *= 2.0 / long
        table[:, 2 * rows :] *= 2.0 / short
    rebuild = analyse[:, rows : 2 * rows].T * (2.0 / long)
    rebuild_short = analyse_short.T * (2.0 / short)
    return (
        analyse.astype(BF16),
        analyse_short.astype(BF16),
        rebuild.astype(BF16),
        rebuild_short.astype(BF16),
        *split_bf16(causal),
        *split_bf16(anti),
        *split_bf16(forward),
        *split_bf16(backward),
    )


def mm(a, b):
    return jnp.dot(a, b, preferred_element_type=F32)


def mm_t(a, b):
    return lax.dot_general(a, b, (((1,), (1,)), ((), ())), preferred_element_type=F32)


def mm_fine(hi, lo, x):
    x_hi = x.astype(BF16)
    x_lo = (x - x_hi.astype(F32)).astype(BF16)
    return mm(hi, x_hi) + mm(hi, x_lo) + mm(lo, x_hi)


def product_of(a, b):
    return (a.astype(F32) * b.astype(F32)).astype(BF16)


def flag(mask):
    return mask.astype(F32).astype(BF16)


def times(a, x):
    half = a.shape[0] // 2
    a_re, a_im, x_re, x_im = a[:half], a[half:], x[:half], x[half:]
    return a_re * x_re - a_im * x_im, a_re * x_im + a_im * x_re


def times_conj(a, x):
    half = a.shape[0] // 2
    a_re, a_im, x_re, x_im = a[:half], a[half:], x[:half], x[half:]
    return a_re * x_re + a_im * x_im, a_re * x_im - a_im * x_re


def remote(src, dst, sems, index, device):
    return pltpu.make_async_remote_copy(
        src_ref=src, dst_ref=dst, send_sem=sems[0].at[index], recv_sem=sems[1].at[index],
        device_id=device, device_id_type=pl.DeviceIdType.MESH,
    )


def announce(devices):
    barrier = pltpu.get_barrier_semaphore()
    for device in devices:
        pl.semaphore_signal(barrier, inc=1, device_id=device, device_id_type=pl.DeviceIdType.MESH)


def gathered_in(devices):
    pl.semaphore_wait(pltpu.get_barrier_semaphore(), len(devices))


def partner_places(complement, ch, channels):
    mine = lax.axis_index("ch")
    owner = sum((complement >= k * channels).astype(jnp.int32) for k in range(1, ch)) + jnp.zeros_like(complement)
    step = mine - owner
    step = jnp.where(step < 0, step + ch, step)
    local = complement - owner * channels
    block = step * (channels // LANES) + lax.shift_right_logical(local, 7)
    return block, lax.bitwise_and(local, LANES - 1)


def pick_partners(block, chosen, landed, first, last):
    ch, height, channels = landed.shape
    places = [(s, b) for s in range(ch) for b in range(first, last)]
    stacked = jnp.concatenate([landed[s, :, b * LANES : (b + 1) * LANES] for s, b in places], axis=0)
    spread_out = mm(stacked, chosen[...])
    total = jnp.zeros((height, channels), F32)
    for i, (s, b) in enumerate(places):
        wanted = block == s * (channels // LANES) + b
        total = total + jnp.where(wanted, spread_out[i * height : (i + 1) * height], 0.0)
    return total


def survey(lens, rows, first_place):
    limit = rows // PACK
    lane3 = lax.broadcasted_iota(jnp.int32, (1, 3 * rows), 1) - rows
    lane = lax.broadcasted_iota(jnp.int32, (1, rows), 1)
    column = lax.broadcasted_iota(jnp.int32, (rows, 1), 0)
    low = -first_place
    found, base, last = jnp.int32(0), jnp.int32(0), jnp.int32(0)
    seen = jnp.zeros_like(lane3)
    seen_column = jnp.zeros_like(column)
    long_lane, short_lane = jnp.zeros_like(lane), jnp.zeros_like(lane)
    long_column, short_column = jnp.zeros_like(column), jnp.zeros_like(column)
    for d in range(lens.shape[0]):
        high = low + lens[d]
        own = jnp.minimum(high, rows) - jnp.maximum(low, 0)
        is_long = jnp.where(own > limit, 1, 0)
        found = found + is_long
        long_code = is_long * found
        short_code = (1 - is_long) * (d + 1)
        inside = (lane >= low) & (lane < high)
        long_lane = jnp.where(inside, long_code, long_lane)
        short_lane = jnp.where(inside, short_code, short_lane)
        inside = (column >= low) & (column < high)
        long_column = jnp.where(inside, long_code, long_column)
        short_column = jnp.where(inside, short_code, short_column)
        seen = seen + jnp.where(lane3 >= low, 1, 0)
        seen_column = seen_column + jnp.where(column >= low, 1, 0)
        base = base + jnp.where(low <= 0, 1, 0)
        last = last + jnp.where(low <= rows - 1, 1, 0)
        low = high
    seen = seen + jnp.where(lane3 >= low, 1, 0)
    return long_lane, short_lane, long_column, short_column, seen, seen_column, base, last


def mixer_kernel(
    ctx, ch, groups, widths, relay, fetches,
    lens, query, key, value, cot, filters, complement,
    analyse, analyse_short, rebuild, rebuild_short,
    causal_hi, causal_lo, anti_hi, anti_lo, fwd_hi, fwd_lo, bwd_hi, bwd_lo,
    mixer_out, grad_query, grad_key, grad_value, grad,
    u, r, halos, via, landed, picked, chosen, partner, pieces, twins, joined, arrived, sent,
    masked, back, outer, own_ends,
    ahead, behind, both, u_hat, o_hat, far_hat, ends_hat, acc_g, z_ref, q_ref, acc_t,
    halo_send, halo_recv, via_send, via_recv, ch_send, ch_recv, mate_send, mate_recv,
    twin_send, twin_recv, sum_send, sum_recv, back_send, back_recv, local,
):
    me, mine = lax.axis_index("ctx"), lax.axis_index("ch")
    rows, channels = query.shape
    taps = filters.shape[1]
    size = 2 * rows
    chunks = len(widths)
    offsets = [sum(widths[:c]) for c in range(chunks)]
    spans = [pl.ds(offset, width) for offset, width in zip(offsets, widths)]
    slots = masked.shape[0]
    longs = PACK - 1
    after, before = {"ctx": (me + 1) % ctx}, {"ctx": (me + ctx - 1) % ctx}
    core, half = me % 2, groups // 2
    spot, octet = (me % groups) // 2, me - me % groups
    group = core * half + spot
    height = taps // groups
    share = grad.shape[0]
    others = [{"ctx": (me + step) % ctx} for step in range(1, ctx)]
    peers = [{"ch": (mine + step) % ch} for step in range(1, ch)]
    mates = [{"ctx": octet + 2 * ((spot + step) % half) + core} for step in range(1, half)]
    announce(others + peers)
    for copy in fetches:
        copy.start()
    for copy in fetches[:5]:
        copy.wait()

    row = lax.broadcasted_iota(jnp.int32, (height, taps), 0)
    tap = lax.broadcasted_iota(jnp.int32, (height, taps), 1)
    landed[0] = mm_t(flag(tap == row + group * height), filters[...]).astype(BF16)

    def fields(c):
        lanes = spans[c]
        u[:, lanes] = product_of(key[:, lanes], value[:, lanes])
        r[:, lanes] = product_of(cot[:, lanes], query[:, lanes])

    fields(0)

    gathered_in(others + peers)
    along = [
        remote(landed.at[0], landed.at[step], (ch_send, ch_recv), step - 1, peers[step - 1])
        for step in range(1, ch)
    ]
    for copy in along[::-1]:
        copy.start()
    has_next, has_prev = me < ctx - 1, me > 0
    middle = ctx // 2 - 1
    at_middle = (me == middle) | (me == middle + 1)
    end = jnp.where(me == middle, ctx - 1, 0)
    starts, send_waits, recv_waits, forwards = [], [], [], []
    for c in range(chunks):
        lanes = spans[c]
        for kind, field in enumerate((u, r)):
            index = c * 2 + kind
            detour = relay and kind == 1
            to_next = remote(field.at[:, lanes], halos.at[kind, :, lanes],
                             (halo_send, halo_recv), c * 4 + kind, after)
            to_prev = remote(field.at[:, lanes], halos.at[2 + kind, :, lanes],
                             (halo_send, halo_recv), c * 4 + 2 + kind, before)
            starts.append([(has_next & (me != middle) if detour else has_next, to_next),
                           (has_prev & (me != middle + 1) if detour else has_prev, to_prev)])
            send_waits += starts[-1]
            recv_waits.append([(has_prev, to_next), (has_next, to_prev)])
            if detour:
                away = remote(field.at[:, lanes], via.at[kind, :, lanes], (via_send, via_recv), index, {"ctx": end})
                starts[-1].append((at_middle, away))
                send_waits.append((at_middle, away))
                from_last = remote(via.at[kind, :, lanes], halos.at[kind, :, lanes],
                                   (halo_send, halo_recv), c * 4 + kind, {"ctx": middle + 1})
                from_first = remote(via.at[kind, :, lanes], halos.at[2 + kind, :, lanes],
                                    (halo_send, halo_recv), c * 4 + 2 + kind, {"ctx": middle})
                forwards.append((away, from_last, from_first))

    def start_halos(chunk):
        for condition, copy in starts[2 * chunk] + starts[2 * chunk + 1]:
            pl.when(condition)(copy.start)

    for chunk in range(chunks):
        if chunk > 0:
            fields(chunk)
        start_halos(chunk)

    @pl.when(jnp.logical_not(has_prev))
    def _():
        halos[0:2] = jnp.zeros((2, rows, channels), BF16)

    @pl.when(jnp.logical_not(has_next))
    def _():
        halos[2:4] = jnp.zeros((2, rows, channels), BF16)

    long_lane, short_lane, long_column, short_column, seen, seen_column, base, last = survey(
        lens, rows, me * rows
    )
    for copy in fetches[5:]:
        copy.wait()
    quarter = rows // PACK
    packed_row = (lax.broadcasted_iota(jnp.int32, (size, 1), 0) % rows) // quarter
    packed_lane = (lax.broadcasted_iota(jnp.int32, (1, size), 1) % rows) // quarter
    for s in range(slots):
        cols = pl.ds(s * size, size)
        if s < longs:
            masked[s] = analyse[:, rows : 2 * rows] * flag(long_lane == s + 1)
            back[:, cols] = rebuild[...] * flag(long_column == s + 1)
        else:
            first = (s - longs) * PACK + 1
            masked[s] = analyse_short[...] * flag(short_lane == first + packed_row)
            back[:, cols] = rebuild_short[...] * flag(short_column == first + packed_lane)
    for e, code in enumerate((base, last)):
        section = slice(2 * e * rows, (2 * e + 1) * rows)
        outer[e] = analyse[:, section] * flag(seen[:, section] == code)
        own_ends[e] = analyse[:, rows : 2 * rows] * flag(seen[:, rows : 2 * rows] == code)
        back[:, pl.ds((slots + e) * size, size)] = rebuild[...] * flag(seen_column == code)

    ahead[...] = mm_t(causal_hi[...], filters[...]) + mm_t(causal_lo[...], filters[...])

    def analysis(c):
        lanes = spans[c]
        u_own, r_own = u[:, lanes], r[:, lanes]
        for s in range(slots):
            u_now, o_now = mm(masked[s], u_own), mm(masked[s], r_own)
            u_hat[s, :, lanes] = u_now
            o_hat[s, :, lanes] = o_now
            g_re, g_im = times_conj(u_now, o_now)
            kind = 0 if s < longs else 1
            if s == 0 or s == longs:
                acc_g[kind, :rows, lanes] = g_re
                acc_g[kind, rows:, lanes] = g_im
            else:
                acc_g[kind, :rows, lanes] += g_re
                acc_g[kind, rows:, lanes] += g_im
        for e in range(2):
            ends_hat[e, :, lanes] = mm(own_ends[e], r_own)
        own = jnp.concatenate([acc_g[0, :, lanes], acc_g[1, :, lanes]], axis=0)
        acc_t[0, :, lanes] = mm_fine(fwd_hi[...], fwd_lo[...], own)
        acc_t[1, :, lanes] = mm_fine(bwd_hi[...], bwd_lo[...], own)

    for c in range(chunks):
        analysis(c)
    partner_block, within = partner_places(complement[...].reshape(1, channels), ch, channels)
    chosen[...] = flag(lax.broadcasted_iota(jnp.int32, (LANES, channels), 0) == within)

    for arriving, from_last, from_first in forwards:
        @pl.when(me == ctx - 1)
        def _():
            arriving.wait_recv()
            from_last.start()

        @pl.when(me == 0)
        def _():
            arriving.wait_recv()
            from_first.start()


    for copy in along:
        copy.wait()
    picked[...] = pick_partners(partner_block, chosen, landed, 0, channels // LANES).astype(BF16)
    shared = [
        remote(picked, partner.at[group], (mate_send, mate_recv), step - 1, mates[step - 1])
        for step in range(1, half)
    ]
    for copy in shared:
        copy.start()
    keep = pltpu.make_async_copy(picked, partner.at[group], local.at[0])
    keep.start()
    chip, chips = me // 2, ctx // 2
    swaps, sums = [], []

    def send_taps(c):
        lanes = spans[c]
        for condition, copy in recv_waits[2 * c] + recv_waits[2 * c + 1]:
            pl.when(condition)(copy.wait_recv)
        for e in range(2):
            u_far = mm(outer[e], halos[2 * e, :, lanes])
            far_hat[e, 0, :, lanes] = u_far
            far_hat[e, 1, :, lanes] = mm(outer[e], halos[2 * e + 1, :, lanes])
            g_re, g_im = times_conj(u_far, ends_hat[e, :, lanes])
            hi, lo = (fwd_hi, fwd_lo) if e == 0 else (bwd_hi, bwd_lo)
            far = jnp.concatenate([g_re, g_im], axis=0)
            tap_sums = acc_t[e, :, lanes] + mm_fine(hi[:, :size], lo[:, :size], far)
            for i in range(ctx):
                pieces[i % 2, e, i // 2, :, lanes] = tap_sums[i * share : (i + 1) * share].astype(BF16)
        copy = remote(pieces.at[1 - core, :, :, :, lanes], twins.at[:, :, :, lanes],
                      (twin_send, twin_recv), c, {"ctx": me + 1 - 2 * core})
        copy.start()
        swaps.append(copy)

    def join_taps(c):
        lanes = spans[c]
        swaps[c].wait()
        joined[:, :, :, lanes] = (
            pieces[core, :, :, :, lanes].astype(F32) + twins[:, :, :, lanes].astype(F32)
        ).astype(BF16)
        for step in range(1, chips):
            copy = remote(joined.at[:, (chip + step) % chips, :, lanes], arrived.at[step - 1, :, :, lanes],
                          (sum_send, sum_recv), c * (chips - 1) + step - 1, {"ctx": (me + 2 * step) % ctx})
            copy.start()
            sums.append(copy)

    def filtering(c):
        lanes, width = spans[c], widths[c]

        def keep_products(s, z, q):
            z_ref[s * size : s * size + rows, :width] = z[0].astype(BF16)
            z_ref[s * size + rows : (s + 1) * size, :width] = z[1].astype(BF16)
            q_ref[s * size : s * size + rows, :width] = q[0].astype(BF16)
            q_ref[s * size + rows : (s + 1) * size, :width] = q[1].astype(BF16)

        for s in range(slots):
            kind = 0 if s < longs else 1
            h = both[kind * size : (kind + 1) * size, lanes]
            keep_products(s, times(h, u_hat[s, :, lanes]), times_conj(h, o_hat[s, :, lanes]))
        for e in range(2):
            for_u, for_r = (ahead, behind) if e == 0 else (behind, ahead)
            keep_products(
                slots + e,
                times(for_u[:size, lanes], far_hat[e, 0, :, lanes]),
                times_conj(for_r[:size, lanes], far_hat[e, 1, :, lanes]),
            )
        combined = mm(back[...], z_ref[:, :width])
        grad_product = mm(back[...], q_ref[:, :width])
        mixer_out[:, lanes] = (query[:, lanes].astype(F32) * combined).astype(BF16)
        grad_query[:, lanes] = (cot[:, lanes].astype(F32) * combined).astype(BF16)
        grad_key[:, lanes] = (grad_product * value[:, lanes].astype(F32)).astype(BF16)
        grad_value[:, lanes] = (grad_product * key[:, lanes].astype(F32)).astype(BF16)

    across = []

    def send_mirrored(c):
        lanes = spans[c]
        for copy in sums[c * (chips - 1) : (c + 1) * (chips - 1)]:
            copy.wait()
        total = sum(arrived[step, 1, :, lanes].astype(F32) for step in range(chips - 1))
        sent[0, :share, lanes] = (total + joined[1, chip, :, lanes].astype(F32)).astype(BF16)
        for step in range(1, ch):
            copy = remote(sent.at[0, :, lanes], sent.at[step, :, lanes],
                          (back_send, back_recv), c * (ch - 1) + step - 1, peers[step - 1])
            copy.start()
            across.append(copy)

    if share < sent.shape[1]:
        sent[...] = jnp.zeros_like(sent)
    for c in range(chunks):
        send_taps(c)
        if 0 < c < chunks - 1:
            join_taps(c - 1)
    for copy in shared:
        copy.wait()
    keep.wait()
    side = partner.at[pl.ds(core * half, half)]
    handed = remote(side, side, (mate_send, mate_recv), half - 1, {"ctx": me + 1 - 2 * core})
    handed.start()
    for c in range(max(chunks - 2, 0), chunks):
        join_taps(c)
    handed.wait()
    g = partner[...].reshape(taps, channels)
    for offset, width, lanes in zip(offsets, widths, spans):
        g_now = g[:, offset : offset + width]
        now = mm(anti_hi[...], g_now) + mm(anti_lo[...], g_now)
        behind[:, lanes] = now
        both[:, lanes] = ahead[:, lanes] + now
    filtering(0)
    for c in range(chunks):
        send_mirrored(c)
    for c in range(1, chunks):
        filtering(c)
    own = joined[0, chip].astype(F32) + sum(arrived[step, 0].astype(F32) for step in range(chips - 1))
    for condition, copy in send_waits:
        pl.when(condition)(copy.wait_send)
    for _, from_last, from_first in forwards:
        pl.when(me == ctx - 1)(from_last.wait_send)
        pl.when(me == 0)(from_first.wait_send)
    for c in range(chunks):
        for copy in across[c * (ch - 1) : (c + 1) * (ch - 1)]:
            copy.wait()
        first = offsets[c] // LANES
        last = first + widths[c] // LANES
        own = own + pick_partners(partner_block, chosen, sent, first, last)[:share]
    grad[...] = own


def entry_kernel(ctx, ch, groups, widths, relay, count, lens, complement, *refs):
    given, results, held, fetch = refs[:count], refs[count : count + 5], refs[count + 5 : 2 * count + 5], refs[2 * count + 5]
    fetches = [pltpu.make_async_copy(given[i], held[i], fetch.at[i]) for i in range(count)]
    mixer_kernel(
        ctx, ch, groups, widths, relay, fetches,
        lens, *held[:5], complement, *held[5:], *results, *refs[2 * count + 6 :],
    )


def channel_widths(channels):
    tiles = channels // LANES
    if tiles < 4 or channels % LANES:
        return (channels,)
    first = tiles // 2
    return (first * LANES, (tiles - 2 - first) * LANES, 2 * LANES)


def hand_over_kernel(*refs):
    count = len(refs) // 2
    copies = [pltpu.make_async_copy(refs[i], refs[count + i], refs[-1].at[i]) for i in range(count)]
    for copy in copies:
        copy.start()
    for copy in copies:
        copy.wait()


def hand_over(*arrays):
    hbm = pl.BlockSpec(memory_space=pl.ANY)
    return pl.pallas_call(
        hand_over_kernel,
        in_specs=[pl.BlockSpec(memory_space=pltpu.VMEM)] * len(arrays),
        out_specs=[hbm] * len(arrays),
        out_shape=[jax.ShapeDtypeStruct(a.shape, a.dtype) for a in arrays],
        scratch_shapes=[pltpu.SemaphoreType.DMA((len(arrays),))],
        name="hand_over",
    )(*[pltpu.with_memory_space_constraint(a, pltpu.VMEM) for a in arrays])


def needs_relay(mesh):
    axis = mesh.axis_names.index("ctx")
    line = np.moveaxis(mesh.devices, axis, 0).reshape(mesh.shape["ctx"], -1)[:, 0]
    places = [getattr(device, "coords", None) for device in line]
    if any(place is None for place in places) or len(places) < 4:
        return False
    hops = lambda a, b: sum(abs(x - y) for x, y in zip(places[a], places[b]))
    middle, end = len(places) // 2 - 1, len(places) - 1
    return (
        hops(middle, middle + 1) == 2
        and hops(middle, end) == hops(end, middle + 1) == 1
        and hops(middle + 1, 0) == hops(0, middle) == 1
    )


def shards(relay, query_input, key_input, value_input, filters, complement, doc_lengths, cotangent):
    rows, channels = query_input.shape
    taps = filters.shape[1]
    ctx, ch = lax.axis_size("ctx"), lax.axis_size("ch")
    groups = min(ctx, taps // TILE)
    height, share, size = taps // groups, taps // ctx, 2 * rows
    widths = channel_widths(channels)
    chunks, block = len(widths), max(widths)
    slots = PACK - 1 + -(-doc_lengths.shape[0] // PACK)
    tables = [jnp.asarray(table) for table in fourier_tables(rows, taps)]
    fetched = [query_input, key_input, value_input, cotangent, filters, *tables]
    hbm = pl.BlockSpec(memory_space=pl.ANY)
    vmem = pl.BlockSpec(memory_space=pltpu.VMEM)
    dma = pltpu.SemaphoreType.DMA
    *mixed, grad_filter = pl.pallas_call(
        functools.partial(entry_kernel, ctx, ch, groups, widths, relay, len(fetched)),
        in_specs=[pl.BlockSpec(memory_space=pltpu.SMEM), vmem] + [hbm] * len(fetched),
        out_specs=[vmem] * 5,
        out_shape=[pltpu.VMEM((rows, channels), BF16)] * 4 + [pltpu.VMEM((share, channels), F32)],
        scratch_shapes=[pltpu.VMEM(a.shape, a.dtype) for a in fetched]
        + [
            dma((len(fetched),)),
            pltpu.VMEM((rows, channels), BF16),
            pltpu.VMEM((rows, channels), BF16),
            pltpu.VMEM((4, rows, channels), BF16),
            pltpu.VMEM((2, rows, channels), BF16),
            pltpu.VMEM((ch, height, channels), BF16),
            pltpu.VMEM((height, channels), BF16),
            pltpu.VMEM((LANES, channels), BF16),
            pltpu.VMEM((groups, height, channels), BF16),
            pltpu.VMEM((2, 2, ctx // 2, share, channels), BF16),
            pltpu.VMEM((2, ctx // 2, share, channels), BF16),
            pltpu.VMEM((2, ctx // 2, share, channels), BF16),
            pltpu.VMEM((ctx // 2 - 1, 2, share, channels), BF16),
            pltpu.VMEM((ch, -(-share // TILE) * TILE, channels), BF16),
            pltpu.VMEM((slots, size, rows), BF16),
            pltpu.VMEM((rows, (slots + 2) * size), BF16),
            pltpu.VMEM((2, size, rows), BF16),
            pltpu.VMEM((2, size, rows), BF16),
            pltpu.VMEM((2 * size, channels), F32),
            pltpu.VMEM((2 * size, channels), F32),
            pltpu.VMEM((2 * size, channels), F32),
            pltpu.VMEM((slots, size, channels), F32),
            pltpu.VMEM((slots, size, channels), F32),
            pltpu.VMEM((2, 2, size, channels), F32),
            pltpu.VMEM((2, size, channels), F32),
            pltpu.VMEM((2, size, channels), F32),
            pltpu.VMEM(((slots + 2) * size, block), BF16),
            pltpu.VMEM(((slots + 2) * size, block), BF16),
            pltpu.VMEM((2, taps, channels), F32),
            dma((4 * chunks,)), dma((4 * chunks,)), dma((2 * chunks,)), dma((2 * chunks,)), dma((ch - 1,)), dma((ch - 1,)),
            dma((groups // 2,)), dma((groups // 2,)),
            dma((chunks,)), dma((chunks,)),
            dma(((ctx // 2 - 1) * chunks,)), dma(((ctx // 2 - 1) * chunks,)), dma(((ch - 1) * chunks,)), dma(((ch - 1) * chunks,)), dma((1,)),
        ],
        compiler_params=pltpu.CompilerParams(
            collective_id=0, has_side_effects=True, vmem_limit_bytes=VMEM_BYTES
        ),
        name="mixer",
    )(doc_lengths, complement, *fetched)
    *mixed, grad_filter = hand_over(*mixed, grad_filter)
    return (*mixed, grad_filter.T)


def solution(mesh):
    placed = (
        P("ctx", "ch"),
        P("ctx", "ch"),
        P("ctx", "ch"),
        P("ch", None),
        P("ch"),
        P(),
        P("ctx", "ch"),
    )
    return jax.shard_map(
        functools.partial(shards, needs_relay(mesh)),
        mesh=mesh,
        in_specs=placed,
        out_specs=(P("ctx", "ch"), P("ctx", "ch"), P("ctx", "ch"), P("ctx", "ch"), P("ch", "ctx")),
        check_vma=False,
    )
```
